32 devices in a mesh: dp: 8 (over y, x, core), tensor: 4 (over z).
Axes of the slice: x: 2, y: 2, z: 4, core: 2. Of those that a mesh axis runs over, the one named last changes fastest.
Arguments:
- inputs: bfloat16 [2, 2048, 768], P(None, 'dp'), may hold values from -6 to 6
- cotangent: bfloat16 [2, 2048, 768], P(None, 'dp'), may hold values from -6 to 6
- lengths: int32 [2, 128], P(None, 'dp'), may hold values from 0 to 256, as said below
- owner_rows: int32 [2, 2048], P(None, 'dp'), may hold values from 0 to 2047, as said below
- given_rows: int32 [2, 2048], P(None, 'dp'), may hold values from 0 to 2047, as said below
- norm_gain: float32 [768], replicated, may hold values from 0.1 to 1.9
- qkv_weight: bfloat16 [768, 3, 768], P(None, None, 'tensor'), may hold values from -0.21875 to 0.21875
- rate_weight: bfloat16 [768, 12], P(None, 'tensor'), may hold values from -0.21875 to 0.21875
- rate_bias: float32 [12], P('tensor'), may hold values from -1 to 1
- inner_first: float32 [12, 64, 256], P('tensor'), may hold values from -0.75 to 0.75
- inner_first_bias: float32 [12, 256], P('tensor'), may hold values from -3 to 3
- inner_second: float32 [12, 256, 64], P('tensor'), may hold values from -0.375 to 0.375
- inner_second_bias: float32 [12, 64], P('tensor'), may hold values from -3 to 3
- inner_gain: float32 [12, 64], P('tensor'), may hold values from 0.1 to 1.9
- inner_shift: float32 [12, 64], P('tensor'), may hold values from -2 to 2
- gate_weight: bfloat16 [768, 768], P(None, 'tensor'), may hold values from -0.21875 to 0.21875
- post_gain: float32 [768], P('tensor'), may hold values from 0.1 to 1.9
- post_bias: float32 [768], P('tensor'), may hold values from -2 to 2
- out_weight: bfloat16 [768, 768], P('tensor'), may hold values from -0.4375 to 0.4375
- ffn_gain: float32 [768], replicated, may hold values from 0.1 to 1.9
- swiglu_weight: bfloat16 [768, 2, 2048], P(None, None, 'tensor'), may hold values from -0.21875 to 0.21875
- down_weight: bfloat16 [2048, 768], P('tensor'), may hold values from -0.375 to 0.375
Outputs:
- outputs: bfloat16 [2, 2048, 768], P(None, 'dp')
- input_grad: bfloat16 [2, 2048, 768], P(None, 'dp')
- grad_norm_gain: float32 [768], replicated
- grad_qkv_weight: float32 [768, 3, 768], P(None, None, 'tensor')
- grad_rate_weight: float32 [768, 12], P(None, 'tensor')
- grad_rate_bias: float32 [12], P('tensor')
- grad_inner_first: float32 [12, 64, 256], P('tensor')
- grad_inner_first_bias: float32 [12, 256], P('tensor')
- grad_inner_second: float32 [12, 256, 64], P('tensor')
- grad_inner_second_bias: float32 [12, 64], P('tensor')
- grad_inner_gain: float32 [12, 64], P('tensor')
- grad_inner_shift: float32 [12, 64], P('tensor')
- grad_gate_weight: float32 [768, 768], P(None, 'tensor')
- grad_post_gain: float32 [768], P('tensor')
- grad_post_bias: float32 [768], P('tensor')
- grad_out_weight: float32 [768, 768], P('tensor')
- grad_ffn_gain: float32 [768], replicated
- grad_swiglu_weight: float32 [768, 2, 2048], P(None, None, 'tensor')
- grad_down_weight: float32 [2048, 768], P('tensor')
The draws below stay inside these ranges and needn't reach their ends.
Inputs may be any that keep to these rules, and one draw needn't show every extreme that they name: In micro-batch m, dp index d's 16 entries are the lengths, in order, of the sequences that fill its 256 owner rows: multiples of 16 summing to 256, then zeros. In every micro-batch some index owns a single sequence of 256 rows. `owner_rows`: each row of a micro-batch is one input row once. For any two dp indices s and d, exactly 32 of the input rows held by s are owner rows of d. The inverse of owner_rows: owner_rows[m, given_rows[m, i]] = i.
All inputs are finite; a program needn't handle non-finite values.
Results may differ from the reference program's by a relative error of at most 0.03.
Values may be sent and summed in bfloat16 or wider, within the bound.
No kernel may reach another device: no remote copies, remote signals or barrier semaphores. Data moves between devices by JAX's collectives and lax.ppermute only.
A program may use at most 128 MiB of HBM per device.

```python
from functools import partial
import jax
import jax.numpy as jnp
from jax import lax

D = 768
H = 12
HS = 64
FI = 256
FF = 2048
MB = 16
MICRO = 2
TOK_DEV = 256
HD = 768
SLOTS = 16
PAIR = 32
TOKENS = 2048


def routing_tables(key):
    owners = TOKENS // TOK_DEV
    base = jnp.repeat(jnp.arange(owners, dtype=jnp.int32), PAIR)
    columns = jnp.arange(owners, dtype=jnp.int32)

    def one_micro(micro_key):
        key_anchor, key_local = jax.random.split(micro_key)
        anchor = jax.vmap(lambda sub_key: jax.random.permutation(sub_key, base))(jax.random.split(key_anchor, owners)).astype(jnp.int32)
        local = jax.vmap(lambda sub_key: jax.random.permutation(sub_key, TOK_DEV))(jax.random.split(key_local, owners)).astype(jnp.int32)
        onehot = (anchor[:, :, None] == columns[None, None, :]).astype(jnp.int32)
        earlier = jnp.cumsum(onehot, 1).astype(jnp.int32) - onehot
        rank = jnp.sum(earlier * onehot, 2).astype(jnp.int32)
        column = columns[:, None] * PAIR + rank
        picked = local[anchor, column]
        source = (anchor * TOK_DEV + picked).reshape(-1).astype(jnp.int32)
        inverse = jnp.zeros((TOKENS,), jnp.int32).at[source].set(jnp.arange(TOKENS, dtype=jnp.int32))
        return (source, inverse)
    return jax.vmap(one_micro)(jax.random.split(key, MICRO))


def draw_owner_rows(key, part):
    return routing_tables(jax.random.fold_in(key, 7))[0]


def draw_given_rows(key, part):
    return routing_tables(jax.random.fold_in(key, 7))[1]


def draw_lengths(key, part):
    owners = TOKENS // TOK_DEV
    column = jnp.arange(SLOTS, dtype=jnp.int32)
    first = (column == 0).astype(jnp.int32)

    def one_micro(micro_key):
        key_cuts, key_full = jax.random.split(micro_key)
        cuts = (jax.random.randint(key_cuts, (owners, SLOTS), 0, 8) == 0).astype(jnp.int32)
        cuts = jnp.maximum(cuts, first[None, :])
        full = jax.random.randint(key_full, (), 0, owners)
        single = jnp.arange(owners, dtype=jnp.int32)[:, None] == full
        cuts = jnp.where(single, first[None, :], cuts)
        segment = jnp.cumsum(cuts, 1).astype(jnp.int32) - 1
        counts = jnp.sum((segment[:, :, None] == column[None, None, :]).astype(jnp.int32), 1)
        return (counts * MB).reshape(-1).astype(jnp.int32)
    return jax.vmap(one_micro)(jax.random.split(jax.random.fold_in(key, 11), MICRO))


def level_of(stream_key, extent, cuts, low, high):
    level = 1.0
    for axis_at, shards_of in cuts:
        heights = jax.random.uniform(jax.random.fold_in(jax.random.fold_in(stream_key, 6), axis_at), (shards_of,), jnp.float32, low / len(cuts), high / len(cuts))
        level = level * jnp.repeat(jnp.exp(heights), extent[axis_at] // shards_of).reshape((-1,) + (1,) * (len(extent) - 1 - axis_at))
    return level


def bell_draw(own_key, dims, scale, bound, cuts=(), kind=jnp.bfloat16):
    values = jax.random.normal(own_key, dims, jnp.float32) * scale
    if len(cuts) > 0:
        values = level_of(own_key, dims, cuts, -0.22, 0.18) * values
    return jnp.clip(values, min=-bound, max=bound).astype(kind)


def setup_inputs(seed: int = 0) -> dict:
    arg_keys = jax.random.split(jax.random.key(seed), 23)
    inputs = bell_draw(arg_keys[0], (MICRO, TOKENS, D), 1.0, 6.0, ((1, 8),))
    cotangent = bell_draw(arg_keys[1], (MICRO, TOKENS, D), 1.0, 6.0, ((1, 8),))
    lengths = draw_lengths(jax.random.fold_in(arg_keys[22], 71), 0)
    owner_rows = draw_owner_rows(jax.random.fold_in(arg_keys[22], 71), 0)
    given_rows = draw_given_rows(jax.random.fold_in(arg_keys[22], 71), 0)
    norm_gain = jnp.clip(1.0 + 0.18 * jax.random.normal(arg_keys[5], (D,), jnp.float32), 0.1, 1.9)
    qkv_weight = bell_draw(arg_keys[6], (D, 3, HD), D ** -0.5, 0.21875, ((2, 4),))
    rate_weight = bell_draw(arg_keys[7], (D, H), D ** -0.5, 0.21875, ((1, 4),))
    rate_bias = jnp.clip(jax.random.uniform(arg_keys[8], (H,), jnp.float32, -1.0, 1.0) * level_of(arg_keys[8], (H,), ((0, 4),), -0.4, 0.0), -1.0, 1.0)
    inner_first = bell_draw(arg_keys[9], (H, HS, FI), HS ** -0.5, 0.75, ((0, 4),), jnp.float32)
    inner_first_bias = bell_draw(arg_keys[10], (H, FI), 0.5, 3.0, ((0, 4),), jnp.float32)
    inner_second = bell_draw(arg_keys[11], (H, FI, HS), FI ** -0.5, 0.375, ((0, 4),), jnp.float32)
    inner_second_bias = bell_draw(arg_keys[12], (H, HS), 0.5, 3.0, ((0, 4),), jnp.float32)
    inner_gain = jnp.clip(1.0 + 0.18 * jax.random.normal(arg_keys[13], (H, HS), jnp.float32), 0.1, 1.9)
    inner_shift = bell_draw(arg_keys[14], (H, HS), 0.3, 2.0, ((0, 4),), jnp.float32)
    gate_weight = bell_draw(arg_keys[15], (D, HD), D ** -0.5, 0.21875, ((1, 4),))
    post_gain = jnp.clip(1.0 + 0.18 * jax.random.normal(arg_keys[16], (HD,), jnp.float32), 0.1, 1.9)
    post_bias = bell_draw(arg_keys[17], (HD,), 0.3, 2.0, ((0, 4),), jnp.float32)
    out_weight = bell_draw(arg_keys[18], (HD, D), (HD // 4) ** -0.5, 0.4375, ((0, 4),))
    ffn_gain = jnp.clip(1.0 + 0.18 * jax.random.normal(arg_keys[19], (D,), jnp.float32), 0.1, 1.9)
    swiglu_weight = bell_draw(arg_keys[20], (D, 2, FF), D ** -0.5, 0.21875, ((2, 4),))
    down_weight = bell_draw(arg_keys[21], (FF, D), (FF // 8) ** -0.5, 0.375, ((0, 4),))
    return {"inputs": inputs, "cotangent": cotangent, "lengths": lengths, "owner_rows": owner_rows, "given_rows": given_rows, "norm_gain": norm_gain, "qkv_weight": qkv_weight, "rate_weight": rate_weight, "rate_bias": rate_bias, "inner_first": inner_first, "inner_first_bias": inner_first_bias, "inner_second": inner_second, "inner_second_bias": inner_second_bias, "inner_gain": inner_gain, "inner_shift": inner_shift, "gate_weight": gate_weight, "post_gain": post_gain, "post_bias": post_bias, "out_weight": out_weight, "ffn_gain": ffn_gain, "swiglu_weight": swiglu_weight, "down_weight": down_weight}


EPS = 1e-06
GELU_SCALE = 0.7978845608028654
EXACT = lax.Precision.HIGHEST

@jax.custom_vjp
def low(v):
    return lax.optimization_barrier(v.astype(jnp.bfloat16)).astype(jnp.float32)

@jax.custom_vjp
def low_back(v):
    return v

def low_keep(v):
    return (low(v), None)

def low_pass(kept, grad):
    return (grad,)

def back_keep(v):
    return (v, None)

def back_low(kept, grad):
    return (low(grad),)
low.defvjp(low_keep, low_pass)
low_back.defvjp(back_keep, back_low)

def gelu_tanh(value):
    return 0.5 * value * (1.0 + jnp.tanh(GELU_SCALE * (value + 0.044715 * value * value * value)))

def gelu_slope(value):
    tangent = jnp.tanh(GELU_SCALE * (value + 0.044715 * value * value * value))
    return 0.5 * (1.0 + tangent) + 0.5 * value * (1.0 - tangent * tangent) * GELU_SCALE * (1.0 + 3.0 * 0.044715 * value * value)

def norm_rows(value, gain, shift):
    center = lax.optimization_barrier(jnp.mean(value, -1, keepdims=True))
    centered = value - center
    return centered * lax.rsqrt(lax.optimization_barrier(jnp.mean(centered * centered, -1, keepdims=True)) + EPS) * gain + shift

def inner_step(params, state, block):
    init_first, init_first_bias, init_second, init_second_bias, inner_gain, inner_shift = params
    query, key_rows, value_rows, rate_rows, flag = block
    restart = flag > 0.5
    first = jnp.where(restart, init_first, state[0])
    first_bias = jnp.where(restart, init_first_bias, state[1])
    second = jnp.where(restart, init_second, state[2])
    second_bias = jnp.where(restart, init_second_bias, state[3])
    contract = partial(jnp.einsum, precision=EXACT)
    gain = inner_gain[:, None, :]
    shift = inner_shift[:, None, :]
    inner_pre = contract('hbe,hef->hbf', key_rows, first) + first_bias[:, None, :]
    inner_act = gelu_tanh(inner_pre)
    inner_out = contract('hbf,hfe->hbe', inner_act, second) + second_bias[:, None, :]
    center = lax.optimization_barrier(jnp.mean(inner_out, -1, keepdims=True))
    centered = inner_out - center
    inv_std = lax.rsqrt(lax.optimization_barrier(jnp.mean(centered * centered, -1, keepdims=True)) + EPS)
    inner_std = centered * inv_std
    inner_error = inner_std * gain + shift - (value_rows - key_rows)
    error_std = inner_error * gain
    grad_out = inv_std * (error_std - lax.optimization_barrier(jnp.mean(error_std, -1, keepdims=True)) - inner_std * lax.optimization_barrier(jnp.mean(error_std * inner_std, -1, keepdims=True)))
    grad_act = contract('hbe,hfe->hbf', grad_out, second)
    grad_pre = grad_act * gelu_slope(inner_pre)
    position = jnp.arange(MB, dtype=jnp.int32)
    lower = position[:, None] >= position[None, :]
    divisor = (position[:, None] + 1).astype(jnp.float32)
    step_weights = jnp.where(lower[None], rate_rows[:, None, :] / divisor[None], 0.0)
    first_mix = step_weights * (contract('hie,hje->hij', query, key_rows) + 1.0)
    query_pre = contract('hie,hef->hif', query, first) + first_bias[:, None, :] - contract('hij,hjf->hif', first_mix, grad_pre)
    query_act = gelu_tanh(query_pre)
    second_mix = step_weights * (contract('hif,hjf->hij', query_act, inner_act) + 1.0)
    query_out = contract('hif,hfe->hie', query_act, second) + second_bias[:, None, :] - contract('hij,hje->hie', second_mix, grad_out)
    result = query + norm_rows(query_out, gain, shift)
    final_rates = rate_rows[:, :, None] / MB
    new_first = first - contract('hbe,hbf->hef', key_rows, final_rates * grad_pre)
    new_first_bias = first_bias - lax.optimization_barrier(jnp.sum(final_rates * grad_pre, 1))
    new_second = second - contract('hbf,hbe->hfe', inner_act, final_rates * grad_out)
    new_second_bias = second_bias - lax.optimization_barrier(jnp.sum(final_rates * grad_out, 1))
    return ((new_first, new_first_bias, new_second, new_second_bias), result)

def inner_scan(query, key_rows, value_rows, rates, flags, params):
    rows, heads, width = query.shape
    owners = rows // TOK_DEV
    count = TOK_DEV // MB

    def blocks(array):
        return array.reshape(owners, count, MB, heads, width).transpose(0, 1, 3, 2, 4)
    rate_blocks = rates.reshape(owners, count, MB, heads).transpose(0, 1, 3, 2)
    flag_blocks = flags.reshape(owners, count)
    stepper = jax.checkpoint(partial(inner_step, params))
    state = (params[0], params[1], params[2], params[3])

    def owner_run(pieces):
        _, results = lax.scan(stepper, state, pieces)
        return results
    results = lax.map(owner_run, (blocks(query), blocks(key_rows), blocks(value_rows), rate_blocks, flag_blocks))
    return results.transpose(0, 1, 3, 2, 4).reshape(rows, heads * width)

def sequence_flags(length_row):
    table = length_row.reshape(-1, SLOTS).astype(jnp.int32)
    owners = table.shape[0]
    offsets = jnp.arange(owners, dtype=jnp.int32)[:, None] * TOK_DEV
    starts = (jnp.cumsum(table, 1).astype(jnp.int32) - table + offsets).reshape(-1)
    positions = jnp.arange(TOKENS // MB, dtype=jnp.int32) * MB
    hit = (starts[None, :] == positions[:, None]) & (table.reshape(-1)[None, :] > 0)
    return jnp.any(hit, 1).astype(jnp.float32)

def layer(residual_in, params, flags):
    norm_gain, qkv_weight, rate_weight, rate_bias, inner_first, inner_first_bias, inner_second, inner_second_bias, inner_gain, inner_shift, gate_weight, post_gain, post_bias, out_weight, ffn_gain, swiglu_weight, down_weight = params
    rows = residual_in.shape[0]
    scale_in = lax.rsqrt(lax.optimization_barrier(jnp.mean(residual_in * residual_in, -1, keepdims=True)) + EPS)
    normed = low(residual_in * scale_in * norm_gain)
    projected = low_back(jnp.dot(normed, qkv_weight.reshape(D, 3 * HD), precision=EXACT)).reshape(rows, 3, H, HS)
    rates = jax.nn.sigmoid(jnp.dot(normed, rate_weight, precision=EXACT) + rate_bias) / HS
    inner_params = (inner_first, inner_first_bias, inner_second, inner_second_bias, inner_gain, inner_shift)
    mixed_heads = inner_scan(projected[:, 0], projected[:, 1], projected[:, 2], rates, flags, inner_params)
    post_normed = norm_rows(mixed_heads, post_gain, post_bias)
    gate_pre = low_back(jnp.dot(normed, gate_weight, precision=EXACT))
    gated = low(post_normed * gelu_tanh(gate_pre))
    mixer_out = low_back(jnp.dot(gated, out_weight, precision=EXACT))
    hidden = residual_in + mixer_out
    scale_mid = lax.rsqrt(lax.optimization_barrier(jnp.mean(hidden * hidden, -1, keepdims=True)) + EPS)
    normed_mid = low(hidden * scale_mid * ffn_gain)
    swiglu = low_back(jnp.dot(normed_mid, swiglu_weight.reshape(D, 2 * FF), precision=EXACT)).reshape(rows, 2, FF)
    activation = low(jax.nn.silu(swiglu[:, 0]) * swiglu[:, 1])
    feed_out = low_back(jnp.dot(activation, down_weight, precision=EXACT))
    return hidden + feed_out

def reference(inputs, cotangent, lengths, owner_rows, given_rows, norm_gain, qkv_weight, rate_weight, rate_bias, inner_first, inner_first_bias, inner_second, inner_second_bias, inner_gain, inner_shift, gate_weight, post_gain, post_bias, out_weight, ffn_gain, swiglu_weight, down_weight):
    weights = tuple((array.astype(jnp.float32) for array in (norm_gain, qkv_weight, rate_weight, rate_bias, inner_first, inner_first_bias, inner_second, inner_second_bias, inner_gain, inner_shift, gate_weight, post_gain, post_bias, out_weight, ffn_gain, swiglu_weight, down_weight)))
    totals = [jnp.zeros(array.shape, jnp.float32) for array in weights]
    outputs_list = []
    input_list = []
    for micro in range(MICRO):
        order = owner_rows[micro].astype(jnp.int32)
        residual_in = inputs[micro][order].astype(jnp.float32)
        upstream = cotangent[micro][order].astype(jnp.float32)
        flags = sequence_flags(lengths[micro])

        def forward(rows_in, *params):
            return layer(rows_in, params, flags)
        result, pull = jax.vjp(forward, residual_in, *weights)
        pulled = pull(upstream)
        back = given_rows[micro].astype(jnp.int32)
        outputs_list.append(result.astype(jnp.bfloat16)[back])
        input_list.append(pulled[0].astype(jnp.bfloat16)[back])
        totals = [total + grad for total, grad in zip(totals, pulled[1:])]
    return (jnp.stack(outputs_list), jnp.stack(input_list), totals[0], totals[1], totals[2], totals[3], totals[4], totals[5], totals[6], totals[7], totals[8], totals[9], totals[10], totals[11], totals[12], totals[13], totals[14], totals[15], totals[16])
```

```python
from functools import partial
import jax, jax.numpy as jnp
from jax import lax
from jax.experimental import pallas as pl
from jax.experimental.pallas import tpu as pltpu

HS=64; MB=16; FI=256; EPS=1e-6
GS=0.7978845608028654; GC=0.044715
bf16=jnp.bfloat16; f32=jnp.float32
NN=((1,),(0,)); NT=((1,),(1,)); TN=((0,),(0,))
def dot(a,b,dims): return lax.dot_general(a,b,(dims,((),())),preferred_element_type=f32)
def rsum(x): return jnp.sum(x,-1,keepdims=True)
def csum(x): return jnp.sum(x,0,keepdims=True)
AUG=80

def gelu_parts(v):
    v2=v*v
    t=jnp.tanh(v*(GS+(GS*GC)*v2))
    hp=0.5+0.5*t
    return v2,t,hp
def gelu(v):
    _,_,hp=gelu_parts(v)
    return v*hp
def gelu_and_slope(v):
    v2,t,hp=gelu_parts(v)
    q=(1.0-t*t)*(0.5*GS+(1.5*GS*GC)*v2)
    return v*hp, hp+v*q
def gelu_slope_curve(v):
    v2,t,hp=gelu_parts(v)
    du=GS+(3*GS*GC)*v2
    s=1.0-t*t
    dt=s*du
    half=0.5*v
    return v*hp, hp+half*dt, dt*(1.0-v*t*du)+half*s*((6*GS*GC)*v)

def lower_table():
    i=lax.broadcasted_iota(jnp.int32,(MB,MB),0); j=lax.broadcasted_iota(jnp.int32,(MB,MB),1)
    return jnp.where(j<=i, 1.0/(i+1).astype(f32), 0.0)

def forward_kernel(NH, steps, flags, proj, rate, w1, w2, c2, gain, shift,
                   mixed, z1h, u1h, deh, zch, u2h, w1h, w2h,
                   kq, k16, tg, w1s, w2s, c2s):
    micro=2
    chains=[(m,h) for m in range(micro) for h in range(NH)]
    lane=lax.broadcasted_iota(jnp.int32,(MB,128),1)
    one=jnp.where(lane==HS,1.0,0.0)
    tab=lower_table()
    @pl.loop(0,micro*steps)
    def _(r):
        for h in range(NH):
            q=proj[r,:,h*128:(h+1)*128]+one
            k=proj[r,:,(NH+h)*128:(NH+h+1)*128]+one
            kq[r,h,0:MB,:]=k.astype(bf16)
            kq[r,h,MB:2*MB,:]=q.astype(bf16)
            k16[r,h]=(k*(1.0/MB)).astype(bf16)
            kk=proj[r,:,(NH+h)*128:(NH+h)*128+HS]
            vv=proj[r,:,(2*NH+h)*128:(2*NH+h)*128+HS]
            tg[r,h]=gain[h]*(shift[h]-vv+kk)
    @pl.loop(0,steps)
    def _(b):
        for m in range(micro):
            @pl.when(flags[m,b]>0)
            def _():
                for h in range(NH):
                    c=m*NH+h
                    w1s[c]=w1[h]; w2s[c]=w2[h]; c2s[c]=c2[h]
        zu={};x2={};sl={};g2e={};g2b={};g1b={};x2b={};w1b={};w2b={}
        for c,(m,h) in enumerate(chains):
            w1b[c]=w1s[c].astype(bf16); w2b[c]=w2s[c].astype(bf16)
            w1h[b,c]=w1b[c]; w2h[b,c]=w2b[c]
        for c,(m,h) in enumerate(chains):
            r=m*steps+b
            zu[c]=dot(kq[r,h,:,0:AUG],w1b[c],NN)
        for c,(m,h) in enumerate(chains):
            z=zu[c][0:MB]
            z1h[b,c]=z
            x2[c],sl[c]=gelu_and_slope(z)
            x2b[c]=x2[c].astype(bf16)
        zc={}
        for c,(m,h) in enumerate(chains):
            zc[c]=dot(x2b[c],w2b[c],NT)+c2s[c]
            zch[b,c]=zc[c]
        for c,(m,h) in enumerate(chains):
            r=m*steps+b
            g=gain[h]; t=tg[r,h]; z=zc[c]
            gz=g*g*z
            var=rsum(z*z)*(1.0/HS)
            m1=rsum(gz)*(1.0/HS); m2=rsum(gz*z)*(1.0/HS); m3=rsum(t*z)*(1.0/HS); mt=rsum(t)*(1.0/HS)
            r2=lax.rsqrt(var+EPS)
            mean_e=r2*m1+mt
            a=r2*(r2*m2+m3)
            er=rate[r,:,h:h+1]*r2
            g2e[c]=er*(r2*gz+t-mean_e-(r2*a)*z)
            g2b[c]=g2e[c].astype(bf16)
        for c,(m,h) in enumerate(chains):
            de=dot(g2b[c],w2b[c],NN)
            deh[b,c]=de
            g1b[c]=(de*sl[c]).astype(bf16)
        for c,(m,h) in enumerate(chains):
            r=m*steps+b
            w1s[c]=w1s[c]-dot(k16[r,h,:,0:AUG],g1b[c],TN)
            w2s[c]=w2s[c]-dot((g2e[c]*(1.0/MB)).astype(bf16),x2b[c],TN)
        for c,(m,h) in enumerate(chains):
            r=m*steps+b
            s1=dot(kq[r,h,MB:2*MB,:],kq[r,h,0:MB,:],NT)
            u1=zu[c][MB:2*MB]-dot((tab*s1).astype(bf16),g1b[c],NN)
            u1h[b,c]=u1
            x3=gelu(u1).astype(bf16)
            s2=dot(x3,x2b[c],NT)+1.0
            u2=dot(x3,w2b[c],NT)+c2s[c]-dot((tab*s2).astype(bf16),g2b[c],NN)
            u2h[b,c]=u2
            c2s[c]=c2s[c]-csum(g2e[c])*(1.0/MB)
    @pl.loop(0,steps)
    def _(b):
        for c,(m,h) in enumerate(chains):
            r=m*steps+b
            u=u2h[b,c]
            u=u-rsum(u)*(1.0/HS)
            n=u*lax.rsqrt(rsum(u*u)*(1.0/HS)+EPS)
            mixed[r,:,h*128:h*128+HS]=proj[r,:,h*128:h*128+HS]+n*gain[h]+shift[h]
            mixed[r,:,h*128+HS:(h+1)*128]=jnp.zeros((MB,128-HS),f32)

def scan_forward(flags,proj,rate,w1,w2,c2,gain,shift):
    rows,_,lanes=proj.shape
    NH=lanes//384; steps=rows//2; C=2*NH
    vm=pl.BlockSpec(memory_space=pltpu.VMEM); sm=pl.BlockSpec(memory_space=pltpu.SMEM)
    S=jax.ShapeDtypeStruct
    return pl.pallas_call(partial(forward_kernel,NH,steps),
        in_specs=[sm]+[vm]*7, out_specs=[vm]*8,
        out_shape=[S((rows,MB,NH*128),f32),S((steps,C,MB,FI),f32),S((steps,C,MB,FI),f32),S((steps,C,MB,FI),f32),
                   S((steps,C,MB,HS),f32),S((steps,C,MB,HS),f32),S((steps,C,AUG,FI),bf16),S((steps,C,HS,FI),bf16)],
        scratch_shapes=[pltpu.VMEM((rows,NH,2*MB,128),bf16),pltpu.VMEM((rows,NH,MB,128),bf16),pltpu.VMEM((rows,NH,MB,HS),f32),
                        pltpu.VMEM((C,AUG,FI),f32),pltpu.VMEM((C,HS,FI),f32),pltpu.VMEM((C,1,HS),f32)],
        compiler_params=pltpu.CompilerParams(vmem_limit_bytes=58<<20),
        name="inner_forward")(flags,proj,rate,w1,w2,c2,gain,shift)

def backward_kernel(NH, steps, flags, dmix, proj, rate, gain, shift, z1h, u1h, deh, zch, u2h, w1h, w2h,
                    dproj, drate, dw1, dw2, dc2, dgain, dshift,
                    kq, k16, tt, p1, p2, pc, eb, p1h, p2h):
    micro=2
    chains=[(m,h) for m in range(micro) for h in range(NH)]
    lane=lax.broadcasted_iota(jnp.int32,(MB,128),1)
    one=jnp.where(lane==HS,1.0,0.0)
    tab=lower_table()
    I=1.0/HS
    @pl.loop(0,micro*steps)
    def _(r):
        for h in range(NH):
            q=proj[r,:,h*128:(h+1)*128]+one
            k=proj[r,:,(NH+h)*128:(NH+h+1)*128]+one
            kq[r,h,0:MB,:]=k.astype(bf16)
            kq[r,h,MB:2*MB,:]=q.astype(bf16)
            k16[r,h]=(k*(-1.0/MB)).astype(bf16)
            kk=proj[r,:,(NH+h)*128:(NH+h)*128+HS]
            vv=proj[r,:,(2*NH+h)*128:(2*NH+h)*128+HS]
            tt[r,h]=shift[h]-vv+kk
    for c in range(2*NH):
        p1[c]=jnp.zeros((AUG,FI),f32); p2[c]=jnp.zeros((HS,FI),f32); pc[c]=jnp.zeros((1,HS),f32)
    for h in range(NH):
        dw1[h]=jnp.zeros((AUG,FI),f32); dw2[h]=jnp.zeros((HS,FI),f32); dc2[h]=jnp.zeros((1,HS),f32)
        dgain[h]=jnp.zeros((1,HS),f32); dshift[h]=jnp.zeros((1,HS),f32)
    drate[...]=jnp.zeros(drate.shape,f32)
    @pl.loop(0,steps)
    def _(back):
        b=steps-1-back
        du2={};du2b={};x2b={};sl={};cv={};g2={};g2b={};g1b={};n2={};ee={};dq={};dk={};dg2={};dg1={};dx2={};du1b={};x3b={};r2={};aa={};me={};e1={};e2={}
        for c,(m,h) in enumerate(chains):
            r=m*steps+b
            g=gain[h]
            u=u2h[b,c]; u=u-rsum(u)*I
            r3=lax.rsqrt(rsum(u*u)*I+EPS); n3=u*r3
            dr=dmix[r,:,h*128:h*128+HS]
            hh=dr*g
            du2[c]=r3*(hh-rsum(hh)*I-n3*(rsum(hh*n3)*I))
            du2b[c]=du2[c].astype(bf16)
            dgain[h]=dgain[h]+csum(dr*n3); dshift[h]=dshift[h]+csum(dr)
            z=zch[b,c]; t=g*tt[r,h]
            r2[c]=lax.rsqrt(rsum(z*z)*I+EPS)
            n2[c]=z*r2[c]
            gn=g*g*n2[c]
            e=gn+t; ee[c]=e
            me[c]=rsum(e)*I; aa[c]=rsum(e*n2[c])*I
            e1[c]=rsum(gn)*I; e2[c]=rsum(gn*n2[c])*I
            g2[c]=r2[c]*(e-me[c]-n2[c]*aa[c])
            g2b[c]=(rate[r,:,h:h+1]*g2[c]).astype(bf16)
        for c,(m,h) in enumerate(chains):
            x2,sl[c],cv[c]=gelu_slope_curve(z1h[b,c])
            x2b[c]=x2.astype(bf16)
            g1b[c]=(deh[b,c]*sl[c]).astype(bf16)
        for c,(m,h) in enumerate(chains):
            r=m*steps+b
            x3,sl3=gelu_and_slope(u1h[b,c])
            x3b[c]=x3.astype(bf16)
            s2=dot(x3b[c],x2b[c],NT)+1.0
            m2=(tab*s2).astype(bf16)
            ds2=(tab*dot(du2b[c],g2b[c],NT)).astype(bf16)
            dg2[c]=-dot(m2,du2b[c],TN)
            dx3=dot(du2b[c],w2h[b,c],NN)-dot(ds2,x2b[c],NN)
            dx2[c]=-dot(ds2,x3b[c],TN)
            du1=(dx3*sl3)
            du1b[c]=du1.astype(bf16)
            s1=dot(kq[r,h,MB:2*MB,:],kq[r,h,0:MB,:],NT)
            m1=(tab*s1).astype(bf16)
            ds1=(tab*dot(du1b[c],g1b[c],NT)).astype(bf16)
            dg1[c]=-dot(m1,du1b[c],TN)
            dq[c]=dot(du1b[c],w1h[b,c],NT)[:,0:HS]-dot(ds1,kq[r,h,0:MB,:],NN)[:,0:HS]
            dk[c]=-dot(ds1,kq[r,h,MB:2*MB,:],TN)[:,0:HS]
        gh={};dde={};dz1a={}
        for c in range(2*NH):
            p1h[c]=p1[c].astype(bf16); p2h[c]=p2[c].astype(bf16)
        for c,(m,h) in enumerate(chains):
            r=m*steps+b
            p1b=p1h[c]; p2b=p2h[c]
            gg1=dg1[c]-dot(k16[r,h,:,0:AUG],p1b,NN)
            gh[c]=dg2[c]+(dot(x2b[c],p2b,NT)+pc[c])*(1.0/MB)
            dk[c]=dk[c]+dot(g1b[c],p1b,NT)[:,0:HS]*(1.0/MB)
            dx2[c]=dx2[c]+dot(g2b[c],p2b,NN)*(1.0/MB)
            dde[c]=(gg1*sl[c]).astype(bf16)
            dz1a[c]=gg1*deh[b,c]*cv[c]
        for c,(m,h) in enumerate(chains):
            gh[c]=gh[c]+dot(dde[c],w2h[b,c],NT)
        dz2={};dz2b={}
        for c,(m,h) in enumerate(chains):
            r=m*steps+b
            g=gain[h]
            q=rsum(gh[c]*g2[c])
            drate[r,:,h:h+1]=q
            rt=rate[r,:,h:h+1]
            G=rt*gh[c]; q=rt*q*I
            n=n2[c]
            gg=g*g
            mg=rsum(G)*I; bb=rsum(G*n)*I
            ds=r2[c]*(G-mg-n*bb)
            eb[b,c]=ds
            dn=gg*ds-r2[c]*(G*aa[c]+ee[c]*bb)
            dz2[c]=r2[c]*(dn-rsum(dn)*I-n*(rsum(dn*n)*I+q))
            dz2b[c]=dz2[c].astype(bf16)
        for c,(m,h) in enumerate(chains):
            r=m*steps+b
            dx=dx2[c]+dot(dz2b[c],w2h[b,c],NN)
            dz1b=(dz1a[c]+dx*sl[c]).astype(bf16)
            dk[c]=dk[c]+dot(dz1b,w1h[b,c],NT)[:,0:HS]
            p1[c]=p1[c]-dot(kq[r,h,:,0:AUG],jnp.concatenate([dz1b,du1b[c]],0),TN)
            p2[c]=p2[c]-dot(jnp.concatenate([du2b[c],g2b[c],dz2b[c]],0),jnp.concatenate([x3b[c],dde[c],x2b[c]],0),TN)
            pc[c]=pc[c]-csum(du2[c]+dz2[c])
        for c,(m,h) in enumerate(chains):
            r=m*steps+b
            ds=eb[b,c]
            g=gain[h]
            dy=ds*g
            dr=dmix[r,:,h*128:h*128+HS]
            zero=jnp.zeros((MB,128-HS),bf16)
            dproj[r,:,h*128:h*128+HS]=(dr+dq[c]).astype(bf16)
            dproj[r,:,(NH+h)*128:(NH+h)*128+HS]=(dy+dk[c]).astype(bf16)
            dproj[r,:,(2*NH+h)*128:(2*NH+h)*128+HS]=(-dy).astype(bf16)
            for p in range(3):
                dproj[r,:,(p*NH+h)*128+HS:(p*NH+h+1)*128]=zero
            dshift[h]=dshift[h]+csum(dy)
            dgain[h]=dgain[h]+csum(ds*(2.0*g*n2[c]+tt[r,h]))
        for m in range(micro):
            @pl.when(flags[m,b]>0)
            def _():
                for h in range(NH):
                    c=m*NH+h
                    dw1[h]=dw1[h]-p1[c]; dw2[h]=dw2[h]-p2[c]; dc2[h]=dc2[h]-pc[c]
                    p1[c]=jnp.zeros((AUG,FI),f32); p2[c]=jnp.zeros((HS,FI),f32); pc[c]=jnp.zeros((1,HS),f32)

def scan_backward(flags,dmix,proj,rate,gain,shift,*hist):
    rows,_,lanes=proj.shape
    NH=lanes//384; steps=rows//2; C=2*NH
    vm=pl.BlockSpec(memory_space=pltpu.VMEM); sm=pl.BlockSpec(memory_space=pltpu.SMEM)
    S=jax.ShapeDtypeStruct
    return pl.pallas_call(partial(backward_kernel,NH,steps),
        in_specs=[sm]+[vm]*12, out_specs=[vm]*7,
        out_shape=[S((rows,MB,lanes),bf16),S((rows,MB,8),f32),S((NH,AUG,FI),f32),S((NH,HS,FI),f32),S((NH,1,HS),f32),S((NH,1,HS),f32),S((NH,1,HS),f32)],
        scratch_shapes=[pltpu.VMEM((rows,NH,2*MB,128),bf16),pltpu.VMEM((rows,NH,MB,128),bf16),pltpu.VMEM((rows,NH,MB,HS),f32),
                        pltpu.VMEM((C,AUG,FI),f32),pltpu.VMEM((C,HS,FI),f32),pltpu.VMEM((C,1,HS),f32),pltpu.VMEM((steps,C,MB,HS),f32),pltpu.VMEM((C,AUG,FI),bf16),pltpu.VMEM((C,HS,FI),bf16)],
        compiler_params=pltpu.CompilerParams(vmem_limit_bytes=58<<20),
        name="inner_backward")(flags,dmix,proj,rate,gain,shift,*hist)

from jax.sharding import PartitionSpec as P

MICRO=2

def gelu_tanh(value):
    return 0.5 * value * (1.0 + jnp.tanh(GS * (value + GC * value * value * value)))

def gelu_slope(value):
    tangent = jnp.tanh(GS * (value + GC * value * value * value))
    return 0.5 * (1.0 + tangent) + 0.5 * value * (1.0 - tangent * tangent) * GS * (1.0 + 3.0 * GC * value * value)

def exchange_slots(owner_rows, given_rows, tok, pair):
    micro = jnp.arange(MICRO, dtype=jnp.int32)[:, None]
    rank = jnp.sum((given_rows[:, None, :] < given_rows[:, :, None]).astype(jnp.int32), 2)
    send = (rank // pair) * (MICRO * pair) + micro * pair + rank % pair
    anchor = owner_rows // tok
    index = jnp.arange(tok, dtype=jnp.int32)
    earlier = index[None, :] < index[:, None]
    order = jnp.sum(((anchor[:, None, :] == anchor[:, :, None]) & earlier[None]).astype(jnp.int32), 2)
    recv = anchor * (MICRO * pair) + micro * pair + order
    return send.reshape(-1), recv.reshape(-1)

def one_hot(slot):
    return (slot[:, None] == jnp.arange(slot.shape[0], dtype=jnp.int32)[None, :]).astype(bf16)

def restart_flags(lengths, steps):
    k = jnp.arange(lengths.shape[1], dtype=jnp.int32)
    starts = jnp.sum(jnp.where((k[None, :] < k[:, None])[None], lengths[:, None, :], 0), 2)
    at = jnp.arange(steps, dtype=jnp.int32) * MB
    hit = (starts[:, None, :] == at[None, :, None]) & (lengths[:, None, :] > 0)
    return jnp.any(hit, 2).astype(jnp.int32)

def mm(a, b):
    return lax.dot_general(a, b, (((1,), (0,)), ((), ())), preferred_element_type=f32)

def mm_nt(a, b):
    return lax.dot_general(a, b, (((1,), (1,)), ((), ())), preferred_element_type=f32)

def mm_tn(a, b):
    return lax.dot_general(a, b, (((0,), (0,)), ((), ())), preferred_element_type=f32)

def pad_heads(array, axis):
    shape = array.shape
    split = shape[:axis] + (shape[axis] // HS, HS) + shape[axis + 1:]
    padded = jnp.pad(array.reshape(split), [(0, 0)] * (axis + 1) + [(0, HS)] + [(0, 0)] * (len(shape) - axis - 1))
    return padded.reshape(shape[:axis] + (2 * shape[axis],) + shape[axis + 1:])

def drop_pad(array, axis):
    shape = array.shape
    split = array.reshape(shape[:axis] + (shape[axis] // 128, 128) + shape[axis + 1:])
    kept = lax.slice_in_dim(split, 0, HS, axis=axis + 1)
    return kept.reshape(shape[:axis] + (shape[axis] // 2,) + shape[axis + 1:])

def swap(array):
    return lax.all_to_all(array, "dp", split_axis=0, concat_axis=0, tiled=True)

def shards(
    inputs, cotangent, lengths, owner_rows, given_rows, norm_gain, qkv_weight, rate_weight, rate_bias,
    inner_first, inner_first_bias, inner_second, inner_second_bias, inner_gain, inner_shift, gate_weight,
    post_gain, post_bias, out_weight, ffn_gain, swiglu_weight, down_weight,
):
    tok = inputs.shape[1]
    width = inputs.shape[2]
    rows = MICRO * tok
    steps = tok // MB
    heads = rate_weight.shape[1]
    pair = tok // lax.axis_size("dp")
    heads_width = heads * HS * lax.axis_size("tensor")
    send, recv = exchange_slots(owner_rows, given_rows, tok, pair)
    send_hot = one_hot(send)
    recv_hot = one_hot(recv)
    sent_in = mm_tn(send_hot, inputs.reshape(rows, width)).astype(bf16)
    sent_up = mm_tn(send_hot, cotangent.reshape(rows, width)).astype(bf16)
    residual = mm(recv_hot, swap(sent_in))
    feed_grad = mm(recv_hot, swap(sent_up)).astype(bf16)
    upstream = feed_grad.astype(f32)
    flags = restart_flags(lengths, steps)
    scale_in = lax.rsqrt(jnp.mean(residual * residual, -1, keepdims=True) + EPS)
    normed = (residual * scale_in * norm_gain).astype(bf16)
    qkv_flat = pad_heads(qkv_weight.reshape(width, -1), 1)
    gate_pad = pad_heads(gate_weight, 1)
    out_pad = pad_heads(out_weight, 0)
    post_gain_pad = pad_heads(post_gain, 0)
    post_bias_pad = pad_heads(post_bias, 0)
    projected = mm(normed, qkv_flat).reshape(rows // MB, MB, -1)
    rate_sig = jax.nn.sigmoid(mm(normed, rate_weight) + rate_bias)
    rates = jnp.pad((rate_sig / HS).reshape(rows // MB, MB, heads), ((0, 0), (0, 0), (0, 8 - heads)))
    first = jnp.concatenate(
        [inner_first, inner_first_bias[:, None], jnp.zeros((heads, AUG - HS - 1, FI), f32)], 1
    )
    second = jnp.swapaxes(inner_second - jnp.mean(inner_second, -1, keepdims=True), 1, 2)
    second_bias = (inner_second_bias - jnp.mean(inner_second_bias, -1, keepdims=True))[:, None]
    gain = inner_gain[:, None]
    shift = inner_shift[:, None]
    mixed, *history = scan_forward(flags, projected, rates, first, second, second_bias, gain, shift)
    mixed = mixed.reshape(rows, -1)
    moments = lax.psum(jnp.stack([jnp.sum(mixed, 1), jnp.sum(mixed * mixed, 1)]), "tensor")
    center = moments[0] / heads_width
    inv_std = lax.rsqrt(moments[1] / heads_width - center * center + EPS)[:, None]
    standard = (mixed - center[:, None]) * inv_std
    post_normed = standard * post_gain_pad + post_bias_pad
    gate_pre = mm(normed, gate_pad)
    gate_act = gelu_tanh(gate_pre)
    gated = (post_normed * gate_act).astype(bf16)
    mixer_out = lax.psum(mm(gated, out_pad).astype(bf16), "tensor").astype(f32)
    hidden = residual + mixer_out
    scale_mid = lax.rsqrt(jnp.mean(hidden * hidden, -1, keepdims=True) + EPS)
    normed_mid = (hidden * scale_mid * ffn_gain).astype(bf16)
    half = swiglu_weight.shape[2]
    swiglu_flat = swiglu_weight.reshape(width, -1)
    swiglu = mm(normed_mid, swiglu_flat)
    gate_half = swiglu[:, :half]
    up_half = swiglu[:, half:]
    gate_sig = jax.nn.sigmoid(gate_half)
    gate_silu = gate_half * gate_sig
    activation = (gate_silu * up_half).astype(bf16)
    activation_grad = mm_nt(feed_grad, down_weight)
    swiglu_grad = jnp.concatenate(
        [activation_grad * up_half * gate_sig * (1.0 + gate_half * (1.0 - gate_sig)), activation_grad * gate_silu], 1
    ).astype(bf16)
    mid_grad = lax.psum(mm_nt(swiglu_grad, swiglu_flat).astype(bf16), "tensor").astype(f32)
    feed_part, mid_grad = lax.optimization_barrier((mm(activation, down_weight).astype(bf16), mid_grad))
    feed_out = lax.psum(feed_part, "tensor").astype(f32)
    out_own = (hidden + feed_out).astype(bf16)
    grad_ffn_gain = jnp.sum(mid_grad * hidden * scale_mid, 0)
    mid_scaled = mid_grad * ffn_gain
    hidden_grad = (
        upstream
        + scale_mid * mid_scaled
        - hidden * scale_mid * scale_mid * scale_mid * jnp.mean(mid_scaled * hidden, -1, keepdims=True)
    )
    mixer_grad = hidden_grad.astype(bf16)
    gated_grad = mm_nt(mixer_grad, out_pad)
    post_grad = gated_grad * gate_act
    gate_grad = (gated_grad * post_normed * gelu_slope(gate_pre)).astype(bf16)
    grad_down = mm_tn(activation, feed_grad)
    grad_swiglu = mm_tn(normed_mid, swiglu_grad)
    grad_out = mm_tn(gated, mixer_grad)
    grad_gate = mm_tn(normed, gate_grad)
    early = lax.psum(
        (grad_down.astype(bf16), grad_swiglu.astype(bf16), drop_pad(grad_out, 0).astype(bf16), drop_pad(grad_gate, 1).astype(bf16)),
        "dp",
    )
    standard_grad = post_grad * post_gain_pad
    grad_moments = lax.psum(
        jnp.stack([jnp.sum(standard_grad, 1), jnp.sum(standard_grad * standard, 1)]), "tensor"
    )
    heads_grad = inv_std * (
        standard_grad - grad_moments[0][:, None] / heads_width - standard * grad_moments[1][:, None] / heads_width
    )
    projected_grad, rate_grad, grad_first, grad_second, grad_second_bias, grad_gain, grad_shift = scan_backward(
        flags, heads_grad.reshape(rows // MB, MB, -1), projected, rates, gain, shift, *history
    )
    logit_grad = rate_grad.reshape(rows, -1)[:, :heads] * rate_sig * (1.0 - rate_sig) / HS
    projected_grad = projected_grad.reshape(rows, -1)
    in_grad = lax.psum(
        (
            mm_nt(projected_grad, qkv_flat)
            + mm_nt(gate_grad, gate_pad)
            + mm_nt(logit_grad.astype(bf16), rate_weight)
        ).astype(bf16),
        "tensor",
    ).astype(f32)
    in_scaled = in_grad * norm_gain
    input_back = (
        hidden_grad
        + scale_in * in_scaled
        - residual * scale_in * scale_in * scale_in * jnp.mean(in_scaled * residual, -1, keepdims=True)
    ).astype(bf16)
    outputs = mm(send_hot, swap(mm_tn(recv_hot, out_own).astype(bf16))).astype(bf16)
    input_grad = mm(send_hot, swap(mm_tn(recv_hot, input_back).astype(bf16))).astype(bf16)
    grad_qkv = drop_pad(mm_tn(normed, projected_grad), 1)
    grad_rate = mm_tn(normed, logit_grad.astype(bf16))
    late_in, early = lax.optimization_barrier(((grad_qkv, grad_first, grad_second), early))
    late = lax.psum(
        (late_in[0].astype(bf16), late_in[1][:, :HS].astype(bf16), jnp.swapaxes(late_in[2], 1, 2).astype(bf16)), "dp"
    )
    small = lax.psum(
        (
            jnp.sum(in_grad * residual * scale_in, 0),
            grad_rate,
            jnp.sum(logit_grad, 0),
            grad_first[:, HS],
            grad_second_bias[:, 0],
            grad_gain[:, 0],
            grad_shift[:, 0],
            drop_pad(jnp.sum(post_grad * standard, 0), 0),
            drop_pad(jnp.sum(post_grad, 0), 0),
            grad_ffn_gain,
        ),
        "dp",
    )
    shape = (MICRO, tok, width)
    return (
        outputs.reshape(shape),
        input_grad.reshape(shape),
        small[0],
        late[0].astype(f32).reshape(qkv_weight.shape),
        small[1],
        small[2],
        late[1].astype(f32),
        small[3],
        late[2].astype(f32),
        small[4],
        small[5],
        small[6],
        early[3].astype(f32),
        small[7],
        small[8],
        early[2].astype(f32),
        small[9],
        early[1].astype(f32).reshape(swiglu_weight.shape),
        early[0].astype(f32),
    )

def solution(mesh):
    rows, heads, columns = P(None, "dp", None), P("tensor", None), P(None, "tensor")
    table = P(None, "dp")
    vector = P("tensor")
    cube = P("tensor", None, None)
    wide = P(None, None, "tensor")
    return jax.shard_map(
        shards,
        mesh=mesh,
        in_specs=(
            rows, rows, table, table, table, P(), wide, columns, vector, cube, heads, cube, heads, heads, heads,
            columns, vector, vector, heads, P(), wide, heads,
        ),
        out_specs=(
            rows, rows, P(), wide, columns, vector, cube, heads, cube, heads, heads, heads, columns, vector, vector,
            heads, P(), wide, heads,
        ),
        check_vma=False,
    )
```

```python
from functools import partial
import jax, jax.numpy as jnp
from jax import lax
from jax.experimental import pallas as pl
from jax.experimental.pallas import tpu as pltpu

HS=64; MB=16; FI=256; EPS=1e-6
GS=0.7978845608028654; GC=0.044715
bf16=jnp.bfloat16; f32=jnp.float32
NN=((1,),(0,)); NT=((1,),(1,)); TN=((0,),(0,))
def dot(a,b,dims): return lax.dot_general(a,b,(dims,((),())),preferred_element_type=f32)
def rsum(x): return jnp.sum(x,-1,keepdims=True)
def csum(x): return jnp.sum(x,0,keepdims=True)
AUG=80
INV=1.0/HS

def gelu_parts(v):
    v2=v*v
    t=jnp.tanh(v*(GS+(GS*GC)*v2))
    hp=0.5+0.5*t
    return v2,t,hp
def gelu(v):
    _,_,hp=gelu_parts(v)
    return v*hp
def gelu_and_slope(v):
    v2,t,hp=gelu_parts(v)
    q=(1.0-t*t)*(0.5*GS+(1.5*GS*GC)*v2)
    return v*hp, hp+v*q
def gelu_slope_curve(v):
    v2,t,hp=gelu_parts(v)
    du=GS+(3*GS*GC)*v2
    s=1.0-t*t
    dt=s*du
    half=0.5*v
    return hp+half*dt, dt*(1.0-v*t*du)+half*s*((6*GS*GC)*v)

def lower_table(turned=False):
    i=lax.broadcasted_iota(jnp.int32,(MB,MB),1 if turned else 0); j=lax.broadcasted_iota(jnp.int32,(MB,MB),0 if turned else 1)
    return jnp.where(j<=i, 1.0/(i+1).astype(f32), 0.0)

def interleave(*runs):
    runs=list(runs)
    while runs:
        for run in list(runs):
            if next(run,"end")=="end": runs.remove(run)

def load_rows(NH, proj, kq, kqt, tt, shift, width):
    rows=proj.shape[0]
    lane=lax.broadcasted_iota(jnp.int32,(1,1,128),2)
    one=jnp.where(lane==HS,1.0,0.0)
    for h in range(NH):
        q=proj[:,:,h*128:(h+1)*128]+one
        k=proj[:,:,(NH+h)*128:(NH+h+1)*128]+one
        kq[:,h,0:MB,:]=k.astype(bf16)
        kq[:,h,MB:2*MB,:]=q.astype(bf16)
        kk=proj[:,:,(NH+h)*128:(NH+h)*128+HS]
        vv=proj[:,:,(2*NH+h)*128:(2*NH+h)*128+HS]
        tt[:,h]=shift[h][None]-vv+kk
    @pl.loop(0,rows,step=4)
    def _(r0):
        for r in range(4):
            for h in range(NH):
                both=kq[r0+r,h,0:width,:].astype(f32)
                kqt[r0+r,h]=both.T[0:AUG].astype(bf16)

def forward_kernel(NH, micro, steps, flags, proj, rate, w1, w2, c2, gain, shift,
                   mixed, z1h, u1h, deh, zch, n3h, w1h, w2h, x2h, g1h, g2h,
                   kq, kqt, tt, w1s, w2s, c2s, zus, c2h):
    chains=[(c,m,h) for c,(m,h) in enumerate((m,h) for m in range(micro) for h in range(NH))]
    tab=lower_table()
    load_rows(NH,proj,kq,kqt,tt,shift,MB)
    def restart(b):
        for m in range(micro):
            @pl.when(flags[m,b]>0)
            def _():
                for h in range(NH):
                    c=m*NH+h
                    w1s[c]=w1[h]; w2s[c]=w2[h]; c2s[c]=c2[h]
                    zus[c]=dot(kq[m*steps+b,h,:,0:AUG],w1[h].astype(bf16),NN)
    def chain(b):
        w1b={};w2b={};x2b={};sl={};zc={};g2e={};g2b={};g1b={};g1c={};base={};coef={};de={}
        nb=jnp.minimum(b+1,steps-1)
        for c,m,h in chains:
            z=zus[c,0:MB]
            z1h[b,c]=z
            u1h[b,c]=zus[c,MB:2*MB]
            x2,sl[c]=gelu_and_slope(z)
            x2b[c]=x2.astype(bf16)
            x2h[b,c]=x2b[c]
        for c,m,h in chains:
            w2b[c]=w2s[c].astype(bf16)
            w2h[b,c]=w2b[c]
            c2h[b,c]=c2s[c]
        yield
        for c,m,h in chains:
            zc[c]=dot(x2b[c],w2b[c],NT)+c2s[c]
        for c,m,h in chains:
            w1b[c]=w1s[c].astype(bf16)
            w1h[b,c]=w1b[c]
        yield
        for c,m,h in chains:
            coef[c]=dot(kq[m*steps+nb,h],kq[m*steps+b,h,0:MB],NT).astype(bf16)
            base[c]=dot(kq[m*steps+nb,h,:,0:AUG],w1b[c],NN)
        for c,m,h in chains:
            r=m*steps+b
            g=gain[h]; t=g*tt[r,h]; z=zc[c]
            gz=g*g*z
            var=rsum(z*z)*INV
            m1=rsum(gz)*INV; m2=rsum(gz*z)*INV; m3=rsum(t*z)*INV; mt=rsum(t)*INV
            r2=lax.rsqrt(var+EPS)
            mean_e=r2*m1+mt
            a=r2*(r2*m2+m3)
            er=rate[r,:,h:h+1]*r2
            g2e[c]=er*(r2*gz+t-mean_e-(r2*a)*z)
            g2b[c]=g2e[c].astype(bf16)
            g2h[b,c]=g2b[c]
            zch[b,c,:,0:HS]=z
            zch[b,c,:,HS:HS+1]=r2
            zch[b,c,:,HS+1:HS+2]=mean_e
            zch[b,c,:,HS+2:HS+3]=a
        yield
        for c,m,h in chains:
            de[c]=dot(g2b[c],w2b[c],NN)
        yield
        for c,m,h in chains:
            deh[b,c]=de[c]
            g1=de[c]*sl[c]
            g1b[c]=g1.astype(bf16)
            g1c[c]=(g1*(1.0/MB)).astype(bf16)
            g1h[b,c]=g1b[c]
        for c,m,h in chains:
            zus[c]=base[c]-dot(coef[c],g1c[c],NN)
        yield
        for c,m,h in chains:
            w1s[c]=w1s[c]-dot(kqt[m*steps+b,h],g1c[c],NN)
        for c,m,h in chains:
            w2s[c]=w2s[c]-dot((g2e[c]*(1.0/MB)).astype(bf16),x2b[c],TN)
            c2s[c]=c2s[c]-csum(g2e[c])*(1.0/MB)
        yield
    def query(b):
        m1={};u1={};x3={};s2={};ua={}
        for c,m,h in chains:
            r=m*steps+b
            m1[c]=(tab*dot(kq[r,h,MB:2*MB],kq[r,h,0:MB],NT)).astype(bf16)
        yield
        for c,m,h in chains:
            u1[c]=u1h[b,c]-dot(m1[c],g1h[b,c],NN)
            u1h[b,c]=u1[c]
        yield
        for c,m,h in chains:
            x3[c]=gelu(u1[c]).astype(bf16)
        yield
        for c,m,h in chains:
            s2[c]=dot(x3[c],x2h[b,c],NT)
            ua[c]=dot(x3[c],w2h[b,c],NT)
        yield
        for c,m,h in chains:
            n3h[b,c,:,0:HS]=ua[c]+c2h[b,c]-dot((tab*(s2[c]+1.0)).astype(bf16),g2h[b,c],NN)
        yield
    restart(0)
    interleave(chain(0))
    restart(1)
    @pl.loop(1,steps)
    def _(b):
        interleave(chain(b),query(b-1))
        restart(b+1)
    interleave(query(steps-1))
    for c,m,h in chains:
        u=n3h[:,c,:,0:HS]
        u=u-rsum(u)*INV
        r3=lax.rsqrt(rsum(u*u)*INV+EPS)
        n=u*r3
        n3h[:,c,:,0:HS]=n
        n3h[:,c,:,HS:HS+1]=r3
        s=slice(m*steps,(m+1)*steps)
        mixed[s,:,h*128:h*128+HS]=proj[s,:,h*128:h*128+HS]+n*gain[h][None]+shift[h][None]
        mixed[s,:,h*128+HS:(h+1)*128]=jnp.zeros((steps,MB,128-HS),f32)

def scan_forward(flags,proj,rate,w1,w2,c2,gain,shift):
    rows,_,lanes=proj.shape
    micro=flags.shape[0]
    NH=lanes//384; steps=rows//micro; C=micro*NH
    vm=pl.BlockSpec(memory_space=pltpu.VMEM); sm=pl.BlockSpec(memory_space=pltpu.SMEM)
    S=jax.ShapeDtypeStruct
    wide=(steps,C,MB,FI)
    return pl.pallas_call(partial(forward_kernel,NH,micro,steps),
        in_specs=[sm]+[vm]*7, out_specs=[vm]*11,
        out_shape=[S((rows,MB,NH*128),f32),S(wide,f32),S(wide,f32),S(wide,f32),
                   S((steps,C,MB,128),f32),S((steps,C,MB,128),f32),S((steps,C,AUG,FI),bf16),S((steps,C,HS,FI),bf16),
                   S(wide,bf16),S(wide,bf16),S((steps,C,MB,HS),bf16)],
        scratch_shapes=[pltpu.VMEM((rows,NH,2*MB,128),bf16),pltpu.VMEM((rows,NH,AUG,MB),bf16),pltpu.VMEM((rows,NH,MB,HS),f32),
                        pltpu.VMEM((C,AUG,FI),f32),pltpu.VMEM((C,HS,FI),f32),pltpu.VMEM((C,1,HS),f32),
                        pltpu.VMEM((C,2*MB,FI),f32),pltpu.VMEM((steps,C,1,HS),f32)],
        compiler_params=pltpu.CompilerParams(vmem_limit_bytes=58<<20),
        name="inner_forward")(jnp.pad(flags,((0,0),(0,1))),proj,rate,w1,w2,c2,gain,shift)

def backward_kernel(NH, micro, steps, flags, dmix, proj, rate, gain, shift, z1h, u1h, deh, zch, n3h, w1h, w2h, x2h, g1h, g2h,
                    dproj, drate, dw1, dw2, dc2, dgain, dshift,
                    kq, kqt, tt, p1, p2, pc, eb, p1h, p2h, ff1, qg1, qx2, qg2, qk, qsl, qcv, qd2, qu2, qu1, qx3):
    chains=[(c,m,h) for c,(m,h) in enumerate((m,h) for m in range(micro) for h in range(NH))]
    C=micro*NH
    tab=lower_table(); tabt=lower_table(True)
    load_rows(NH,proj,kq,kqt,tt,shift,2*MB)
    p1[...]=jnp.zeros(p1.shape,f32); p2[...]=jnp.zeros(p2.shape,f32); pc[...]=jnp.zeros(pc.shape,f32)
    p1h[...]=jnp.zeros(p1h.shape,bf16); p2h[...]=jnp.zeros(p2h.shape,bf16); ff1[...]=jnp.zeros(ff1.shape,f32)
    dw1[...]=jnp.zeros(dw1.shape,f32); dw2[...]=jnp.zeros(dw2.shape,f32); dc2[...]=jnp.zeros(dc2.shape,f32)
    drate[...]=jnp.zeros(drate.shape,f32)
    def query(b):
        o=lax.rem(b,2)
        du2b={};s2t={};d2={};dx3={};m2t={};ds2={};sl3={};du1b={};ds1={};m1t={};dqa={};x3={}
        for c,m,h in chains:
            r=m*steps+b
            n3=n3h[b,c,:,0:HS]; r3=n3h[b,c,:,HS:HS+1]
            hh=dmix[r,:,h*128:h*128+HS]*gain[h]
            du2=r3*(hh-rsum(hh)*INV-n3*(rsum(hh*n3)*INV))
            qd2[o,c]=du2
            du2b[c]=du2.astype(bf16)
            qu2[o,c]=du2b[c]
        for c,m,h in chains:
            x,sl3[c]=gelu_and_slope(u1h[b,c])
            x3[c]=x.astype(bf16)
            qx3[o,c]=x3[c]
        yield
        for c,m,h in chains:
            s2t[c]=dot(x2h[b,c],x3[c],NT)
            d2[c]=dot(du2b[c],g2h[b,c],NT)
            dx3[c]=dot(du2b[c],w2h[b,c],NN)
        yield
        for c,m,h in chains:
            m2t[c]=(tabt*(s2t[c]+1.0)).astype(bf16)
            ds2[c]=(tab*d2[c]).astype(bf16)
        for c,m,h in chains:
            dx3[c]=dx3[c]-dot(ds2[c],x2h[b,c],NN)
            qg2[o,c]=-dot(m2t[c],du2b[c],NN)
            qx2[o,c]=-dot(ds2[c],x3[c],TN)
        yield
        for c,m,h in chains:
            du1b[c]=(dx3[c]*sl3[c]).astype(bf16)
            qu1[o,c]=du1b[c]
        for c,m,h in chains:
            r=m*steps+b
            ds1[c]=dot(du1b[c],g1h[b,c],NT)
            m1t[c]=dot(kq[r,h,0:MB],kq[r,h,MB:2*MB],NT)
            dqa[c]=dot(du1b[c],w1h[b,c],NT)[:,0:HS]
        yield
        for c,m,h in chains:
            ds1[c]=(tab*ds1[c]).astype(bf16)
            m1t[c]=(tabt*m1t[c]).astype(bf16)
        for c,m,h in chains:
            r=m*steps+b
            qg1[o,c]=-dot(m1t[c],du1b[c],NN)
            dr=dmix[r,:,h*128:h*128+HS]
            dproj[r,:,h*128:h*128+HS]=(dr+dqa[c]-dot(ds1[c],kq[r,h,0:MB,:],NN)[:,0:HS]).astype(bf16)
            qk[o,c]=-dot(ds1[c],kq[r,h,MB:2*MB,:],TN)[:,0:HS]
        yield
        for c,m,h in chains:
            sl,cv=gelu_slope_curve(z1h[b,c])
            qsl[o,c]=sl
            qcv[o,c]=deh[b,c]*cv
        yield
    def chain(b):
        o=lax.rem(b,2); pb=jnp.maximum(b-1,0)
        dde={};dz1a={};n2p={};gh={};dz2b={};dx={};dz1b={};base={};coef={};dk={};x2p={}
        for c,m,h in chains:
            gg1=qg1[o,c]+ff1[c]
            dde[c]=(gg1*qsl[o,c]).astype(bf16)
            dz1a[c]=gg1*qcv[o,c]
        yield
        for c,m,h in chains:
            gh[c]=dot(dde[c],w2h[b,c],NT)
        for c,m,h in chains:
            n2p[c]=dot(x2h[b,c],p2h[c],NT)
        yield
        for c,m,h in chains:
            r=m*steps+b
            g=gain[h]; gg=g*g
            zc=zch[b,c,:,0:HS]; r2=zch[b,c,:,HS:HS+1]; me=zch[b,c,:,HS+1:HS+2]; a=zch[b,c,:,HS+2:HS+3]
            n=zc*r2
            e=gg*n+g*tt[r,h]
            g2=r2*(e-me-n*a)
            hg=gh[c]+qg2[o,c]+(n2p[c]+pc[c])*(1.0/MB)
            rt=rate[r,:,h:h+1]
            q=rsum(hg*g2)
            drate[r,:,h:h+1]=q
            G=rt*hg
            mg=rsum(G)*INV; bb=rsum(G*n)*INV
            ds=r2*(G-mg-n*bb)
            eb[b,c]=ds
            dn=gg*ds-r2*(G*a+e*bb)
            dz2=r2*(dn-rsum(dn)*INV-n*(rsum(dn*n)*INV+rt*q*INV))
            dz2b[c]=dz2.astype(bf16)
            pc[c]=pc[c]-csum(qd2[o,c]+dz2)
        for c,m,h in chains:
            base[c]=dot(kq[m*steps+pb,h,0:MB,0:AUG],p1h[c],NN)
            coef[c]=dot(kq[m*steps+pb,h,0:MB],kq[m*steps+b,h],NT).astype(bf16)
        for c,m,h in chains:
            x2p[c]=dot(g2h[b,c],p2h[c],NN)
            dk[c]=dot(g1h[b,c],p1h[c],NT)[:,0:HS]
        yield
        for c,m,h in chains:
            dx[c]=dot(dz2b[c],w2h[b,c],NN)
        yield
        for c,m,h in chains:
            full=dx[c]+qx2[o,c]+x2p[c]*(1.0/MB)
            dz1b[c]=(dz1a[c]+full*qsl[o,c]).astype(bf16)
        both={}
        for c,m,h in chains:
            both[c]=jnp.concatenate([dz1b[c],qu1[o,c]],0)
            ff1[c]=(base[c]-dot(coef[c],both[c],NN))*(1.0/MB)
        yield
        for c,m,h in chains:
            r=m*steps+b
            p1[c]=p1[c]-dot(kqt[r,h],both[c],NN)
            p2[c]=p2[c]-dot(jnp.concatenate([qu2[o,c],g2h[b,c],dz2b[c]],0),jnp.concatenate([qx3[o,c],dde[c],x2h[b,c]],0),TN)
        for c,m,h in chains:
            r=m*steps+b
            dy=eb[b,c]*gain[h]
            dkk=dy+qk[o,c]+dk[c]*(1.0/MB)+dot(dz1b[c],w1h[b,c],NT)[:,0:HS]
            dproj[r,:,(NH+h)*128:(NH+h)*128+HS]=dkk.astype(bf16)
            dproj[r,:,(2*NH+h)*128:(2*NH+h)*128+HS]=(-dy).astype(bf16)
        for c,m,h in chains:
            p1h[c]=p1[c].astype(bf16); p2h[c]=p2[c].astype(bf16)
        yield
    def restart(b):
        for m in range(micro):
            @pl.when(flags[m,b]>0)
            def _():
                for h in range(NH):
                    c=m*NH+h
                    dw1[h]=dw1[h]-p1[c]; dw2[h]=dw2[h]-p2[c]; dc2[h]=dc2[h]-pc[c]
                    p1[c]=jnp.zeros((AUG,FI),f32); p2[c]=jnp.zeros((HS,FI),f32); pc[c]=jnp.zeros((1,HS),f32)
                    p1h[c]=jnp.zeros((AUG,FI),bf16); p2h[c]=jnp.zeros((HS,FI),bf16); ff1[c]=jnp.zeros((MB,FI),f32)
    interleave(query(steps-1))
    @pl.loop(0,steps-1)
    def _(back):
        b=steps-1-back
        interleave(chain(b),query(b-1))
        restart(b)
    interleave(chain(0))
    restart(0)
    for h in range(NH):
        dg=jnp.zeros((1,HS),f32); ds=jnp.zeros((1,HS),f32)
        for m in range(micro):
            c=m*NH+h; s=slice(m*steps,(m+1)*steps)
            dr=dmix[s,:,h*128:h*128+HS]
            zc=zch[:,c,:,0:HS]; r2=zch[:,c,:,HS:HS+1]
            g=gain[h][None]
            dm=eb[:,c]
            part=dr*n3h[:,c,:,0:HS]+dm*(2.0*g*(zc*r2)+tt[s,h])
            dg=dg+jnp.sum(jnp.sum(part,0),0,keepdims=True)
            ds=ds+jnp.sum(jnp.sum(dr+dm*g,0),0,keepdims=True)
        dgain[h]=dg; dshift[h]=ds
    for p in range(3*NH):
        dproj[:,:,p*128+HS:(p+1)*128]=jnp.zeros((micro*steps,MB,128-HS),bf16)

def scan_backward(flags,dmix,proj,rate,gain,shift,*hist):
    rows,_,lanes=proj.shape
    micro=flags.shape[0]
    NH=lanes//384; steps=rows//micro; C=micro*NH
    vm=pl.BlockSpec(memory_space=pltpu.VMEM); sm=pl.BlockSpec(memory_space=pltpu.SMEM)
    S=jax.ShapeDtypeStruct; V=pltpu.VMEM
    return pl.pallas_call(partial(backward_kernel,NH,micro,steps),
        in_specs=[sm]+[vm]*15, out_specs=[vm]*7,
        out_shape=[S((rows,MB,lanes),bf16),S((rows,MB,8),f32),S((NH,AUG,FI),f32),S((NH,HS,FI),f32),S((NH,1,HS),f32),S((NH,1,HS),f32),S((NH,1,HS),f32)],
        scratch_shapes=[V((rows,NH,2*MB,128),bf16),V((rows,NH,AUG,2*MB),bf16),V((rows,NH,MB,HS),f32),
                        V((C,AUG,FI),f32),V((C,HS,FI),f32),V((C,1,HS),f32),V((steps,C,MB,HS),f32),
                        V((C,AUG,FI),bf16),V((C,HS,FI),bf16),V((C,MB,FI),f32),
                        V((2,C,MB,FI),f32),V((2,C,MB,FI),f32),V((2,C,MB,HS),f32),V((2,C,MB,HS),f32),V((2,C,MB,FI),f32),V((2,C,MB,FI),f32),
                        V((2,C,MB,HS),f32),V((2,C,MB,HS),bf16),V((2,C,MB,FI),bf16),V((2,C,MB,FI),bf16)],
        compiler_params=pltpu.CompilerParams(vmem_limit_bytes=58<<20),
        name="inner_backward")(flags,dmix,proj,rate,gain,shift,*hist)

from jax.sharding import PartitionSpec as P

MICRO=2

def gelu_tanh(value):
    return 0.5 * value * (1.0 + jnp.tanh(GS * (value + GC * value * value * value)))

def gelu_slope(value):
    tangent = jnp.tanh(GS * (value + GC * value * value * value))
    return 0.5 * (1.0 + tangent) + 0.5 * value * (1.0 - tangent * tangent) * GS * (1.0 + 3.0 * GC * value * value)

def exchange_slots(owner_rows, given_rows, tok, pair):
    micro = jnp.arange(MICRO, dtype=jnp.int32)[:, None]
    rank = jnp.sum((given_rows[:, None, :] < given_rows[:, :, None]).astype(jnp.int32), 2)
    send = (rank // pair) * (MICRO * pair) + micro * pair + rank % pair
    anchor = owner_rows // tok
    index = jnp.arange(tok, dtype=jnp.int32)
    earlier = index[None, :] < index[:, None]
    order = jnp.sum(((anchor[:, None, :] == anchor[:, :, None]) & earlier[None]).astype(jnp.int32), 2)
    recv = anchor * (MICRO * pair) + micro * pair + order
    return send.reshape(-1), recv.reshape(-1)

def one_hot(slot):
    return (slot[:, None] == jnp.arange(slot.shape[0], dtype=jnp.int32)[None, :]).astype(bf16)

def restart_flags(lengths, steps):
    k = jnp.arange(lengths.shape[1], dtype=jnp.int32)
    starts = jnp.sum(jnp.where((k[None, :] < k[:, None])[None], lengths[:, None, :], 0), 2)
    at = jnp.arange(steps, dtype=jnp.int32) * MB
    hit = (starts[:, None, :] == at[None, :, None]) & (lengths[:, None, :] > 0)
    return jnp.any(hit, 2).astype(jnp.int32)

def mm(a, b):
    return lax.dot_general(a, b, (((1,), (0,)), ((), ())), preferred_element_type=f32)

def mm_nt(a, b):
    return lax.dot_general(a, b, (((1,), (1,)), ((), ())), preferred_element_type=f32)

def mm_tn(a, b):
    return lax.dot_general(a, b, (((0,), (0,)), ((), ())), preferred_element_type=f32)

def pad_heads(array, axis):
    shape = array.shape
    split = shape[:axis] + (shape[axis] // HS, HS) + shape[axis + 1:]
    padded = jnp.pad(array.reshape(split), [(0, 0)] * (axis + 1) + [(0, HS)] + [(0, 0)] * (len(shape) - axis - 1))
    return padded.reshape(shape[:axis] + (2 * shape[axis],) + shape[axis + 1:])

def drop_pad(array, axis):
    shape = array.shape
    split = array.reshape(shape[:axis] + (shape[axis] // 128, 128) + shape[axis + 1:])
    kept = lax.slice_in_dim(split, 0, HS, axis=axis + 1)
    return kept.reshape(shape[:axis] + (shape[axis] // 2,) + shape[axis + 1:])

def swap(array):
    return lax.all_to_all(array, "dp", split_axis=0, concat_axis=0, tiled=True)

def shards(
    inputs, cotangent, lengths, owner_rows, given_rows, norm_gain, qkv_weight, rate_weight, rate_bias,
    inner_first, inner_first_bias, inner_second, inner_second_bias, inner_gain, inner_shift, gate_weight,
    post_gain, post_bias, out_weight, ffn_gain, swiglu_weight, down_weight,
):
    tok = inputs.shape[1]
    width = inputs.shape[2]
    rows = MICRO * tok
    steps = tok // MB
    heads = rate_weight.shape[1]
    pair = tok // lax.axis_size("dp")
    heads_width = heads * HS * lax.axis_size("tensor")
    send, recv = exchange_slots(owner_rows, given_rows, tok, pair)
    send_hot = one_hot(send)
    recv_hot = one_hot(recv)
    sent_in = mm_tn(send_hot, inputs.reshape(rows, width)).astype(bf16)
    sent_up = mm_tn(send_hot, cotangent.reshape(rows, width)).astype(bf16)
    residual = mm(recv_hot, swap(sent_in))
    feed_grad = mm(recv_hot, swap(sent_up)).astype(bf16)
    upstream = feed_grad.astype(f32)
    flags = restart_flags(lengths, steps)
    scale_in = lax.rsqrt(jnp.mean(residual * residual, -1, keepdims=True) + EPS)
    normed = (residual * scale_in * norm_gain).astype(bf16)
    qkv_flat = pad_heads(qkv_weight.reshape(width, -1), 1)
    gate_pad = pad_heads(gate_weight, 1)
    out_pad = pad_heads(out_weight, 0)
    post_gain_pad = pad_heads(post_gain, 0)
    post_bias_pad = pad_heads(post_bias, 0)
    projected = mm(normed, qkv_flat).reshape(rows // MB, MB, -1)
    rate_sig = jax.nn.sigmoid(mm(normed, rate_weight) + rate_bias)
    rates = jnp.pad((rate_sig / HS).reshape(rows // MB, MB, heads), ((0, 0), (0, 0), (0, 8 - heads)))
    first = jnp.concatenate(
        [inner_first, inner_first_bias[:, None], jnp.zeros((heads, AUG - HS - 1, FI), f32)], 1
    )
    second = jnp.swapaxes(inner_second - jnp.mean(inner_second, -1, keepdims=True), 1, 2)
    second_bias = (inner_second_bias - jnp.mean(inner_second_bias, -1, keepdims=True))[:, None]
    gain = inner_gain[:, None]
    shift = inner_shift[:, None]
    mixed, *history = scan_forward(flags, projected, rates, first, second, second_bias, gain, shift)
    mixed = mixed.reshape(rows, -1)
    moments = lax.psum(jnp.stack([jnp.sum(mixed, 1), jnp.sum(mixed * mixed, 1)]), "tensor")
    center = moments[0] / heads_width
    inv_std = lax.rsqrt(moments[1] / heads_width - center * center + EPS)[:, None]
    standard = (mixed - center[:, None]) * inv_std
    post_normed = standard * post_gain_pad + post_bias_pad
    gate_pre = mm(normed, gate_pad)
    gate_act = gelu_tanh(gate_pre)
    gated = (post_normed * gate_act).astype(bf16)
    mixer_out = lax.psum(mm(gated, out_pad).astype(bf16), "tensor").astype(f32)
    hidden = residual + mixer_out
    scale_mid = lax.rsqrt(jnp.mean(hidden * hidden, -1, keepdims=True) + EPS)
    normed_mid = (hidden * scale_mid * ffn_gain).astype(bf16)
    half = swiglu_weight.shape[2]
    swiglu_flat = swiglu_weight.reshape(width, -1)
    swiglu = mm(normed_mid, swiglu_flat)
    gate_half = swiglu[:, :half]
    up_half = swiglu[:, half:]
    gate_sig = jax.nn.sigmoid(gate_half)
    gate_silu = gate_half * gate_sig
    activation = (gate_silu * up_half).astype(bf16)
    activation_grad = mm_nt(feed_grad, down_weight)
    swiglu_grad = jnp.concatenate(
        [activation_grad * up_half * gate_sig * (1.0 + gate_half * (1.0 - gate_sig)), activation_grad * gate_silu], 1
    ).astype(bf16)
    mid_grad = lax.psum(mm_nt(swiglu_grad, swiglu_flat).astype(bf16), "tensor").astype(f32)
    feed_part, mid_grad = lax.optimization_barrier((mm(activation, down_weight).astype(bf16), mid_grad))
    feed_out = lax.psum(feed_part, "tensor").astype(f32)
    out_own = (hidden + feed_out).astype(bf16)
    grad_ffn_gain = jnp.sum(mid_grad * hidden * scale_mid, 0)
    mid_scaled = mid_grad * ffn_gain
    hidden_grad = (
        upstream
        + scale_mid * mid_scaled
        - hidden * scale_mid * scale_mid * scale_mid * jnp.mean(mid_scaled * hidden, -1, keepdims=True)
    )
    mixer_grad = hidden_grad.astype(bf16)
    gated_grad = mm_nt(mixer_grad, out_pad)
    post_grad = gated_grad * gate_act
    gate_grad = (gated_grad * post_normed * gelu_slope(gate_pre)).astype(bf16)
    grad_down = mm_tn(activation, feed_grad)
    grad_swiglu = mm_tn(normed_mid, swiglu_grad)
    grad_out = mm_tn(gated, mixer_grad)
    grad_gate = mm_tn(normed, gate_grad)
    early = lax.psum(
        (grad_down.astype(bf16), grad_swiglu.astype(bf16), drop_pad(grad_out, 0).astype(bf16), drop_pad(grad_gate, 1).astype(bf16)),
        "dp",
    )
    standard_grad = post_grad * post_gain_pad
    grad_moments = lax.psum(
        jnp.stack([jnp.sum(standard_grad, 1), jnp.sum(standard_grad * standard, 1)]), "tensor"
    )
    heads_grad = inv_std * (
        standard_grad - grad_moments[0][:, None] / heads_width - standard * grad_moments[1][:, None] / heads_width
    )
    projected_grad, rate_grad, grad_first, grad_second, grad_second_bias, grad_gain, grad_shift = scan_backward(
        flags, heads_grad.reshape(rows // MB, MB, -1), projected, rates, gain, shift, *history
    )
    logit_grad = rate_grad.reshape(rows, -1)[:, :heads] * rate_sig * (1.0 - rate_sig) / HS
    projected_grad = projected_grad.reshape(rows, -1)
    in_grad = lax.psum(
        (
            mm_nt(projected_grad, qkv_flat)
            + mm_nt(gate_grad, gate_pad)
            + mm_nt(logit_grad.astype(bf16), rate_weight)
        ).astype(bf16),
        "tensor",
    ).astype(f32)
    in_scaled = in_grad * norm_gain
    input_back = (
        hidden_grad
        + scale_in * in_scaled
        - residual * scale_in * scale_in * scale_in * jnp.mean(in_scaled * residual, -1, keepdims=True)
    ).astype(bf16)
    outputs = mm(send_hot, swap(mm_tn(recv_hot, out_own).astype(bf16))).astype(bf16)
    input_grad = mm(send_hot, swap(mm_tn(recv_hot, input_back).astype(bf16))).astype(bf16)
    grad_qkv = drop_pad(mm_tn(normed, projected_grad), 1)
    grad_rate = mm_tn(normed, logit_grad.astype(bf16))
    late_in, early = lax.optimization_barrier(((grad_qkv, grad_first, grad_second), early))
    late = lax.psum(
        (late_in[0].astype(bf16), late_in[1][:, :HS].astype(bf16), jnp.swapaxes(late_in[2], 1, 2).astype(bf16)), "dp"
    )
    small = lax.psum(
        (
            jnp.sum(in_grad * residual * scale_in, 0),
            grad_rate,
            jnp.sum(logit_grad, 0),
            grad_first[:, HS],
            grad_second_bias[:, 0],
            grad_gain[:, 0],
            grad_shift[:, 0],
            drop_pad(jnp.sum(post_grad * standard, 0), 0),
            drop_pad(jnp.sum(post_grad, 0), 0),
            grad_ffn_gain,
        ),
        "dp",
    )
    shape = (MICRO, tok, width)
    return (
        outputs.reshape(shape),
        input_grad.reshape(shape),
        small[0],
        late[0].astype(f32).reshape(qkv_weight.shape),
        small[1],
        small[2],
        late[1].astype(f32),
        small[3],
        late[2].astype(f32),
        small[4],
        small[5],
        small[6],
        early[3].astype(f32),
        small[7],
        small[8],
        early[2].astype(f32),
        small[9],
        early[1].astype(f32).reshape(swiglu_weight.shape),
        early[0].astype(f32),
    )

def solution(mesh):
    rows, heads, columns = P(None, "dp", None), P("tensor", None), P(None, "tensor")
    table = P(None, "dp")
    vector = P("tensor")
    cube = P("tensor", None, None)
    wide = P(None, None, "tensor")
    return jax.shard_map(
        shards,
        mesh=mesh,
        in_specs=(
            rows, rows, table, table, table, P(), wide, columns, vector, cube, heads, cube, heads, heads, heads,
            columns, vector, vector, heads, P(), wide, heads,
        ),
        out_specs=(
            rows, rows, P(), wide, columns, vector, cube, heads, cube, heads, heads, heads, columns, vector, vector,
            heads, P(), wide, heads,
        ),
        check_vma=False,
    )
```

```python
from functools import partial
import jax, jax.numpy as jnp
from jax import lax
from jax.experimental import pallas as pl
from jax.experimental.pallas import tpu as pltpu

HS=64; MB=16; FI=256; EPS=1e-6
GS=0.7978845608028654; GC=0.044715
bf16=jnp.bfloat16; f32=jnp.float32
NN=((1,),(0,)); NT=((1,),(1,)); TN=((0,),(0,))
def dot(a,b,dims): return lax.dot_general(a,b,(dims,((),())),preferred_element_type=f32)
def rsum(x): return jnp.sum(x,-1,keepdims=True)
def csum(x): return jnp.sum(x,0,keepdims=True)
AUG=80
INV=1.0/HS
VMEM_LIMIT=58<<20

def gelu_parts(v):
    v2=v*v
    t=jnp.tanh(v*(GS+(GS*GC)*v2))
    hp=0.5+0.5*t
    return v2,t,hp
def gelu(v):
    _,_,hp=gelu_parts(v)
    return v*hp
def gelu_and_slope(v):
    v2,t,hp=gelu_parts(v)
    q=(1.0-t*t)*(0.5*GS+(1.5*GS*GC)*v2)
    return v*hp, hp+v*q
def gelu_slope_curve(v):
    v2,t,hp=gelu_parts(v)
    du=GS+(3*GS*GC)*v2
    s=1.0-t*t
    dt=s*du
    half=0.5*v
    return hp+half*dt, dt*(1.0-v*t*du)+half*s*((6*GS*GC)*v)

def lower_table(turned=False):
    i=lax.broadcasted_iota(jnp.int32,(MB,MB),1 if turned else 0); j=lax.broadcasted_iota(jnp.int32,(MB,MB),0 if turned else 1)
    return jnp.where(j<=i, 1.0/(i+1).astype(f32), 0.0)

def interleave(*runs):
    runs=list(runs)
    while runs:
        for run in list(runs):
            if next(run,"end")=="end": runs.remove(run)

def load_rows(NH, proj, kq, kqt, tt, shift, width):
    rows=proj.shape[0]
    lane=lax.broadcasted_iota(jnp.int32,(1,1,128),2)
    one=jnp.where(lane==HS,1.0,0.0)
    for h in range(NH):
        q=proj[:,:,h*128:(h+1)*128]+one
        k=proj[:,:,(NH+h)*128:(NH+h+1)*128]+one
        kq[:,h,0:MB,:]=k.astype(bf16)
        kq[:,h,MB:2*MB,:]=q.astype(bf16)
        kk=proj[:,:,(NH+h)*128:(NH+h)*128+HS]
        vv=proj[:,:,(2*NH+h)*128:(2*NH+h)*128+HS]
        tt[:,h]=shift[h][None]-vv+kk
    @pl.loop(0,rows,step=4)
    def _(r0):
        for r in range(4):
            for h in range(NH):
                both=kq[r0+r,h,0:width,:].astype(f32)
                kqt[r0+r,h]=both.T[0:AUG].astype(bf16)

def forward_kernel(NH, micro, steps, flags, proj, rate, w1, w2, c2, gain, shift,
                   mixed, z1h, u1h, deh, zch, n3h, w1h, w2h, x2h, g1h, g2h,
                   kq, kqt, tt, w1s, w2s, c2s, zus, c2h):
    chains=[(c,m,h) for c,(m,h) in enumerate((m,h) for m in range(micro) for h in range(NH))]
    tab=lower_table()
    load_rows(NH,proj,kq,kqt,tt,shift,MB)
    def restart(b):
        for m in range(micro):
            @pl.when(flags[m,b]>0)
            def _():
                for h in range(NH):
                    c=m*NH+h
                    w1s[c]=w1[h]; w2s[c]=w2[h]; c2s[c]=c2[h]
                    zus[c]=dot(kq[m*steps+b,h,:,0:AUG],w1[h].astype(bf16),NN)
    def chain(b):
        w1b={};w2b={};x2b={};sl={};zc={};g2e={};g2b={};g1b={};g1c={};base={};coef={};de={}
        nb=jnp.minimum(b+1,steps-1)
        for c,m,h in chains:
            z=zus[c,0:MB]
            z1h[b,c]=z
            u1h[b,c]=zus[c,MB:2*MB]
            x2,sl[c]=gelu_and_slope(z)
            x2b[c]=x2.astype(bf16)
            x2h[b,c]=x2b[c]
        for c,m,h in chains:
            w2b[c]=w2s[c].astype(bf16)
            w2h[b,c]=w2b[c]
            c2h[b,c]=c2s[c]
        yield
        for c,m,h in chains:
            zc[c]=dot(x2b[c],w2b[c],NT)+c2s[c]
        for c,m,h in chains:
            w1b[c]=w1s[c].astype(bf16)
            w1h[b,c]=w1b[c]
        yield
        for c,m,h in chains:
            coef[c]=dot(kq[m*steps+nb,h],kq[m*steps+b,h,0:MB],NT).astype(bf16)
            base[c]=dot(kq[m*steps+nb,h,:,0:AUG],w1b[c],NN)
        for c,m,h in chains:
            r=m*steps+b
            g=gain[h]; t=g*tt[r,h]; z=zc[c]
            gz=g*g*z
            var=rsum(z*z)*INV
            m1=rsum(gz)*INV; m2=rsum(gz*z)*INV; m3=rsum(t*z)*INV; mt=rsum(t)*INV
            r2=lax.rsqrt(var+EPS)
            mean_e=r2*m1+mt
            a=r2*(r2*m2+m3)
            er=rate[r,:,h:h+1]*r2
            g2e[c]=er*(r2*gz+t-mean_e-(r2*a)*z)
            g2b[c]=g2e[c].astype(bf16)
            g2h[b,c]=g2b[c]
            zch[b,c,:,0:HS]=z
            zch[b,c,:,HS:HS+1]=r2
            zch[b,c,:,HS+1:HS+2]=mean_e
            zch[b,c,:,HS+2:HS+3]=a
        yield
        for c,m,h in chains:
            de[c]=dot(g2b[c],w2b[c],NN)
        yield
        for c,m,h in chains:
            deh[b,c]=de[c]
            g1=de[c]*sl[c]
            g1b[c]=g1.astype(bf16)
            g1c[c]=(g1*(1.0/MB)).astype(bf16)
            g1h[b,c]=g1b[c]
        for c,m,h in chains:
            zus[c]=base[c]-dot(coef[c],g1c[c],NN)
        yield
        for c,m,h in chains:
            w1s[c]=w1s[c]-dot(kqt[m*steps+b,h],g1c[c],NN)
        for c,m,h in chains:
            w2s[c]=w2s[c]-dot((g2e[c]*(1.0/MB)).astype(bf16),x2b[c],TN)
            c2s[c]=c2s[c]-csum(g2e[c])*(1.0/MB)
        yield
    def query(b):
        m1={};u1={};x3={};s2={};ua={}
        for c,m,h in chains:
            r=m*steps+b
            m1[c]=(tab*dot(kq[r,h,MB:2*MB],kq[r,h,0:MB],NT)).astype(bf16)
        yield
        for c,m,h in chains:
            u1[c]=u1h[b,c]-dot(m1[c],g1h[b,c],NN)
            u1h[b,c]=u1[c]
        yield
        for c,m,h in chains:
            x3[c]=gelu(u1[c]).astype(bf16)
        yield
        for c,m,h in chains:
            s2[c]=dot(x3[c],x2h[b,c],NT)
            ua[c]=dot(x3[c],w2h[b,c],NT)
        yield
        for c,m,h in chains:
            n3h[b,c,:,0:HS]=ua[c]+c2h[b,c]-dot((tab*(s2[c]+1.0)).astype(bf16),g2h[b,c],NN)
        yield
    for c,m,h in chains:
        w1s[c]=w1[h]; w2s[c]=w2[h]; c2s[c]=c2[h]
        zus[c]=dot(kq[m*steps,h,:,0:AUG],w1[h].astype(bf16),NN)
    interleave(chain(0))
    restart(1)
    @pl.loop(1,steps)
    def _(b):
        interleave(chain(b),query(b-1))
        @pl.when(b+1<steps)
        def _():
            restart(b+1)
    interleave(query(steps-1))
    heads={}
    for c,m,h in chains:
        u=n3h[:,c,:,0:HS]
        u=u-rsum(u)*INV
        r3=lax.rsqrt(rsum(u*u)*INV+EPS)
        n=u*r3
        n3h[:,c,:,0:HS]=n
        n3h[:,c,:,HS:HS+1]=r3
        s=slice(m*steps,(m+1)*steps)
        heads[m,h]=proj[s,:,h*128:h*128+HS]+n*gain[h][None]+shift[h][None]
    for m in range(micro):
        mixed[m*steps:(m+1)*steps]=jnp.concatenate([heads[m,h] for h in range(NH)],-1).astype(bf16)

def scan_forward(flags,proj,rate,w1,w2,c2,gain,shift):
    rows,_,lanes=proj.shape
    micro=flags.shape[0]
    NH=lanes//384; steps=rows//micro; C=micro*NH
    vm=pl.BlockSpec(memory_space=pltpu.VMEM); sm=pl.BlockSpec(memory_space=pltpu.SMEM)
    S=jax.ShapeDtypeStruct
    wide=(steps,C,MB,FI)
    out=pl.pallas_call(partial(forward_kernel,NH,micro,steps),
        in_specs=[sm]+[vm]*7, out_specs=[vm]*11,
        out_shape=[S((rows,MB,NH*HS),bf16),S(wide,f32),S(wide,f32),S(wide,f32),
                   S((steps,C,MB,128),f32),S((steps,C,MB,128),f32),S((steps,C,AUG,FI),bf16),S((steps,C,HS,FI),bf16),
                   S(wide,bf16),S(wide,bf16),S((steps,C,MB,HS),bf16)],
        scratch_shapes=[pltpu.VMEM((rows,NH,2*MB,128),bf16),pltpu.VMEM((rows,NH,AUG,MB),bf16),pltpu.VMEM((rows,NH,MB,HS),f32),
                        pltpu.VMEM((C,AUG,FI),f32),pltpu.VMEM((C,HS,FI),f32),pltpu.VMEM((C,1,HS),f32),
                        pltpu.VMEM((C,2*MB,FI),f32),pltpu.VMEM((steps,C,1,HS),f32)],
        compiler_params=pltpu.CompilerParams(vmem_limit_bytes=VMEM_LIMIT),
        cost_estimate=pl.CostEstimate(flops=18_000_000_000,bytes_accessed=12_000_000,transcendentals=0),
        name="inner_forward")(flags,proj,rate,w1,w2,c2,gain,shift)
    return out[0],tuple(out[1:])

def backward_kernel(NH, micro, steps, flags, dmix, proj, rate, gain, shift, z1h, u1h, deh, zch, n3h, w1h, w2h, x2h, g1h, g2h,
                    dproj, drate, dw1, dw2, dc2, dgain, dshift,
                    kq, kqt, tt, p1, p2, pc, eb, p1h, p2h, ff1, qg1, qx2, qg2, qk, qsl, qcv, qd2, qu2, qu1, qx3):
    chains=[(c,m,h) for c,(m,h) in enumerate((m,h) for m in range(micro) for h in range(NH))]
    C=micro*NH
    tab=lower_table(); tabt=lower_table(True)
    load_rows(NH,proj,kq,kqt,tt,shift,2*MB)
    p1[...]=jnp.zeros(p1.shape,f32); p2[...]=jnp.zeros(p2.shape,f32); pc[...]=jnp.zeros(pc.shape,f32)
    p1h[...]=jnp.zeros(p1h.shape,bf16); p2h[...]=jnp.zeros(p2h.shape,bf16); ff1[...]=jnp.zeros(ff1.shape,f32)
    dw1[...]=jnp.zeros(dw1.shape,f32); dw2[...]=jnp.zeros(dw2.shape,f32); dc2[...]=jnp.zeros(dc2.shape,f32)
    drate[...]=jnp.zeros(drate.shape,f32)
    def query(b):
        o=lax.rem(b,2)
        du2b={};s2t={};d2={};dx3={};m2t={};ds2={};sl3={};du1b={};ds1={};m1t={};dqa={};x3={}
        for c,m,h in chains:
            r=m*steps+b
            n3=n3h[b,c,:,0:HS]; r3=n3h[b,c,:,HS:HS+1]
            hh=dmix[r,:,h*HS:(h+1)*HS]*gain[h]
            du2=r3*(hh-rsum(hh)*INV-n3*(rsum(hh*n3)*INV))
            qd2[o,c]=du2
            du2b[c]=du2.astype(bf16)
            qu2[o,c]=du2b[c]
        for c,m,h in chains:
            x,sl3[c]=gelu_and_slope(u1h[b,c])
            x3[c]=x.astype(bf16)
            qx3[o,c]=x3[c]
        yield
        for c,m,h in chains:
            s2t[c]=dot(x2h[b,c],x3[c],NT)
            d2[c]=dot(du2b[c],g2h[b,c],NT)
            dx3[c]=dot(du2b[c],w2h[b,c],NN)
        yield
        for c,m,h in chains:
            m2t[c]=(tabt*(s2t[c]+1.0)).astype(bf16)
            ds2[c]=(tab*d2[c]).astype(bf16)
        for c,m,h in chains:
            dx3[c]=dx3[c]-dot(ds2[c],x2h[b,c],NN)
            qg2[o,c]=-dot(m2t[c],du2b[c],NN)
            qx2[o,c]=-dot(ds2[c],x3[c],TN)
        yield
        for c,m,h in chains:
            du1b[c]=(dx3[c]*sl3[c]).astype(bf16)
            qu1[o,c]=du1b[c]
        for c,m,h in chains:
            r=m*steps+b
            ds1[c]=dot(du1b[c],g1h[b,c],NT)
            m1t[c]=dot(kq[r,h,0:MB],kq[r,h,MB:2*MB],NT)
            dqa[c]=dot(du1b[c],w1h[b,c],NT)[:,0:HS]
        yield
        for c,m,h in chains:
            ds1[c]=(tab*ds1[c]).astype(bf16)
            m1t[c]=(tabt*m1t[c]).astype(bf16)
        for c,m,h in chains:
            r=m*steps+b
            qg1[o,c]=-dot(m1t[c],du1b[c],NN)
            dr=dmix[r,:,h*HS:(h+1)*HS]
            dproj[r,:,h*128:h*128+HS]=(dr+dqa[c]-dot(ds1[c],kq[r,h,0:MB,:],NN)[:,0:HS]).astype(bf16)
            qk[o,c]=-dot(ds1[c],kq[r,h,MB:2*MB,:],TN)[:,0:HS]
        yield
        for c,m,h in chains:
            sl,cv=gelu_slope_curve(z1h[b,c])
            qsl[o,c]=sl
            qcv[o,c]=deh[b,c]*cv
        yield
    def chain(b):
        o=lax.rem(b,2); pb=jnp.maximum(b-1,0)
        dde={};dz1a={};n2p={};gh={};dz2b={};dx={};dz1b={};base={};coef={};dk={};x2p={}
        for c,m,h in chains:
            gg1=qg1[o,c]+ff1[c]
            dde[c]=(gg1*qsl[o,c]).astype(bf16)
            dz1a[c]=gg1*qcv[o,c]
        yield
        for c,m,h in chains:
            gh[c]=dot(dde[c],w2h[b,c],NT)
        for c,m,h in chains:
            n2p[c]=dot(x2h[b,c],p2h[c],NT)
        yield
        for c,m,h in chains:
            r=m*steps+b
            g=gain[h]; gg=g*g
            zc=zch[b,c,:,0:HS]; r2=zch[b,c,:,HS:HS+1]; me=zch[b,c,:,HS+1:HS+2]; a=zch[b,c,:,HS+2:HS+3]
            n=zc*r2
            e=gg*n+g*tt[r,h]
            g2=r2*(e-me-n*a)
            hg=gh[c]+qg2[o,c]+(n2p[c]+pc[c])*(1.0/MB)
            rt=rate[r,:,h:h+1]
            q=rsum(hg*g2)
            drate[r,:,h:h+1]=q
            G=rt*hg
            mg=rsum(G)*INV; bb=rsum(G*n)*INV
            ds=r2*(G-mg-n*bb)
            eb[b,c]=ds
            dn=gg*ds-r2*(G*a+e*bb)
            dz2=r2*(dn-rsum(dn)*INV-n*(rsum(dn*n)*INV+rt*q*INV))
            dz2b[c]=dz2.astype(bf16)
            pc[c]=pc[c]-csum(qd2[o,c]+dz2)
        for c,m,h in chains:
            base[c]=dot(kq[m*steps+pb,h,0:MB,0:AUG],p1h[c],NN)
            coef[c]=dot(kq[m*steps+pb,h,0:MB],kq[m*steps+b,h],NT).astype(bf16)
        for c,m,h in chains:
            x2p[c]=dot(g2h[b,c],p2h[c],NN)
            dk[c]=dot(g1h[b,c],p1h[c],NT)[:,0:HS]
        yield
        for c,m,h in chains:
            dx[c]=dot(dz2b[c],w2h[b,c],NN)
        yield
        for c,m,h in chains:
            full=dx[c]+qx2[o,c]+x2p[c]*(1.0/MB)
            dz1b[c]=(dz1a[c]+full*qsl[o,c]).astype(bf16)
        both={}
        for c,m,h in chains:
            both[c]=jnp.concatenate([dz1b[c],qu1[o,c]],0)
            ff1[c]=(base[c]-dot(coef[c],both[c],NN))*(1.0/MB)
        yield
        for c,m,h in chains:
            r=m*steps+b
            p1[c]=p1[c]-dot(kqt[r,h],both[c],NN)
            p2[c]=p2[c]-dot(jnp.concatenate([qu2[o,c],g2h[b,c],dz2b[c]],0),jnp.concatenate([qx3[o,c],dde[c],x2h[b,c]],0),TN)
        for c,m,h in chains:
            r=m*steps+b
            dy=eb[b,c]*gain[h]
            dkk=dy+qk[o,c]+dk[c]*(1.0/MB)+dot(dz1b[c],w1h[b,c],NT)[:,0:HS]
            dproj[r,:,(NH+h)*128:(NH+h)*128+HS]=dkk.astype(bf16)
            dproj[r,:,(2*NH+h)*128:(2*NH+h)*128+HS]=(-dy).astype(bf16)
        for c,m,h in chains:
            p1h[c]=p1[c].astype(bf16); p2h[c]=p2[c].astype(bf16)
        yield
    def restart(b):
        for m in range(micro):
            @pl.when(flags[m,b]>0)
            def _():
                for h in range(NH):
                    c=m*NH+h
                    dw1[h]=dw1[h]-p1[c]; dw2[h]=dw2[h]-p2[c]; dc2[h]=dc2[h]-pc[c]
                    p1[c]=jnp.zeros((AUG,FI),f32); p2[c]=jnp.zeros((HS,FI),f32); pc[c]=jnp.zeros((1,HS),f32)
                    p1h[c]=jnp.zeros((AUG,FI),bf16); p2h[c]=jnp.zeros((HS,FI),bf16); ff1[c]=jnp.zeros((MB,FI),f32)
    interleave(query(steps-1))
    @pl.loop(0,steps-1)
    def _(back):
        b=steps-1-back
        interleave(chain(b),query(b-1))
        restart(b)
    interleave(chain(0))
    restart(0)
    for h in range(NH):
        dg=jnp.zeros((1,HS),f32); ds=jnp.zeros((1,HS),f32)
        for m in range(micro):
            c=m*NH+h; s=slice(m*steps,(m+1)*steps)
            dr=dmix[s,:,h*HS:(h+1)*HS]
            zc=zch[:,c,:,0:HS]; r2=zch[:,c,:,HS:HS+1]
            g=gain[h][None]
            dm=eb[:,c]
            part=dr*n3h[:,c,:,0:HS]+dm*(2.0*g*(zc*r2)+tt[s,h])
            dg=dg+jnp.sum(jnp.sum(part,0),0,keepdims=True)
            ds=ds+jnp.sum(jnp.sum(dr+dm*g,0),0,keepdims=True)
        dgain[h]=dg; dshift[h]=ds
    for p in range(3*NH):
        dproj[:,:,p*128+HS:(p+1)*128]=jnp.zeros((micro*steps,MB,128-HS),bf16)

def scan_backward(flags,dmix,proj,rate,gain,shift,hist):
    rows,_,lanes=proj.shape
    micro=flags.shape[0]
    NH=lanes//384; steps=rows//micro; C=micro*NH
    vm=pl.BlockSpec(memory_space=pltpu.VMEM); sm=pl.BlockSpec(memory_space=pltpu.SMEM)
    S=jax.ShapeDtypeStruct; V=pltpu.VMEM
    out=pl.pallas_call(partial(backward_kernel,NH,micro,steps),
        in_specs=[sm]+[vm]*15, out_specs=[vm]*7,
        out_shape=[S((rows,MB,lanes),bf16),S((rows,MB,8),f32),S((NH,AUG,FI),f32),S((NH,HS,FI),f32),S((NH,1,HS),f32),S((NH,1,HS),f32),S((NH,1,HS),f32)],
        scratch_shapes=[V((rows,NH,2*MB,128),bf16),V((rows,NH,AUG,2*MB),bf16),V((rows,NH,MB,HS),f32),
                        V((C,AUG,FI),f32),V((C,HS,FI),f32),V((C,1,HS),f32),V((steps,C,MB,HS),f32),
                        V((C,AUG,FI),bf16),V((C,HS,FI),bf16),V((C,MB,FI),f32),
                        V((2,C,MB,FI),f32),V((2,C,MB,FI),f32),V((2,C,MB,HS),f32),V((2,C,MB,HS),f32),V((2,C,MB,FI),f32),V((2,C,MB,FI),f32),
                        V((2,C,MB,HS),f32),V((2,C,MB,HS),bf16),V((2,C,MB,FI),bf16),V((2,C,MB,FI),bf16)],
        compiler_params=pltpu.CompilerParams(vmem_limit_bytes=VMEM_LIMIT),
        cost_estimate=pl.CostEstimate(flops=36_000_000_000,bytes_accessed=20_000_000,transcendentals=0),
        name="inner_backward")(flags,dmix,proj,rate,gain,shift,*hist)
    return out[0],out[1],tuple(out[2:])

def gelu_full(v):
    v2,t,hp=gelu_parts(v)
    q=(1.0-t*t)*(0.5*GS+(1.5*GS*GC)*v2)
    return v*hp, hp+v*q

def struct(shape, dtype):
    return jax.ShapeDtypeStruct(shape, dtype)

def call(kernel, name, flops, arrays, shapes, scratch=()):
    vm=pl.BlockSpec(memory_space=pltpu.VMEM); sm=pl.BlockSpec(memory_space=pltpu.SMEM)
    specs=[sm if a.ndim==1 else vm for a in arrays]
    moved=sum(a.size*a.dtype.itemsize for a in arrays)+sum(s.size*s.dtype.itemsize for s in shapes)
    return pl.pallas_call(kernel, in_specs=specs, out_specs=[vm]*len(shapes), out_shape=list(shapes), scratch_shapes=list(scratch),
        compiler_params=pltpu.CompilerParams(vmem_limit_bytes=VMEM_LIMIT),
        cost_estimate=pl.CostEstimate(flops=flops,bytes_accessed=moved,transcendentals=0), name=name)(*arrays)

def bits(n):
    return n.bit_length()-1

def near_slot(peer, m, rank, pair, micro):
    return peer*(micro*pair)+m*pair+rank

def far_slot(peer, m, rank, pair, micro, size, part):
    q=pair//size
    return lax.shift_right_logical(rank,bits(q))*part+peer*(micro*q)+m*q+(rank&(q-1))

def send_kernel(pair, size, given, owner, x, up, sent_x, sent_up, recv_col, recv_row, turn_row, fin_col, end_col):
    micro,tok=given.shape
    rows=micro*tok
    part=rows//size
    at=lax.broadcasted_iota(jnp.int32,(rows,tok),0)
    low=lax.broadcasted_iota(jnp.int32,(tok,tok),0); high=lax.broadcasted_iota(jnp.int32,(tok,tok),1)
    ax=None
    for m in range(micro):
        span=slice(m*tok,(m+1)*tok)
        along=jnp.broadcast_to(given[m:m+1,:].astype(f32),(tok,tok))
        down=along.T
        row=jnp.sum(jnp.where(down<along,1.0,0.0),0,keepdims=True).astype(jnp.int32)
        col=jnp.sum(jnp.where(along<down,1.0,0.0),1,keepdims=True).astype(jnp.int32)
        split=lambda r:(lax.shift_right_logical(r,bits(pair)),r&(pair-1))
        peer,rank=split(row)
        hot=jnp.where(at==near_slot(peer,m,rank,pair,micro),1.0,0.0).astype(bf16)
        a=dot(hot,x[m],NN); b=dot(hot,up[m],NN)
        if m==0: ax,au=a,b
        else: ax,au=ax+a,au+b
        peer,rank=split(col)
        fin_col[span,:]=near_slot(peer,m,rank,pair,micro)
        end_col[span,:]=far_slot(peer,m,rank,pair,micro,size,part)
        anchor=lax.shift_right_logical(owner[m:m+1,:],bits(tok))
        along=jnp.broadcast_to(anchor.astype(f32),(tok,tok))
        down=along.T
        same=jnp.where(along==down,1.0,0.0)
        col=jnp.sum(jnp.where(high<low,same,0.0),1,keepdims=True).astype(jnp.int32)
        row=jnp.sum(jnp.where(low<high,same,0.0),0,keepdims=True).astype(jnp.int32)
        recv_col[span,:]=near_slot(down[:,0:1].astype(jnp.int32),m,col,pair,micro)
        recv_row[:,span]=near_slot(anchor,m,row,pair,micro)
        turn_row[:,span]=far_slot(anchor,m,row,pair,micro,size,part)
    sent_x[...]=ax.astype(bf16)
    sent_up[...]=au.astype(bf16)

def send_rows(pair, size, given, owner, x, up):
    micro,tok,width=x.shape
    rows=micro*tok
    i=jnp.int32
    return call(partial(send_kernel,pair,size),"send_rows",2_000_000_000,[given,owner,x,up],
        [struct((rows,width),bf16),struct((rows,width),bf16),struct((rows,1),i),struct((1,rows),i),struct((1,rows),i),struct((rows,1),i),struct((rows,1),i)])

def hot_from_col(col, columns):
    n=col.shape[0]
    return jnp.where(lax.broadcasted_iota(jnp.int32,(n,columns),1)==col,1.0,0.0).astype(bf16)

def hot_from_row(row, count, first=0):
    n=row.shape[1]
    return jnp.where(lax.broadcasted_iota(jnp.int32,(count,n),0)+first==row,1.0,0.0).astype(bf16)

def project_kernel(arrived, col, ngain, qkv, ratew, rateb, resid, normed, proj, rate):
    rows=arrived.shape[0]
    r=dot(hot_from_col(col[...],rows),arrived[...],NN)
    resid[...]=r.astype(bf16)
    n=(r*lax.rsqrt(rsum(r*r)*(1.0/r.shape[1])+EPS)*ngain[...]).astype(bf16)
    normed[...]=n
    rate[...]=(1.0/HS)/(1.0+jnp.exp(-(dot(n,ratew[...],NN)+rateb[...])))
    proj[...]=dot(n,qkv[...],NT)

def project(arrived, col, ngain, qkv, ratew, rateb):
    rows,width=arrived.shape
    return call(project_kernel,"project",1_500_000_000,[arrived,col,ngain,qkv,ratew,rateb],
        [struct((rows,width),bf16),struct((rows,width),bf16),struct((rows,qkv.shape[0]),f32),struct((rows,ratew.shape[1]),f32)])

def middle_kernel(T, cut, me, col, row, arrived, mixed, normed, resid, post, gateout, fgain, swiglu, down,
                  up, out_sent, act, sgrad, nmid, gated, mgrad, hgrad, hgb, ggrad, dpg, dpb, dfg, gin,
                  gpre, hid, feed, mid, stats, pbuf):
    c=pl.program_id(0)
    rows,wide=resid.shape
    hw=mixed.shape[2]
    width=T*hw
    half=sgrad.shape[1]//2
    def flat(ref,i,lead=()):
        w=ref[i]
        return w.reshape(w.shape[0]*w.shape[1],w.shape[2])
    def vectors(i):
        v=post[i,0].astype(f32)
        return v[0:1,0:hw]+v[1:2,0:hw]+v[2:3,0:hw], v[3:4,0:hw]+v[4:5,0:hw]+v[5:6,0:hw]
    @pl.when(c==0)
    def _():
        up[...]=dot(hot_from_col(col[...],rows),arrived[...],NN).astype(bf16)
        center=sum(rsum(mixed[i].astype(f32)) for i in range(T))*(1.0/width)
        square=0.0
        for i in range(T):
            x=mixed[i].astype(f32)-center
            square=square+rsum(x*x)
        inv=lax.rsqrt(square*(1.0/width)+EPS)
        stats[:,0:1]=center
        stats[:,1:2]=inv
        mixer=None
        for i in range(T):
            w=flat(gateout,i)
            pg,pb=vectors(i)
            pre=dot(normed[...],w[0:hw],NT)
            gpre[i]=pre
            g=(((mixed[i].astype(f32)-center)*inv*pg+pb)*gelu(pre)).astype(bf16)
            @pl.when(me[0]==i)
            def _():
                gated[...]=g
            y=dot(g,w[hw:2*hw],NN)
            mixer=y if mixer is None else mixer+y
        h=resid[...].astype(f32)+mixer
        hid[...]=h
        nmid[...]=(h*lax.rsqrt(rsum(h*h)*(1.0/wide)+EPS)*fgain[...]).astype(bf16)
        feed[...]=jnp.zeros((rows,wide),f32)
        mid[...]=jnp.zeros((rows,wide),f32)
    block=rows//2
    @pl.loop(0,2)
    def _(b):
        at=pl.ds(pl.multiple_of(b*block,block),block)
        nm=nmid[at,:]
        sw=flat(swiglu,0)
        dn=flat(down,0)
        gh=dot(nm,sw[0:half],NT)
        uh=dot(nm,sw[half:2*half],NT)
        da=dot(up[at,:],dn,NT)
        sg=1.0/(1.0+jnp.exp(-gh))
        silu=gh*sg
        a=(silu*uh).astype(bf16)
        s1=(da*uh*sg*(1.0+gh*(1.0-sg))).astype(bf16)
        s2=(da*silu).astype(bf16)
        @pl.when(me[0]==c)
        def _():
            act[at,:]=a
            sgrad[at,0:half]=s1
            sgrad[at,half:2*half]=s2
        mid[at,:]=mid[at,:]-(dot(s1,sw[0:half],NN)+dot(s2,sw[half:2*half],NN))
        feed[at,:]=feed[at,:]-dot(a,dn,NN)
    @pl.when(c==T-1)
    def _():
        h=hid[...]
        own=(h-feed[...]).astype(bf16)
        out_sent[...]=dot(hot_from_row(row[...],rows),own,NN).astype(bf16)
        sc=lax.rsqrt(rsum(h*h)*(1.0/wide)+EPS)
        m=-mid[...]
        dfg[...]=csum(m*h*sc)
        ms=m*fgain[...]
        hg=up[...].astype(f32)+sc*ms-h*(sc*sc*sc*(rsum(ms*h)*(1.0/wide)))
        full=hg.astype(bf16)
        mgrad[...]=full
        hgb[...]=(hg-full.astype(f32)).astype(bf16)
        center=stats[:,0:1]; inv=stats[:,1:2]
        s1=0.0; s2=0.0
        for i in range(T):
            w=flat(gateout,i)
            pgn,pb=vectors(i)
            std=(mixed[i].astype(f32)-center)*inv
            a,slope=gelu_full(gpre[i])
            gg=dot(full,w[hw:2*hw],NT)
            gr=(gg*(std*pgn+pb)*slope).astype(bf16)
            ggrad[i]=gr
            pg=gg*a
            p=pg*pgn
            pbuf[i]=p
            s1=s1+rsum(p); s2=s2+rsum(p*std)
            @pl.when(me[0]==i)
            def _():
                dpg[...]=csum(pg*std); dpb[...]=csum(pg)
                r=resid[...].astype(f32)
                gin[...]=csum(dot(gr,w[0:hw],NN)*(r*lax.rsqrt(rsum(r*r)*(1.0/wide)+EPS)))
        std=(mixed[me[0]].astype(f32)-center)*inv
        hgrad[...]=inv*(pbuf[me[0]]-s1*(1.0/width)-std*(s2*(1.0/width)))

def middle(me, col, row, arrived, mixed, normed, resid, weights, fgain):
    T,rows,hw=mixed.shape; wide=resid.shape[1]; D,tall=weights.shape[1:3]
    a,b,g,p=weight_cuts(tall)
    half=a*D//2
    whole=lambda x:pl.BlockSpec(x.shape,lambda c,n=len(x.shape):(0,)*n,pipeline_mode=pl.Buffered(1))
    specs=[pl.BlockSpec(memory_space=pltpu.SMEM)]+[whole(x) for x in (col,row,arrived,mixed,normed,resid)]
    specs+=[pl.BlockSpec((T,1,p,wide),lambda c:(0,0,(a+b+g)//p,0),pipeline_mode=pl.Buffered(1)),
            pl.BlockSpec((T,D,g,wide),lambda c:(0,0,(a+b)//g,0),pipeline_mode=pl.Buffered(1)),
            whole(fgain),
            pl.BlockSpec((1,D,a,wide),lambda c:(c,0,0,0)),
            pl.BlockSpec((1,D,b,wide),lambda c:(c,0,a//b,0))]
    shapes=[struct((rows,wide),bf16),struct((rows,wide),bf16),struct((rows,half),bf16),struct((rows,2*half),bf16),struct((rows,wide),bf16),
            struct((rows,hw),bf16),struct((rows,wide),bf16),struct((rows,hw),f32),struct((rows,wide),bf16),struct((T,rows,hw),bf16),
            struct((1,hw),f32),struct((1,hw),f32),struct((1,wide),f32),struct((1,wide),f32)]
    V=pltpu.VMEM
    return pl.pallas_call(partial(middle_kernel,T,None),
        grid=(T,), in_specs=specs, out_specs=[pl.BlockSpec(s.shape,lambda c,n=len(s.shape):(0,)*n,pipeline_mode=pl.Buffered(1)) for s in shapes], out_shape=shapes,
        scratch_shapes=[V((T,rows,hw),f32),V((rows,wide),f32),V((rows,wide),f32),V((rows,wide),f32),V((rows,128),f32),V((T,rows,hw),f32)],
        compiler_params=pltpu.CompilerParams(vmem_limit_bytes=VMEM_LIMIT,dimension_semantics=("arbitrary",)),
        cost_estimate=pl.CostEstimate(flops=14_000_000_000,bytes_accessed=25_000_000,transcendentals=0),name="middle")(
        me,col,row,arrived,mixed,normed,resid,weights,weights,fgain,weights,weights)

def weight_cuts(tall):
    unit=tall//16
    return 8*unit,4*unit,3*unit,unit

def in_part_kernel(row, dproj, drate, rate, resid, qkv, ratew, gate_gin, sums, gin, logit):
    s=rate[...]
    lg=drate[...]*s*(1.0-HS*s)
    logit[...]=lg
    y=dot(dproj[...],qkv[...],NN)+dot(lg.astype(bf16),ratew[...],NT)
    r=resid[...].astype(f32)
    gin[...]=gate_gin[...]+csum(y*(r*lax.rsqrt(rsum(r*r)*(1.0/r.shape[1])+EPS)))
    sums[...]=dot(hot_from_row(row[...],r.shape[0]),y.astype(bf16),NN).astype(bf16)

def in_part(row, dproj, drate, rate, resid, qkv, ratew, gate_gin):
    rows,width=resid.shape
    return call(in_part_kernel,"in_part",1_500_000_000,[row,dproj,drate,rate,resid,qkv,ratew,gate_gin],
        [struct((rows,width),bf16),struct((1,width),f32),struct(rate.shape,f32)])

def rows_base_kernel(T, me, row, high, low, resid, ggrad, gateout, base, gpart, rpart):
    part,wide=base.shape
    hw=ggrad.shape[2]
    hot=hot_from_row(row[...],part,me[0]*part)
    base[...]=dot(hot,high[...],NN)+dot(hot,low[...],NN)
    acc=None
    for i in range(T):
        w=gateout[i]
        w=w.reshape(w.shape[0]*w.shape[1],w.shape[2])
        y=dot(dot(hot,ggrad[i],NN).astype(bf16),w[0:hw],NN)
        acc=y if acc is None else acc+y
    gpart[...]=acc
    rpart[...]=dot(hot,resid[...],NN)

def rows_base(me, row, high, low, resid, ggrad, weights):
    T,D,tall,wide=weights.shape; rows=resid.shape[0]; part=rows//T
    a,b,g,p=weight_cuts(tall)
    shapes=[struct((part,wide),f32)]*3
    whole=lambda x:pl.BlockSpec(x.shape,lambda c,n=len(x.shape):(0,)*n)
    specs=[pl.BlockSpec(memory_space=pltpu.SMEM)]+[whole(x) for x in (row,high,low,resid,ggrad)]
    specs+=[pl.BlockSpec((T,D,g,wide),lambda c:(0,0,(a+b)//g,0))]
    return pl.pallas_call(partial(rows_base_kernel,T),grid=(1,),in_specs=specs,out_specs=[whole(s) for s in shapes],out_shape=shapes,
        compiler_params=pltpu.CompilerParams(vmem_limit_bytes=VMEM_LIMIT),
        cost_estimate=pl.CostEstimate(flops=800_000_000,bytes_accessed=8_000_000,transcendentals=0),name="rows_base")(
        me,row,high,low,resid,ggrad,weights)

def in_rows_kernel(T, got, base, gpart, rpart, ngain, back):
    part,wide=back.shape
    r=rpart[...]
    sc=lax.rsqrt(rsum(r*r)*(1.0/wide)+EPS)
    s=gpart[...]
    for k in range(T):
        s=s+got[k*part:(k+1)*part,:].astype(f32)
    s=s*ngain[...]
    back[...]=(base[...]+sc*s-r*(sc*sc*sc*(rsum(s*r)*(1.0/wide)))).astype(bf16)

def in_rows(got, base, gpart, rpart, ngain):
    part,wide=base.shape; T=got.shape[0]//part
    return call(partial(in_rows_kernel,T),"in_rows",200_000_000,[got,base,gpart,rpart,ngain],[struct((part,wide),bf16)])[0]

def settle_kernel(micro, col, got, out):
    rows=got.shape[0]; tok=rows//micro
    for m in range(micro):
        out[m]=dot(hot_from_col(col[m*tok:(m+1)*tok,:],rows),got[...],NN).astype(bf16)

def settle(micro, col, got, name):
    rows,wide=got.shape
    return call(partial(settle_kernel,micro),name,500_000_000,[col,got],[struct((micro,rows//micro,wide),bf16)])[0]

from jax.sharding import PartitionSpec as P

MICRO=2

def restart_flags(lengths, steps):
    k = jnp.arange(lengths.shape[1], dtype=jnp.int32)
    starts = jnp.sum(jnp.where((k[None, :] < k[:, None])[None], lengths[:, None, :], 0), 2)
    at = jnp.arange(steps, dtype=jnp.int32) * MB
    hit = (starts[:, None, :] == at[None, :, None]) & (lengths[:, None, :] > 0)
    return jnp.pad(jnp.any(hit, 2).astype(jnp.int32), ((0, 0), (0, 1)))

def pad_heads(array, axis):
    shape = array.shape
    split = shape[:axis] + (shape[axis] // HS, HS) + shape[axis + 1:]
    padded = jnp.pad(array.reshape(split), [(0, 0)] * (axis + 1) + [(0, HS)] + [(0, 0)] * (len(shape) - axis - 1))
    return padded.reshape(shape[:axis] + (2 * shape[axis],) + shape[axis + 1:])

def drop_pad(array, axis):
    shape = array.shape
    split = array.reshape(shape[:axis] + (shape[axis] // 128, 128) + shape[axis + 1:])
    kept = lax.slice_in_dim(split, 0, HS, axis=axis + 1)
    return kept.reshape(shape[:axis] + (shape[axis] // 2,) + shape[axis + 1:])

def swap(array, axis="dp"):
    return lax.all_to_all(array, axis, split_axis=0, concat_axis=0, tiled=True)

def split_three(array):
    high = array.astype(bf16)
    rest = array - high.astype(f32)
    middle_part = rest.astype(bf16)
    return [high, middle_part, (rest - middle_part.astype(f32)).astype(bf16)]

def gather_weights(swiglu, down, gate, out, post_gain, post_bias):
    count = lax.axis_size("dp")
    size = lax.axis_size("tensor")
    d = lax.axis_index("dp")
    width = out.shape[1]
    def rows_of(array):
        piece = array.shape[0] // count
        return lax.dynamic_slice_in_dim(array, d * piece, piece, 0)
    piece = swiglu.shape[1] // count
    turned = lax.dynamic_slice_in_dim(swiglu, d * piece, piece, 1).T
    post = jnp.stack(split_three(post_gain) + split_three(post_bias))
    post = jnp.pad(post, ((0, 10), (0, width - post.shape[1])))
    lines = [turned, rows_of(down), rows_of(jnp.concatenate([gate.T, out], 0))]
    whole = count == 8
    lines.append(post if whole else rows_of(jnp.concatenate([post] * 8, 0)))
    got = lax.all_gather(jnp.concatenate(lines, 0), ("tensor", "dp"))
    if whole:
        return got.reshape(size, count, -1, width)
    parts = []
    at = 0
    for x in lines:
        parts.append(got[:, at:at + x.shape[0]].reshape(size, 8, -1, width))
        at += x.shape[0]
    return jnp.concatenate(parts, 2)

def shards(
    inputs, cotangent, lengths, owner_rows, given_rows, norm_gain, qkv_weight, rate_weight, rate_bias,
    inner_first, inner_first_bias, inner_second, inner_second_bias, inner_gain, inner_shift, gate_weight,
    post_gain, post_bias, out_weight, ffn_gain, swiglu_weight, down_weight,
):
    tok = inputs.shape[1]
    width = inputs.shape[2]
    rows = MICRO * tok
    blocks = rows // MB
    steps = tok // MB
    heads = rate_weight.shape[1]
    size = lax.axis_size("tensor")
    pair = tok // lax.axis_size("dp")
    me = lax.axis_index("tensor").astype(jnp.int32).reshape(1)
    swiglu_flat = swiglu_weight.reshape(width, -1)
    weights = gather_weights(swiglu_flat, down_weight, gate_weight, out_weight, post_gain, post_bias)
    sent_in, sent_up, recv_col, recv_row, turn_row, fin_col, end_col = send_rows(
        pair, size, given_rows, owner_rows, inputs, cotangent
    )
    arrived_in = swap(sent_in)
    arrived_up = swap(sent_up)
    flags = restart_flags(lengths, steps)
    qkv_pad = pad_heads(qkv_weight.transpose(1, 2, 0).reshape(-1, width), 0)
    rate_pad = jnp.pad(rate_weight, ((0, 0), (0, 8 - heads)))
    bias_pad = jnp.pad(rate_bias, (0, 8 - heads))[None]
    first = jnp.concatenate(
        [inner_first, inner_first_bias[:, None], jnp.zeros((heads, AUG - HS - 1, FI), f32)], 1
    )
    second = jnp.swapaxes(inner_second - jnp.mean(inner_second, -1, keepdims=True), 1, 2)
    second_bias = (inner_second_bias - jnp.mean(inner_second_bias, -1, keepdims=True))[:, None]
    gain = inner_gain[:, None]
    shift = inner_shift[:, None]
    resid, normed, projected, rates = project(arrived_in, recv_col, norm_gain[None], qkv_pad, rate_pad, bias_pad)
    projected = projected.reshape(blocks, MB, -1)
    rate_blocks = rates.reshape(blocks, MB, -1)
    own, past = scan_forward(flags, projected, rate_blocks, first, second, second_bias, gain, shift)
    mixed = lax.all_gather(own.reshape(rows, -1), "tensor")
    (
        up, out_sent, act, sgrad, nmid, gated, mixer_grad, heads_grad, grad_low, gate_grad, grad_pgain, grad_pbias, gain_mid, gain_gate
    ) = middle(
        me, recv_col, recv_row, arrived_up, mixed, normed, resid, weights, ffn_gain[None]
    )
    own_gate = lax.dynamic_index_in_dim(gate_grad, lax.axis_index("tensor"), 0, False)
    half = act.shape[1]
    early_in = (
        dot(act, up, TN).astype(bf16),
        dot(nmid, sgrad[:, :half], TN).astype(bf16),
        dot(nmid, sgrad[:, half:], TN).astype(bf16),
        dot(gated, mixer_grad, TN).astype(bf16),
        dot(own_gate, normed, TN).astype(bf16),
    )
    dproj, drate, carry = scan_backward(
        flags, heads_grad.reshape(blocks, MB, -1), projected, rate_blocks, gain, shift, past
    )
    dproj = dproj.reshape(rows, -1)
    sums, gain_in, logit = in_part(turn_row, dproj, drate.reshape(rows, -1), rates, resid, qkv_pad, rate_pad, gain_gate)
    got = swap(sums, "tensor")
    gain_in = lax.psum(gain_in, "dp")
    base, gate_part, resid_part = rows_base(me, turn_row, mixer_grad, grad_low, resid, gate_grad, weights)
    back = in_rows(got, base, gate_part, resid_part, norm_gain[None])
    extra = jnp.pad(jnp.concatenate(split_three(gain_in), 0), ((0, 13), (0, 0)))
    final = lax.all_gather(jnp.concatenate([swap(back), extra], 0), "tensor")
    part = rows // size
    input_grad = settle(MICRO, end_col, final[:, :part].reshape(rows, width), "settle_in")
    norm_total = jnp.sum(final[:, part:part + 3].astype(f32), (0, 1))
    outputs = settle(MICRO, fin_col, swap(out_sent), "settle_out")
    grad_first, grad_second, grad_second_bias, grad_gain, grad_shift = carry
    pieces = [
        dot(normed, logit.astype(bf16), TN)[:, :heads], jnp.sum(logit, 0)[:heads], grad_first[:, HS],
        grad_second_bias[:, 0], grad_gain[:, 0], grad_shift[:, 0], grad_pgain[0], grad_pbias[0], gain_mid[0],
    ]
    flat = jnp.concatenate([x.reshape(-1) for x in pieces])
    flat = jnp.pad(flat, (0, -flat.size % (16 * FI))).reshape(-1, FI)
    inner = jnp.concatenate([grad_first[:, :HS].reshape(-1, FI), grad_second.reshape(-1, FI), flat], 0).astype(bf16)
    grad_qkv = dot(dproj, normed, TN).reshape(3, heads, 128, width)[:, :, :HS].reshape(3, heads * HS, width)
    early, late = lax.psum((early_in, (grad_qkv.astype(bf16), inner)), "dp")
    lines = heads * HS
    inner = late[1].astype(f32)
    packed = inner[2 * lines:].reshape(-1)
    small = []
    at = 0
    for x in pieces:
        small.append(lax.slice_in_dim(packed, at, at + x.size).reshape(x.shape))
        at += x.size
    return (
        outputs,
        input_grad,
        norm_total,
        late[0].astype(f32).transpose(2, 0, 1),
        small[0],
        small[1],
        inner[:lines].reshape(heads, HS, FI),
        small[2],
        jnp.swapaxes(inner[lines:2 * lines].reshape(heads, HS, FI), 1, 2),
        small[3],
        small[4],
        small[5],
        early[4].astype(f32).T,
        small[6],
        small[7],
        early[3].astype(f32),
        small[8],
        jnp.stack([early[1], early[2]], 1).astype(f32),
        early[0].astype(f32),
    )

def solution(mesh):
    rows, heads, columns = P(None, "dp", None), P("tensor", None), P(None, "tensor")
    table = P(None, "dp")
    vector = P("tensor")
    cube = P("tensor", None, None)
    wide = P(None, None, "tensor")
    return jax.shard_map(
        shards,
        mesh=mesh,
        in_specs=(
            rows, rows, table, table, table, P(), wide, columns, vector, cube, heads, cube, heads, heads, heads,
            columns, vector, vector, heads, P(), wide, heads,
        ),
        out_specs=(
            rows, rows, P(), wide, columns, vector, cube, heads, cube, heads, heads, heads, columns, vector, vector,
            heads, P(), wide, heads,
        ),
        check_vma=False,
    )
```

```python
from functools import partial
import jax, jax.numpy as jnp
from jax import lax
from jax.experimental import pallas as pl
from jax.experimental.pallas import tpu as pltpu

HS=64; MB=16; FI=256; EPS=1e-6
GS=0.7978845608028654; GC=0.044715
bf16=jnp.bfloat16; f32=jnp.float32
NN=((1,),(0,)); NT=((1,),(1,)); TN=((0,),(0,))
def dot(a,b,dims): return lax.dot_general(a,b,(dims,((),())),preferred_element_type=f32)
def rsum(x): return jnp.sum(x,-1,keepdims=True)
def csum(x): return jnp.sum(x,0,keepdims=True)
AUG=80
INV=1.0/HS
FORWARD_VMEM=58<<20
BACKWARD_VMEM=58<<20
MIDDLE_VMEM=38<<20
SMALL_VMEM=20<<20

def gelu_parts(v):
    v2=v*v
    t=jnp.tanh(v*(GS+(GS*GC)*v2))
    hp=0.5+0.5*t
    return v2,t,hp
def gelu(v):
    _,_,hp=gelu_parts(v)
    return v*hp
def gelu_and_slope(v):
    v2,t,hp=gelu_parts(v)
    q=(1.0-t*t)*(0.5*GS+(1.5*GS*GC)*v2)
    return v*hp, hp+v*q
def gelu_slope_curve(v):
    v2,t,hp=gelu_parts(v)
    du=GS+(3*GS*GC)*v2
    s=1.0-t*t
    dt=s*du
    half=0.5*v
    return hp+half*dt, dt*(1.0-v*t*du)+half*s*((6*GS*GC)*v)

def lower_table(turned=False):
    i=lax.broadcasted_iota(jnp.int32,(MB,MB),1 if turned else 0); j=lax.broadcasted_iota(jnp.int32,(MB,MB),0 if turned else 1)
    return jnp.where(j<=i, 1.0/(i+1).astype(f32), 0.0)

def interleave(*runs):
    runs=list(runs)
    while runs:
        for run in list(runs):
            if next(run,"end")=="end": runs.remove(run)

Z1,U1,DE=slice(0,MB),slice(MB,2*MB),slice(2*MB,3*MB)
W1,W2,X2,G1=slice(0,AUG),slice(AUG,AUG+HS),slice(AUG+HS,AUG+HS+MB),slice(AUG+HS+MB,AUG+HS+2*MB)
ZC,N3,G2=slice(0,MB),slice(MB,2*MB),slice(2*MB,3*MB)

def load_rows(NH, proj, kq, kqt, tt, shift, width):
    rows=proj.shape[0]
    lane=lax.broadcasted_iota(jnp.int32,(1,1,128),2)
    one=jnp.where(lane==HS,1.0,0.0)
    for h in range(NH):
        q=proj[:,:,h*128:(h+1)*128]+one
        k=proj[:,:,(NH+h)*128:(NH+h+1)*128]+one
        kq[:,h,0:MB,:]=k.astype(bf16)
        kq[:,h,MB:2*MB,:]=q.astype(bf16)
        kk=proj[:,:,(NH+h)*128:(NH+h)*128+HS]
        vv=proj[:,:,(2*NH+h)*128:(2*NH+h)*128+HS]
        tt[:,h]=shift[h][None]-vv+kk
    @pl.loop(0,rows,step=4)
    def _(r0):
        for r in range(4):
            for h in range(NH):
                both=kq[r0+r,h,0:width,:].astype(f32)
                kqt[r0+r,h]=both.T[0:AUG].astype(bf16)

def forward_kernel(NH, micro, steps, flags, proj, rate, w1, w2, c2, gain, shift,
                   mixed, wide_out, state_out, thin_out,
                   wide, held, thin, sems, kq, kqt, tt, w1s, w2s, c2s, zus, c2h, heads):
    chains=[(c,m,h) for c,(m,h) in enumerate((m,h) for m in range(micro) for h in range(NH))]
    tab=lower_table()
    load_rows(NH,proj,kq,kqt,tt,shift,MB)
    def restart(b):
        for m in range(micro):
            @pl.when(flags[m,b]>0)
            def _():
                for h in range(NH):
                    c=m*NH+h
                    w1s[c]=w1[h]; w2s[c]=w2[h]; c2s[c]=c2[h]
                    zus[c]=dot(kq[m*steps+b,h,:,0:AUG],w1[h].astype(bf16),NN)
    def chain(b):
        w1b={};w2b={};x2b={};sl={};zc={};g2e={};g2b={};g1b={};g1c={};base={};coef={};de={}
        nb=jnp.minimum(b+1,steps-1)
        for c,m,h in chains:
            z=zus[c,0:MB]
            wide[b,c,Z1]=z
            wide[b,c,U1]=zus[c,MB:2*MB]
            x2,sl[c]=gelu_and_slope(z)
            x2b[c]=x2.astype(bf16)
            held[b,c,X2]=x2b[c]
        for c,m,h in chains:
            w2b[c]=w2s[c].astype(bf16)
            held[b,c,W2]=w2b[c]
            c2h[b,c]=c2s[c]
        yield
        for c,m,h in chains:
            zc[c]=dot(x2b[c],w2b[c],NT)+c2s[c]
        for c,m,h in chains:
            w1b[c]=w1s[c].astype(bf16)
            held[b,c,W1]=w1b[c]
        yield
        for c,m,h in chains:
            coef[c]=dot(kq[m*steps+nb,h],kq[m*steps+b,h,0:MB],NT).astype(bf16)
            base[c]=dot(kq[m*steps+nb,h,:,0:AUG],w1b[c],NN)
        for c,m,h in chains:
            r=m*steps+b
            g=gain[h]; t=g*tt[r,h]; z=zc[c]
            gz=g*g*z
            var=rsum(z*z)*INV
            m1=rsum(gz)*INV; m2=rsum(gz*z)*INV; m3=rsum(t*z)*INV; mt=rsum(t)*INV
            r2=lax.rsqrt(var+EPS)
            mean_e=r2*m1+mt
            a=r2*(r2*m2+m3)
            er=rate[r,:,h:h+1]*r2
            g2e[c]=er*(r2*gz+t-mean_e-(r2*a)*z)
            g2b[c]=g2e[c].astype(bf16)
            thin[b,c,G2,0:HS]=g2e[c]
            thin[b,c,ZC,0:HS]=z
            thin[b,c,ZC,HS:HS+1]=r2
            thin[b,c,ZC,HS+1:HS+2]=mean_e
            thin[b,c,ZC,HS+2:HS+3]=a
        yield
        for c,m,h in chains:
            de[c]=dot(g2b[c],w2b[c],NN)
        yield
        for c,m,h in chains:
            wide[b,c,DE]=de[c]
            g1=de[c]*sl[c]
            g1b[c]=g1.astype(bf16)
            g1c[c]=(g1*(1.0/MB)).astype(bf16)
            held[b,c,G1]=g1b[c]
        for c,m,h in chains:
            zus[c]=base[c]-dot(coef[c],g1c[c],NN)
        yield
        for c,m,h in chains:
            w1s[c]=w1s[c]-dot(kqt[m*steps+b,h],g1c[c],NN)
        for c,m,h in chains:
            w2s[c]=w2s[c]-dot((g2e[c]*(1.0/MB)).astype(bf16),x2b[c],TN)
            c2s[c]=c2s[c]-csum(g2e[c])*(1.0/MB)
        yield
    def query(b):
        m1={};u1={};x3={};s2={};ua={}
        for c,m,h in chains:
            r=m*steps+b
            m1[c]=(tab*dot(kq[r,h,MB:2*MB],kq[r,h,0:MB],NT)).astype(bf16)
        yield
        for c,m,h in chains:
            u1[c]=wide[b,c,U1]-dot(m1[c],held[b,c,G1],NN)
            wide[b,c,U1]=u1[c]
        yield
        for c,m,h in chains:
            x3[c]=gelu(u1[c]).astype(bf16)
        yield
        for c,m,h in chains:
            s2[c]=dot(x3[c],held[b,c,X2],NT)
            ua[c]=dot(x3[c],held[b,c,W2],NT)
        yield
        for c,m,h in chains:
            ua[c]=ua[c]+c2h[b,c]-dot((tab*(s2[c]+1.0)).astype(bf16),thin[b,c,G2,0:HS].astype(bf16),NN)
        yield
        for c,m,h in chains:
            u=ua[c]
            u=u-rsum(u)*INV
            r3=lax.rsqrt(rsum(u*u)*INV+EPS)
            n=u*r3
            thin[b,c,N3,0:HS]=n
            thin[b,c,N3,HS:HS+1]=r3
            r=m*steps+b
            heads[r,h]=proj[r,:,h*128:h*128+HS]+n*gain[h]+shift[h]
        yield
    for c,m,h in chains:
        w1s[c]=w1[h]; w2s[c]=w2[h]; c2s[c]=c2[h]
        zus[c]=dot(kq[m*steps,h,:,0:AUG],w1[h].astype(bf16),NN)
    def copies(b):
        return [pltpu.make_async_copy(x.at[b],y.at[b],sems.at[i,b])
                for i,(x,y) in enumerate(((wide,wide_out),(held,state_out),(thin,thin_out)))]
    interleave(chain(0))
    restart(1)
    @pl.loop(1,steps)
    def _(b):
        interleave(chain(b),query(b-1))
        for copy in copies(b-1): copy.start()
        @pl.when(b+1<steps)
        def _():
            restart(b+1)
    interleave(query(steps-1))
    for copy in copies(steps-1): copy.start()
    for m in range(micro):
        s=slice(m*steps,(m+1)*steps)
        mixed[s]=jnp.concatenate([heads[s,h] for h in range(NH)],-1).astype(bf16)
    @pl.loop(0,steps)
    def _(b):
        for copy in copies(b): copy.wait()

def history_shapes(steps,C):
    return [((steps,C,3*MB,FI),f32),((steps,C,AUG+HS+2*MB,FI),bf16),((steps,C,3*MB,128),f32)]

def scan_forward(flags,proj,rate,w1,w2,c2,gain,shift):
    rows,_,lanes=proj.shape
    micro=flags.shape[0]
    NH=lanes//384; steps=rows//micro; C=micro*NH
    vm=pl.BlockSpec(memory_space=pltpu.VMEM); sm=pl.BlockSpec(memory_space=pltpu.SMEM); hbm=pl.BlockSpec(memory_space=pltpu.HBM)
    S=jax.ShapeDtypeStruct; V=pltpu.VMEM
    past=history_shapes(steps,C)
    out=pl.pallas_call(partial(forward_kernel,NH,micro,steps),
        in_specs=[sm]+[vm]*7, out_specs=[vm,hbm,hbm,hbm],
        out_shape=[S((rows,MB,NH*HS),bf16)]+[S(*x) for x in past],
        scratch_shapes=[V(*x) for x in past]+[pltpu.SemaphoreType.DMA((3,steps)),
                        V((rows,NH,2*MB,128),bf16),V((rows,NH,AUG,MB),bf16),V((rows,NH,MB,HS),f32),
                        V((C,AUG,FI),f32),V((C,HS,FI),f32),V((C,1,HS),f32),
                        V((C,2*MB,FI),f32),V((steps,C,1,HS),f32),V((rows,NH,MB,HS),f32)],
        compiler_params=pltpu.CompilerParams(vmem_limit_bytes=FORWARD_VMEM),
        cost_estimate=pl.CostEstimate(flops=18_000_000_000,bytes_accessed=12_000_000,transcendentals=0),
        name="inner_forward")(flags,proj,rate,w1,w2,c2,gain,shift)
    return out[0],tuple(out[1:])

def backward_kernel(NH, micro, steps, flags, dmix, proj, rate, gain, shift, wide_in, state_in, thin_in,
                    dproj, drate, dw1, dw2, dc2, dgain, dshift,
                    wide, held, thin, sems, kq, kqt, tt, p1, p2, pc, eb, p1h, p2h, ff1, qg1, qx2, qg2, qk, qsl, qcv, qd2, qu2, qu1, qx3):
    chains=[(c,m,h) for c,(m,h) in enumerate((m,h) for m in range(micro) for h in range(NH))]
    C=micro*NH
    tab=lower_table(); tabt=lower_table(True)
    def copies(b):
        return [pltpu.make_async_copy(x.at[b],y.at[b],sems.at[i,b])
                for i,(x,y) in enumerate(((wide_in,wide),(state_in,held),(thin_in,thin)))]
    @pl.loop(0,steps)
    def _(b):
        for copy in copies(steps-1-b): copy.start()
    load_rows(NH,proj,kq,kqt,tt,shift,2*MB)
    p1[...]=jnp.zeros(p1.shape,f32); p2[...]=jnp.zeros(p2.shape,f32); pc[...]=jnp.zeros(pc.shape,f32)
    p1h[...]=jnp.zeros(p1h.shape,bf16); p2h[...]=jnp.zeros(p2h.shape,bf16); ff1[...]=jnp.zeros(ff1.shape,f32)
    dw1[...]=jnp.zeros(dw1.shape,f32); dw2[...]=jnp.zeros(dw2.shape,f32); dc2[...]=jnp.zeros(dc2.shape,f32)
    drate[...]=jnp.zeros(drate.shape,f32)
    def query(b):
        o=lax.rem(b,2)
        du2b={};s2t={};d2={};dx3={};m2t={};ds2={};sl3={};du1b={};ds1={};m1t={};dqa={};x3={}
        for c,m,h in chains:
            r=m*steps+b
            n3=thin[b,c,N3,0:HS]; r3=thin[b,c,N3,HS:HS+1]
            hh=dmix[r,:,h*HS:(h+1)*HS]*gain[h]
            du2=r3*(hh-rsum(hh)*INV-n3*(rsum(hh*n3)*INV))
            qd2[o,c]=du2
            du2b[c]=du2.astype(bf16)
            qu2[o,c]=du2b[c]
        for c,m,h in chains:
            x,sl3[c]=gelu_and_slope(wide[b,c,U1])
            x3[c]=x.astype(bf16)
            qx3[o,c]=x3[c]
        yield
        for c,m,h in chains:
            s2t[c]=dot(held[b,c,X2],x3[c],NT)
            d2[c]=dot(du2b[c],thin[b,c,G2,0:HS].astype(bf16),NT)
            dx3[c]=dot(du2b[c],held[b,c,W2],NN)
        yield
        for c,m,h in chains:
            m2t[c]=(tabt*(s2t[c]+1.0)).astype(bf16)
            ds2[c]=(tab*d2[c]).astype(bf16)
        for c,m,h in chains:
            dx3[c]=dx3[c]-dot(ds2[c],held[b,c,X2],NN)
            qg2[o,c]=-dot(m2t[c],du2b[c],NN)
            qx2[o,c]=-dot(ds2[c],x3[c],TN)
        yield
        for c,m,h in chains:
            du1b[c]=(dx3[c]*sl3[c]).astype(bf16)
            qu1[o,c]=du1b[c]
        for c,m,h in chains:
            r=m*steps+b
            ds1[c]=dot(du1b[c],held[b,c,G1],NT)
            m1t[c]=dot(kq[r,h,0:MB],kq[r,h,MB:2*MB],NT)
            dqa[c]=dot(du1b[c],held[b,c,W1],NT)[:,0:HS]
        yield
        for c,m,h in chains:
            ds1[c]=(tab*ds1[c]).astype(bf16)
            m1t[c]=(tabt*m1t[c]).astype(bf16)
        for c,m,h in chains:
            r=m*steps+b
            qg1[o,c]=-dot(m1t[c],du1b[c],NN)
            dr=dmix[r,:,h*HS:(h+1)*HS]
            dproj[r,:,h*128:h*128+HS]=(dr+dqa[c]-dot(ds1[c],kq[r,h,0:MB,:],NN)[:,0:HS]).astype(bf16)
            qk[o,c]=-dot(ds1[c],kq[r,h,MB:2*MB,:],TN)[:,0:HS]
        yield
        for c,m,h in chains:
            sl,cv=gelu_slope_curve(wide[b,c,Z1])
            qsl[o,c]=sl
            qcv[o,c]=wide[b,c,DE]*cv
        yield
    def chain(b):
        o=lax.rem(b,2); pb=jnp.maximum(b-1,0)
        dde={};dz1a={};n2p={};gh={};dz2b={};dx={};dz1b={};base={};coef={};dk={};x2p={}
        for c,m,h in chains:
            gg1=qg1[o,c]+ff1[c]
            dde[c]=(gg1*qsl[o,c]).astype(bf16)
            dz1a[c]=gg1*qcv[o,c]
        yield
        for c,m,h in chains:
            gh[c]=dot(dde[c],held[b,c,W2],NT)
        for c,m,h in chains:
            n2p[c]=dot(held[b,c,X2],p2h[c],NT)
        yield
        for c,m,h in chains:
            r=m*steps+b
            g=gain[h]; gg=g*g
            zc=thin[b,c,ZC,0:HS]; r2=thin[b,c,ZC,HS:HS+1]; me=thin[b,c,ZC,HS+1:HS+2]; a=thin[b,c,ZC,HS+2:HS+3]
            n=zc*r2
            e=gg*n+g*tt[r,h]
            g2=r2*(e-me-n*a)
            hg=gh[c]+qg2[o,c]+(n2p[c]+pc[c])*(1.0/MB)
            rt=rate[r,:,h:h+1]
            q=rsum(hg*g2)
            drate[r,:,h:h+1]=q
            G=rt*hg
            mg=rsum(G)*INV; bb=rsum(G*n)*INV
            ds=r2*(G-mg-n*bb)
            eb[b,c]=ds
            dn=gg*ds-r2*(G*a+e*bb)
            dz2=r2*(dn-rsum(dn)*INV-n*(rsum(dn*n)*INV+rt*q*INV))
            dz2b[c]=dz2.astype(bf16)
            pc[c]=pc[c]-csum(qd2[o,c]+dz2)
        for c,m,h in chains:
            base[c]=dot(kq[m*steps+pb,h,0:MB,0:AUG],p1h[c],NN)
            coef[c]=dot(kq[m*steps+pb,h,0:MB],kq[m*steps+b,h],NT).astype(bf16)
        for c,m,h in chains:
            x2p[c]=dot(thin[b,c,G2,0:HS].astype(bf16),p2h[c],NN)
            dk[c]=dot(held[b,c,G1],p1h[c],NT)[:,0:HS]
        yield
        for c,m,h in chains:
            dx[c]=dot(dz2b[c],held[b,c,W2],NN)
        yield
        for c,m,h in chains:
            full=dx[c]+qx2[o,c]+x2p[c]*(1.0/MB)
            dz1b[c]=(dz1a[c]+full*qsl[o,c]).astype(bf16)
        both={}
        for c,m,h in chains:
            both[c]=jnp.concatenate([dz1b[c],qu1[o,c]],0)
            ff1[c]=(base[c]-dot(coef[c],both[c],NN))*(1.0/MB)
        yield
        for c,m,h in chains:
            r=m*steps+b
            p1[c]=p1[c]-dot(kqt[r,h],both[c],NN)
            p2[c]=p2[c]-dot(jnp.concatenate([qu2[o,c],thin[b,c,G2,0:HS].astype(bf16),dz2b[c]],0),jnp.concatenate([qx3[o,c],dde[c],held[b,c,X2]],0),TN)
        for c,m,h in chains:
            r=m*steps+b
            dy=eb[b,c]*gain[h]
            dkk=dy+qk[o,c]+dk[c]*(1.0/MB)+dot(dz1b[c],held[b,c,W1],NT)[:,0:HS]
            dproj[r,:,(NH+h)*128:(NH+h)*128+HS]=dkk.astype(bf16)
            dproj[r,:,(2*NH+h)*128:(2*NH+h)*128+HS]=(-dy).astype(bf16)
        for c,m,h in chains:
            p1h[c]=p1[c].astype(bf16); p2h[c]=p2[c].astype(bf16)
        yield
    def restart(b):
        for m in range(micro):
            @pl.when(flags[m,b]>0)
            def _():
                for h in range(NH):
                    c=m*NH+h
                    dw1[h]=dw1[h]-p1[c]; dw2[h]=dw2[h]-p2[c]; dc2[h]=dc2[h]-pc[c]
                    p1[c]=jnp.zeros((AUG,FI),f32); p2[c]=jnp.zeros((HS,FI),f32); pc[c]=jnp.zeros((1,HS),f32)
                    p1h[c]=jnp.zeros((AUG,FI),bf16); p2h[c]=jnp.zeros((HS,FI),bf16); ff1[c]=jnp.zeros((MB,FI),f32)
    for copy in copies(steps-1): copy.wait()
    interleave(query(steps-1))
    @pl.loop(0,steps-1)
    def _(back):
        b=steps-1-back
        for copy in copies(b-1): copy.wait()
        interleave(chain(b),query(b-1))
        restart(b)
    interleave(chain(0))
    restart(0)
    for h in range(NH):
        dg=jnp.zeros((1,HS),f32); ds=jnp.zeros((1,HS),f32)
        for m in range(micro):
            c=m*NH+h; s=slice(m*steps,(m+1)*steps)
            dr=dmix[s,:,h*HS:(h+1)*HS]
            zc=thin[:,c,ZC,0:HS]; r2=thin[:,c,ZC,HS:HS+1]
            g=gain[h][None]
            dm=eb[:,c]
            part=dr*thin[:,c,N3,0:HS]+dm*(2.0*g*(zc*r2)+tt[s,h])
            dg=dg+jnp.sum(jnp.sum(part,0),0,keepdims=True)
            ds=ds+jnp.sum(jnp.sum(dr+dm*g,0),0,keepdims=True)
        dgain[h]=dg; dshift[h]=ds
    for p in range(3*NH):
        dproj[:,:,p*128+HS:(p+1)*128]=jnp.zeros((micro*steps,MB,128-HS),bf16)
    rt=rate[...]
    drate[...]=drate[...]*rt*(1.0-HS*rt)

def scan_backward(flags,dmix,proj,rate,gain,shift,hist):
    rows,_,lanes=proj.shape
    micro=flags.shape[0]
    NH=lanes//384; steps=rows//micro; C=micro*NH
    vm=pl.BlockSpec(memory_space=pltpu.VMEM); sm=pl.BlockSpec(memory_space=pltpu.SMEM); hbm=pl.BlockSpec(memory_space=pltpu.HBM)
    S=jax.ShapeDtypeStruct; V=pltpu.VMEM
    out=pl.pallas_call(partial(backward_kernel,NH,micro,steps),
        in_specs=[sm]+[vm]*5+[hbm]*3, out_specs=[vm]*7,
        out_shape=[S((rows,MB,lanes),bf16),S((rows,MB,8),f32),S((NH,AUG,FI),f32),S((NH,HS,FI),f32),S((NH,1,HS),f32),S((NH,1,HS),f32),S((NH,1,HS),f32)],
        scratch_shapes=[V(*x) for x in history_shapes(steps,C)]+[pltpu.SemaphoreType.DMA((3,steps)),V((rows,NH,2*MB,128),bf16),V((rows,NH,AUG,2*MB),bf16),V((rows,NH,MB,HS),f32),
                        V((C,AUG,FI),f32),V((C,HS,FI),f32),V((C,1,HS),f32),V((steps,C,MB,HS),f32),
                        V((C,AUG,FI),bf16),V((C,HS,FI),bf16),V((C,MB,FI),f32),
                        V((2,C,MB,FI),f32),V((2,C,MB,FI),f32),V((2,C,MB,HS),f32),V((2,C,MB,HS),f32),V((2,C,MB,FI),f32),V((2,C,MB,FI),f32),
                        V((2,C,MB,HS),f32),V((2,C,MB,HS),bf16),V((2,C,MB,FI),bf16),V((2,C,MB,FI),bf16)],
        compiler_params=pltpu.CompilerParams(vmem_limit_bytes=BACKWARD_VMEM),
        cost_estimate=pl.CostEstimate(flops=1000,bytes_accessed=1000,transcendentals=0),
        name="inner_backward")(flags,dmix,proj,rate,gain,shift,*hist)
    return out[0],out[1],tuple(out[2:])

def gelu_full(v):
    v2,t,hp=gelu_parts(v)
    q=(1.0-t*t)*(0.5*GS+(1.5*GS*GC)*v2)
    return v*hp, hp+v*q

def struct(shape, dtype):
    return jax.ShapeDtypeStruct(shape, dtype)

def call(kernel, name, flops, arrays, shapes, scratch=()):
    vm=pl.BlockSpec(memory_space=pltpu.VMEM); sm=pl.BlockSpec(memory_space=pltpu.SMEM)
    specs=[sm if a.ndim==1 else vm for a in arrays]
    moved=1000 if flops<2000 else sum(a.size*a.dtype.itemsize for a in arrays)+sum(s.size*s.dtype.itemsize for s in shapes)
    return pl.pallas_call(kernel, in_specs=specs, out_specs=[vm]*len(shapes), out_shape=list(shapes), scratch_shapes=list(scratch),
        compiler_params=pltpu.CompilerParams(vmem_limit_bytes=SMALL_VMEM),
        cost_estimate=pl.CostEstimate(flops=flops,bytes_accessed=moved,transcendentals=0), name=name)(*arrays)

def bits(n):
    return n.bit_length()-1

def near_slot(peer, m, rank, pair, micro):
    return peer*(micro*pair)+m*pair+rank

def far_slot(peer, m, rank, pair, micro, size, part):
    q=pair//size
    return lax.shift_right_logical(rank,bits(q))*part+peer*(micro*q)+m*q+(rank&(q-1))

def send_kernel(pair, size, given, owner, x, up, sent_x, sent_up, recv_col, recv_row, turn_row, fin_col, end_col):
    micro,tok=given.shape
    rows=micro*tok
    part=rows//size
    at=lax.broadcasted_iota(jnp.int32,(rows,tok),0)
    low=lax.broadcasted_iota(jnp.int32,(tok,tok),0); high=lax.broadcasted_iota(jnp.int32,(tok,tok),1)
    ax=None
    for m in range(micro):
        span=slice(m*tok,(m+1)*tok)
        along=jnp.broadcast_to(given[m:m+1,:].astype(f32),(tok,tok))
        down=along.T
        row=jnp.sum(jnp.where(down<along,1.0,0.0),0,keepdims=True).astype(jnp.int32)
        col=jnp.sum(jnp.where(along<down,1.0,0.0),1,keepdims=True).astype(jnp.int32)
        split=lambda r:(lax.shift_right_logical(r,bits(pair)),r&(pair-1))
        peer,rank=split(row)
        hot=jnp.where(at==near_slot(peer,m,rank,pair,micro),1.0,0.0).astype(bf16)
        a=dot(hot,x[m],NN); b=dot(hot,up[m],NN)
        if m==0: ax,au=a,b
        else: ax,au=ax+a,au+b
        peer,rank=split(col)
        fin_col[span,:]=near_slot(peer,m,rank,pair,micro)
        end_col[span,:]=far_slot(peer,m,rank,pair,micro,size,part)
        anchor=lax.shift_right_logical(owner[m:m+1,:],bits(tok))
        along=jnp.broadcast_to(anchor.astype(f32),(tok,tok))
        down=along.T
        same=jnp.where(along==down,1.0,0.0)
        col=jnp.sum(jnp.where(high<low,same,0.0),1,keepdims=True).astype(jnp.int32)
        row=jnp.sum(jnp.where(low<high,same,0.0),0,keepdims=True).astype(jnp.int32)
        recv_col[span,:]=near_slot(down[:,0:1].astype(jnp.int32),m,col,pair,micro)
        recv_row[:,span]=near_slot(anchor,m,row,pair,micro)
        turn_row[:,span]=far_slot(anchor,m,row,pair,micro,size,part)
    sent_x[...]=ax.astype(bf16)
    sent_up[...]=au.astype(bf16)

def send_rows(pair, size, given, owner, x, up):
    micro,tok,width=x.shape
    rows=micro*tok
    i=jnp.int32
    return call(partial(send_kernel,pair,size),"send_rows",2_000_000_000,[given,owner,x,up],
        [struct((rows,width),bf16),struct((rows,width),bf16),struct((rows,1),i),struct((1,rows),i),struct((1,rows),i),struct((rows,1),i),struct((rows,1),i)])

def hot_from_col(col, columns):
    n=col.shape[0]
    return jnp.where(lax.broadcasted_iota(jnp.int32,(n,columns),1)==col,1.0,0.0).astype(bf16)

def hot_from_row(row, count, first=0):
    n=row.shape[1]
    return jnp.where(lax.broadcasted_iota(jnp.int32,(count,n),0)+first==row,1.0,0.0).astype(bf16)

def project_kernel(arrived, col, ngain, qkv, ratew, rateb, resid, normed, proj, rate):
    rows=arrived.shape[0]
    r=dot(hot_from_col(col[...],rows),arrived[...],NN)
    resid[...]=r.astype(bf16)
    n=(r*lax.rsqrt(rsum(r*r)*(1.0/r.shape[1])+EPS)*ngain[...]).astype(bf16)
    normed[...]=n
    rate[...]=(1.0/HS)/(1.0+jnp.exp(-(dot(n,ratew[...],NN)+rateb[...])))
    proj[...]=dot(n,qkv[...],NT)

def project(arrived, col, ngain, qkv, ratew, rateb):
    rows,width=arrived.shape
    return call(project_kernel,"project",1_500_000_000,[arrived,col,ngain,qkv,ratew,rateb],
        [struct((rows,width),bf16),struct((rows,width),bf16),struct((rows,qkv.shape[0]),f32),struct((rows,ratew.shape[1]),f32)])

def middle_kernel(T, cut, me, col, row, turn, arrived, mixed, normed, resid, post, gateout, fgain, swiglu, down,
                  up, out_sent, act, sgrad, nmid, gated, mgrad, hgrad, ggrad, dpg, dpb, dfg, base, gpart, rpart,
                  gpre, hid, feed, mid, stats, pbuf):
    c=pl.program_id(0)
    rows,wide=resid.shape
    hw=mixed.shape[2]
    width=T*hw
    half=sgrad.shape[1]//2
    def flat(ref,i,lead=()):
        w=ref[i]
        return w.reshape(w.shape[0]*w.shape[1],w.shape[2])
    def vectors(i):
        v=post[i,0].astype(f32)
        return v[0:1,0:hw]+v[1:2,0:hw]+v[2:3,0:hw], v[3:4,0:hw]+v[4:5,0:hw]+v[5:6,0:hw]
    @pl.when(c==0)
    def _():
        up[...]=dot(hot_from_col(col[...],rows),arrived[...],NN).astype(bf16)
        center=sum(rsum(mixed[i].astype(f32)) for i in range(T))*(1.0/width)
        square=0.0
        for i in range(T):
            x=mixed[i].astype(f32)-center
            square=square+rsum(x*x)
        inv=lax.rsqrt(square*(1.0/width)+EPS)
        stats[:,0:1]=center
        stats[:,1:2]=inv
        mixer=None
        for i in range(T):
            w=flat(gateout,i)
            pg,pb=vectors(i)
            pre=dot(normed[...],w[0:hw],NT)
            gpre[i]=pre
            g=(((mixed[i].astype(f32)-center)*inv*pg+pb)*gelu(pre)).astype(bf16)
            @pl.when(me[0]==i)
            def _():
                gated[...]=g
            y=dot(g,w[hw:2*hw],NN)
            mixer=y if mixer is None else mixer+y
        h=resid[...].astype(f32)+mixer
        hid[...]=h
        nmid[...]=(h*lax.rsqrt(rsum(h*h)*(1.0/wide)+EPS)*fgain[...]).astype(bf16)
        feed[...]=jnp.zeros((rows,wide),f32)
        mid[...]=jnp.zeros((rows,wide),f32)
    block=rows//2
    @pl.loop(0,2)
    def _(b):
        at=pl.ds(pl.multiple_of(b*block,block),block)
        nm=nmid[at,:]
        dn=flat(down,0)
        w=swiglu[0]
        unit=w.shape[1]//2
        wg=w[:,0:unit].reshape(half,wide)
        wu=w[:,unit:2*unit].reshape(half,wide)
        gh=dot(nm,wg,NT)
        uh=dot(nm,wu,NT)
        da=dot(up[at,:],dn,NT)
        sg=1.0/(1.0+jnp.exp(-gh))
        silu=gh*sg
        a=(silu*uh).astype(bf16)
        s1=(da*uh*sg*(1.0+gh*(1.0-sg))).astype(bf16)
        s2=(da*silu).astype(bf16)
        @pl.when(me[0]==c)
        def _():
            act[at,:]=a
            sgrad[at,0:half]=s1
            sgrad[at,half:2*half]=s2
        mid[at,:]=mid[at,:]-(dot(s1,wg,NN)+dot(s2,wu,NN))
        feed[at,:]=feed[at,:]-dot(a,dn,NN)
    @pl.when(c==T-1)
    def _():
        h=hid[...]
        own=(h-feed[...]).astype(bf16)
        out_sent[...]=dot(hot_from_row(row[...],rows),own,NN).astype(bf16)
        sc=lax.rsqrt(rsum(h*h)*(1.0/wide)+EPS)
        m=-mid[...]
        dfg[...]=csum(m*h*sc)
        ms=m*fgain[...]
        hg=up[...].astype(f32)+sc*ms-h*(sc*sc*sc*(rsum(ms*h)*(1.0/wide)))
        full=hg.astype(bf16)
        mgrad[...]=full
        part=base.shape[0]
        hot=hot_from_row(turn[...],part,me[0]*part)
        base[...]=dot(hot,full,NN)+dot(hot,(hg-full.astype(f32)).astype(bf16),NN)
        rpart[...]=dot(hot,resid[...],NN)
        center=stats[:,0:1]; inv=stats[:,1:2]
        s1=0.0; s2=0.0
        for i in range(T):
            w=flat(gateout,i)
            pgn,pb=vectors(i)
            std=(mixed[i].astype(f32)-center)*inv
            a,slope=gelu_full(gpre[i])
            gg=dot(full,w[hw:2*hw],NT)
            gr=(gg*(std*pgn+pb)*slope).astype(bf16)
            y=dot(dot(hot,gr,NN).astype(bf16),w[0:hw],NN)
            if i==0: gpart[...]=y
            else: gpart[...]=gpart[...]-(-y)
            pg=gg*a
            p=pg*pgn
            pbuf[i]=p
            s1=s1+rsum(p); s2=s2+rsum(p*std)
            @pl.when(me[0]==i)
            def _():
                ggrad[...]=gr
                dpg[...]=csum(pg*std); dpb[...]=csum(pg)
        std=(mixed[me[0]].astype(f32)-center)*inv
        hgrad[...]=inv*(pbuf[me[0]]-s1*(1.0/width)-std*(s2*(1.0/width)))

def middle(me, col, row, turn, arrived, mixed, normed, resid, weights, fgain):
    T,rows,hw=mixed.shape; wide=resid.shape[1]; D,tall=weights.shape[1:3]
    a,b,g,p=weight_cuts(tall)
    half=a*D//2
    whole=lambda x:pl.BlockSpec(x.shape,lambda c,n=len(x.shape):(0,)*n,pipeline_mode=pl.Buffered(1))
    specs=[pl.BlockSpec(memory_space=pltpu.SMEM)]+[whole(x) for x in (col,row,turn,arrived,mixed,normed,resid)]
    specs+=[pl.BlockSpec((T,1,p,wide),lambda c:(0,0,(a+b+g)//p,0),pipeline_mode=pl.Buffered(1)),
            pl.BlockSpec((T,D,g,wide),lambda c:(0,0,(a+b)//g,0),pipeline_mode=pl.Buffered(1)),
            whole(fgain),
            pl.BlockSpec((1,D,a,wide),lambda c:(c,0,0,0)),
            pl.BlockSpec((1,D,b,wide),lambda c:(c,0,a//b,0))]
    shapes=[struct((rows,wide),bf16),struct((rows,wide),bf16),struct((rows,half),bf16),struct((rows,2*half),bf16),struct((rows,wide),bf16),
            struct((rows,hw),bf16),struct((rows,wide),bf16),struct((rows,hw),f32),struct((rows,hw),bf16),
            struct((1,hw),f32),struct((1,hw),f32),struct((1,wide),f32)]+[struct((rows//T,wide),f32)]*3
    V=pltpu.VMEM
    return pl.pallas_call(partial(middle_kernel,T,None),
        grid=(T,), in_specs=specs, out_specs=[pl.BlockSpec(s.shape,lambda c,n=len(s.shape):(0,)*n,pipeline_mode=pl.Buffered(1)) for s in shapes], out_shape=shapes,
        scratch_shapes=[V((T,rows,hw),f32),V((rows,wide),f32),V((rows,wide),f32),V((rows,wide),f32),V((rows,128),f32),V((T,rows,hw),f32)],
        compiler_params=pltpu.CompilerParams(vmem_limit_bytes=MIDDLE_VMEM,dimension_semantics=("arbitrary",)),
        cost_estimate=pl.CostEstimate(flops=14_000_000_000,bytes_accessed=25_000_000,transcendentals=0),name="middle")(
        me,col,row,turn,arrived,mixed,normed,resid,weights,weights,fgain,weights,weights)

def thirds(x):
    high=x.astype(bf16).astype(f32)
    rest=x-high
    center=rest.astype(bf16).astype(f32)
    return [high,center,rest-center]

def pack_kernel(count, d, wg, wu, down, turned, out, pgain, pbias, piece):
    unit=wg.shape[1]; width=down.shape[1]; hw=turned.shape[0]
    piece[0:unit,:]=wg[...].astype(f32).T.astype(bf16)
    piece[unit:2*unit,:]=wu[...].astype(f32).T.astype(bf16)
    at=2*unit
    n=down.shape[0]//count
    piece[at:at+n,:]=down[pl.ds(pl.multiple_of(d[0]*n,n),n),:]
    at+=n
    n=2*hw//count
    @pl.when(d[0]<count//2)
    def _():
        piece[at:at+n,:]=turned[pl.ds(pl.multiple_of(d[0]*n,n),n),:]
    @pl.when(d[0]>=count//2)
    def _():
        piece[at:at+n,:]=out[pl.ds(pl.multiple_of((d[0]-count//2)*n,n),n),:]
    at+=n
    rows=jnp.concatenate(thirds(pgain[...])+thirds(pbias[...])+[jnp.zeros((10,hw),f32)],0)
    piece[at:at+16,:]=jnp.concatenate([rows,jnp.zeros((16,width-hw),f32)],1).astype(bf16)

def pack_weights(count, d, wg, wu, down, turned, out, pgain, pbias):
    unit=wg.shape[1]; width=down.shape[1]
    tall=2*unit+(down.shape[0]+2*turned.shape[0])//count+16
    return call(partial(pack_kernel,count),"pack_weights",100_000_000,[d,wg,wu,down,turned,out,pgain,pbias],[struct((tall,width),bf16)])[0]

def weight_cuts(tall):
    unit=tall//16
    return 8*unit,4*unit,3*unit,unit

def in_part_kernel(T, me, row, dproj, logit, qkv, ratew, *sums):
    lg=logit[...]
    y=dot(dproj[...],qkv[...],NN)+dot(lg.astype(bf16),ratew[...],NT)
    y=y.astype(bf16)
    part=y.shape[0]//T
    for k in range(T):
        sums[k][...]=dot(hot_from_row(row[...],part,lax.rem(me[0]+k,T)*part),y,NN).astype(bf16)

def in_part(T, me, row, dproj, logit, qkv, ratew):
    rows=dproj.shape[0]; width=qkv.shape[1]
    return call(partial(in_part_kernel,T),"in_part",1000,[me,row,dproj,logit,qkv,ratew],[struct((rows//T,width),bf16)]*T)

def early_kernel(count, act, up, nmid, sgrad, gated, mgrad, normed, ggrad, *outs):
    width=nmid.shape[1]
    og=jnp.concatenate([dot(gated[...],mgrad[...],TN),dot(ggrad[...],normed[...],TN)],0).astype(bf16)
    dn=dot(act[...],up[...],TN).astype(bf16)
    left=dot(nmid[...],sgrad[:,0:width],TN).astype(bf16)
    right=dot(nmid[...],sgrad[:,width:],TN).astype(bf16)
    third=width//3
    right=jnp.concatenate([right[i*third:(i+1)*third] for i in range(3)],1)
    pieces=(left,right,dn,og)
    if len(outs)==1:
        at=0
        for y in pieces:
            n=y.shape[0]//count
            for d in range(count):
                outs[0][d,at:at+n]=y[d*n:(d+1)*n]
            at+=n
    else:
        for o,y in zip(outs,pieces): o[...]=y

def aligned(count, sizes):
    return all(n%(16*count)==0 for n in sizes)

def early_grads(count, act, up, nmid, sgrad, gated, mgrad, normed, ggrad):
    width=nmid.shape[1]; half=act.shape[1]; hw=gated.shape[1]
    sizes=(width,width//3,half,2*hw)
    whole=aligned(count,sizes)
    shapes=[struct((count,sum(sizes)//count,width),bf16)] if whole else [struct((n,width),bf16) for n in sizes]
    out=call(partial(early_kernel,count),"early_grads",1000,[act,up,nmid,sgrad,gated,mgrad,normed,ggrad],shapes)
    return out[0] if whole else jnp.concatenate([y.reshape(count,-1,width) for y in out],1)

def late_kernel(heads, count, dproj, normed, logit, dw1, dw2, dc2, dgain, dshift, dpg, dpb, dfg, *refs):
    outs=refs[:-1]; rest=refs[-1]
    width=normed.shape[1]
    n=normed[...]
    packed=jnp.concatenate([dot(dproj[:,g*128:(g+1)*128],n,TN)[0:HS] for g in range(3*heads)],0)
    lg=logit[...]
    rest[...]=jnp.zeros(rest.shape,f32)
    for h in range(heads):
        rest[0:HS,h*FI:(h+1)*FI]=dw1[h,0:HS]
        rest[HS:2*HS,h*FI:(h+1)*FI]=dw2[h]
    rest[2*HS:2*HS+8,:]=dot(lg.astype(bf16),n,TN)
    for h in range(heads):
        rest[2*HS+8:2*HS+9,h*FI:(h+1)*FI]=dw1[h,HS:HS+1]
        rest[2*HS+10:2*HS+11,h*HS:(h+1)*HS]=dc2[h]
        rest[2*HS+11:2*HS+12,h*HS:(h+1)*HS]=dgain[h]
        rest[2*HS+12:2*HS+13,h*HS:(h+1)*HS]=dshift[h]
    hw=dpg.shape[1]
    rest[2*HS+9:2*HS+10,:]=dfg[...]
    rest[2*HS+13:2*HS+14,0:hw]=dpg[...]
    rest[2*HS+14:2*HS+15,0:hw]=dpb[...]
    rest[2*HS+15:2*HS+16,0:lg.shape[1]]=csum(lg)
    if len(outs)==1:
        per=packed.shape[0]//count; more=rest.shape[0]//count
        for d in range(count):
            outs[0][d,0:per+more]=jnp.concatenate([packed[d*per:(d+1)*per],rest[d*more:(d+1)*more,:]],0).astype(bf16)
    else:
        outs[0][...]=packed.astype(bf16); outs[1][...]=rest[...].astype(bf16)

def late_grads(count, dproj, normed, logit, dw1, dw2, dc2, dgain, dshift, dpg, dpb, dfg):
    heads=dw1.shape[0]; width=normed.shape[1]
    sizes=(3*heads*HS,3*HS)
    whole=all(n%(8*count)==0 for n in sizes) and sum(sizes)%(16*count)==0
    shapes=[struct((count,sum(sizes)//count,width),bf16)] if whole else [struct((n,width),bf16) for n in sizes]
    out=call(partial(late_kernel,heads,count),"late_grads",1000,[dproj,normed,logit,dw1,dw2,dc2,dgain,dshift,dpg,dpb,dfg],
        shapes,[pltpu.VMEM((3*HS,width),f32)])
    return out[0] if whole else jnp.concatenate([y.reshape(count,-1,width) for y in out],1)

def in_rows_kernel(T, *refs):
    got=refs[:T]
    base,gpart,rpart,ngain=refs[T:T+4]
    outs=refs[T+4:]
    part,wide=base.shape
    r=rpart[...]
    sc=lax.rsqrt(rsum(r*r)*(1.0/wide)+EPS)
    s=gpart[...]
    for k in range(T):
        s=s+got[k][...].astype(f32)
    g=csum(s*(r*sc))
    high=g.astype(bf16)
    rest=g-high.astype(f32)
    center=rest.astype(bf16)
    three=jnp.concatenate([high.astype(f32),center.astype(f32),rest-center.astype(f32),jnp.zeros((13,wide),f32)],0)
    s=s*ngain[...]
    y=(base[...]+sc*s-r*(sc*sc*sc*(rsum(s*r)*(1.0/wide)))).astype(bf16)
    three=three.astype(bf16)
    if len(outs)==1:
        count=outs[0].shape[0]; lines=part//count
        for d in range(count):
            outs[0][d,0:lines]=y[d*lines:(d+1)*lines]
            outs[0][d,lines:lines+16]=three
    else:
        outs[0][...]=y; outs[1][...]=three

def in_rows(count, got, base, gpart, rpart, ngain):
    part,wide=base.shape; T=len(got)
    out=call(partial(in_rows_kernel,T),"in_rows",1000,[*got,base,gpart,rpart,ngain],
        [struct((count,part//count+16,wide),bf16)] if aligned(count,(part,)) else [struct((part,wide),bf16),struct((16,wide),bf16)])
    if len(out)==1: return out[0]
    return jnp.concatenate([out[0].reshape(count,-1,wide),jnp.broadcast_to(out[1][None],(count,16,wide))],1)

def settle_kernel(micro, col, got, out):
    rows=got.shape[0]; tok=rows//micro
    for m in range(micro):
        out[m]=dot(hot_from_col(col[m*tok:(m+1)*tok,:],rows),got[...],NN).astype(bf16)

def settle(micro, col, got, name):
    rows,wide=got.shape
    return call(partial(settle_kernel,micro),name,1000,[col,got],[struct((micro,rows//micro,wide),bf16)])[0]

from jax.sharding import PartitionSpec as P

MICRO=2

def restart_flags(lengths, steps):
    k = jnp.arange(lengths.shape[1], dtype=jnp.int32)
    starts = jnp.sum(jnp.where((k[None, :] < k[:, None])[None], lengths[:, None, :], 0), 2)
    at = jnp.arange(steps, dtype=jnp.int32) * MB
    hit = (starts[:, None, :] == at[None, :, None]) & (lengths[:, None, :] > 0)
    return jnp.pad(jnp.any(hit, 2).astype(jnp.int32), ((0, 0), (0, 1)))

def pad_heads(array, axis):
    shape = array.shape
    split = shape[:axis] + (shape[axis] // HS, HS) + shape[axis + 1:]
    padded = jnp.pad(array.reshape(split), [(0, 0)] * (axis + 1) + [(0, HS)] + [(0, 0)] * (len(shape) - axis - 1))
    return padded.reshape(shape[:axis] + (2 * shape[axis],) + shape[axis + 1:])

def drop_pad(array, axis):
    shape = array.shape
    split = array.reshape(shape[:axis] + (shape[axis] // 128, 128) + shape[axis + 1:])
    kept = lax.slice_in_dim(split, 0, HS, axis=axis + 1)
    return kept.reshape(shape[:axis] + (shape[axis] // 2,) + shape[axis + 1:])

def swap(array, axis="dp"):
    return lax.all_to_all(array, axis, split_axis=0, concat_axis=0, tiled=True)

def turn(array, k):
    size = lax.axis_size("tensor")
    return lax.ppermute(array, "tensor", [(i, (i + k) % size) for i in range(size)])

def split_three(array):
    high = array.astype(bf16)
    rest = array - high.astype(f32)
    middle_part = rest.astype(bf16)
    return [high, middle_part, (rest - middle_part.astype(f32)).astype(bf16)]

def gather_weights(swiglu, down, gate, out, post_gain, post_bias):
    count = lax.axis_size("dp")
    size = lax.axis_size("tensor")
    d = lax.axis_index("dp")
    width = out.shape[1]
    def rows_of(array):
        piece = array.shape[0] // count
        return lax.dynamic_slice_in_dim(array, d * piece, piece, 0)
    piece = swiglu.shape[2] // count
    if count == 8:
        cut = lax.dynamic_slice_in_dim(swiglu, d * piece, piece, 2)
        mine = pack_weights(
            count, d.astype(jnp.int32).reshape(1), cut[:, 0], cut[:, 1], down, gate.T, out, post_gain[None], post_bias[None]
        )
        return lax.all_gather(mine, ("tensor", "dp")).reshape(size, count, -1, width)
    turned = lax.dynamic_slice_in_dim(swiglu, d * piece, piece, 2).transpose(1, 2, 0)
    post = jnp.stack(split_three(post_gain) + split_three(post_bias))
    post = jnp.pad(post, ((0, 10), (0, width - post.shape[1])))
    lines = [turned.reshape(-1, width), rows_of(down), rows_of(jnp.concatenate([gate.T, out], 0))]
    lines.append(rows_of(jnp.concatenate([post] * 8, 0)))
    got = lax.all_gather(jnp.concatenate(lines, 0), ("tensor", "dp"))
    first = got[:, :2 * piece].reshape(size, 8, count // 8, 2, piece, width)
    parts = [jnp.swapaxes(first, 2, 3).reshape(size, 8, -1, width)]
    at = 2 * piece
    for x in lines[1:]:
        parts.append(got[:, at:at + x.shape[0]].reshape(size, 8, -1, width))
        at += x.shape[0]
    return jnp.concatenate(parts, 2)

def shards(
    inputs, cotangent, lengths, owner_rows, given_rows, norm_gain, qkv_weight, rate_weight, rate_bias,
    inner_first, inner_first_bias, inner_second, inner_second_bias, inner_gain, inner_shift, gate_weight,
    post_gain, post_bias, out_weight, ffn_gain, swiglu_weight, down_weight,
):
    tok = inputs.shape[1]
    width = inputs.shape[2]
    rows = MICRO * tok
    blocks = rows // MB
    steps = tok // MB
    heads = rate_weight.shape[1]
    size = lax.axis_size("tensor")
    pair = tok // lax.axis_size("dp")
    me = lax.axis_index("tensor").astype(jnp.int32).reshape(1)
    weights = gather_weights(swiglu_weight, down_weight, gate_weight, out_weight, post_gain, post_bias)
    sent_in, sent_up, recv_col, recv_row, turn_row, fin_col, end_col = send_rows(
        pair, size, given_rows, owner_rows, inputs, cotangent
    )
    arrived_in = swap(sent_in)
    arrived_up = swap(sent_up)
    flags = restart_flags(lengths, steps)
    qkv_pad = pad_heads(qkv_weight.transpose(1, 2, 0).reshape(-1, width), 0)
    rate_pad = jnp.pad(rate_weight, ((0, 0), (0, 8 - heads)))
    bias_pad = jnp.pad(rate_bias, (0, 8 - heads))[None]
    first = jnp.concatenate(
        [inner_first, inner_first_bias[:, None], jnp.zeros((heads, AUG - HS - 1, FI), f32)], 1
    )
    second = jnp.swapaxes(inner_second - jnp.mean(inner_second, -1, keepdims=True), 1, 2)
    second_bias = (inner_second_bias - jnp.mean(inner_second_bias, -1, keepdims=True))[:, None]
    gain = inner_gain[:, None]
    shift = inner_shift[:, None]
    resid, normed, projected, rates = project(arrived_in, recv_col, norm_gain[None], qkv_pad, rate_pad, bias_pad)
    projected = projected.reshape(blocks, MB, -1)
    rate_blocks = rates.reshape(blocks, MB, -1)
    own, past = scan_forward(flags, projected, rate_blocks, first, second, second_bias, gain, shift)
    mixed = lax.all_gather(own.reshape(rows, -1), "tensor")
    (
        up, out_sent, act, sgrad, nmid, gated, mixer_grad, heads_grad, gate_grad, grad_pgain, grad_pbias, gain_mid,
        base, gate_part, resid_part
    ) = middle(
        me, recv_col, recv_row, turn_row, arrived_up, mixed, normed, resid, weights, ffn_gain[None]
    )
    count = lax.axis_size("dp")
    def exchanged(chunks):
        return swap(chunks.reshape(-1, width)).reshape(chunks.shape)
    def summed(got):
        return jnp.sum(got.astype(f32), 0).astype(bf16)
    early_in = early_grads(count, act, up, nmid, sgrad, gated, mixer_grad, normed, gate_grad)
    heads_grad, early_in = lax.optimization_barrier((heads_grad, early_in))
    early_got = exchanged(early_in)
    dproj, drate, carry = scan_backward(
        flags, heads_grad.reshape(blocks, MB, -1), projected, rate_blocks, gain, shift, past
    )
    dproj, early_got = lax.optimization_barrier((dproj.reshape(rows, -1), early_got))
    dproj, early_sum = lax.optimization_barrier((dproj, summed(early_got)))
    early = lax.all_gather(early_sum, "dp")
    logit = drate.reshape(rows, -1)
    late_in = late_grads(count, dproj, normed, logit, *carry, grad_pgain, grad_pbias, gain_mid)
    dproj, late_in = lax.optimization_barrier((dproj, late_in))
    late_got = exchanged(late_in)
    sums = in_part(size, me, turn_row, dproj, logit, qkv_pad, rate_pad)
    got = [sums[0]] + [turn(sums[k], k) for k in range(1, size)]
    late_sum = summed(late_got)
    got, late_sum = lax.optimization_barrier((got, late_sum))
    late_sum, early = lax.optimization_barrier((late_sum, early))
    late = lax.all_gather(late_sum, "dp")
    cut = 3 * heads * HS // count
    back = in_rows(count, got, base, gate_part, resid_part, norm_gain[None])
    part = rows // size
    sent, out_sent = lax.optimization_barrier((exchanged(back), out_sent))
    lines = part // count
    gains = jnp.concatenate(split_three(jnp.sum(sent[:, lines:lines + 3].astype(f32), (0, 1))[None]), 0)
    mine = jnp.concatenate([sent[:, :lines].reshape(part, width), jnp.pad(gains, ((0, 13), (0, 0)))], 0)
    final = lax.all_gather(mine, "tensor")
    input_grad = settle(MICRO, end_col, final[:, :part].reshape(rows, width), "settle_in")
    norm_total = jnp.sum(final[:, part:part + 3].astype(f32), (0, 1))
    outputs = settle(MICRO, fin_col, swap(out_sent), "settle_out")
    big = late[:, :cut].astype(f32).reshape(3, heads * HS, width)
    rest = late[:, cut:].astype(f32).reshape(-1, width)
    third = width // 3
    edges = [0]
    for lines_of in (width, third, act.shape[1], 2 * heads * HS):
        edges.append(edges[-1] + lines_of // count)
    left, right, grad_down, pair_grads = [
        early[:, edges[i]:edges[i + 1]].astype(f32).reshape(-1, width) for i in range(4)
    ]
    right = jnp.concatenate([right[:, i * third:(i + 1) * third] for i in range(3)], 0)
    grad_swiglu = jnp.concatenate([left, right], 1)
    def stack(lines):
        return lines.reshape(HS, heads, FI).transpose(1, 0, 2)
    small = rest[2 * HS:2 * HS + 16]
    def per_head(i):
        return small[i, :heads * HS].reshape(heads, HS)
    return (
        outputs,
        input_grad,
        norm_total,
        big.transpose(2, 0, 1),
        small[:heads].T,
        small[15, :heads],
        stack(rest[:HS]),
        small[8].reshape(heads, FI),
        jnp.swapaxes(stack(rest[HS:2 * HS]), 1, 2),
        per_head(10),
        per_head(11),
        per_head(12),
        pair_grads[heads * HS:].T,
        small[13, :heads * HS],
        small[14, :heads * HS],
        pair_grads[:heads * HS],
        small[9],
        grad_swiglu.reshape(swiglu_weight.shape),
        grad_down,
    )

def solution(mesh):
    rows, heads, columns = P(None, "dp", None), P("tensor", None), P(None, "tensor")
    table = P(None, "dp")
    vector = P("tensor")
    cube = P("tensor", None, None)
    wide = P(None, None, "tensor")
    return jax.shard_map(
        shards,
        mesh=mesh,
        in_specs=(
            rows, rows, table, table, table, P(), wide, columns, vector, cube, heads, cube, heads, heads, heads,
            columns, vector, vector, heads, P(), wide, heads,
        ),
        out_specs=(
            rows, rows, P(), wide, columns, vector, cube, heads, cube, heads, heads, heads, columns, vector, vector,
            heads, P(), wide, heads,
        ),
        check_vma=False,
    )
```

```python
from functools import partial
import jax, jax.numpy as jnp
from jax import lax
from jax.experimental import pallas as pl
from jax.experimental.pallas import tpu as pltpu

HS=64; MB=16; FI=256; EPS=1e-6
GS=0.7978845608028654; GC=0.044715
bf16=jnp.bfloat16; f32=jnp.float32
NN=((1,),(0,)); NT=((1,),(1,)); TN=((0,),(0,))
def dot(a,b,dims): return lax.dot_general(a,b,(dims,((),())),preferred_element_type=f32)
def rsum(x): return jnp.sum(x,-1,keepdims=True)
def csum(x): return jnp.sum(x,0,keepdims=True)
AUG=80
INV=1.0/HS
FORWARD_VMEM=58<<20
BACKWARD_VMEM=58<<20
MIDDLE_VMEM=38<<20
SMALL_VMEM=20<<20

def gelu_parts(v):
    v2=v*v
    t=jnp.tanh(v*(GS+(GS*GC)*v2))
    hp=0.5+0.5*t
    return v2,t,hp
def gelu(v):
    _,_,hp=gelu_parts(v)
    return v*hp
def gelu_and_slope(v):
    v2,t,hp=gelu_parts(v)
    q=(1.0-t*t)*(0.5*GS+(1.5*GS*GC)*v2)
    return v*hp, hp+v*q
def gelu_slope_curve(v):
    v2,t,hp=gelu_parts(v)
    du=GS+(3*GS*GC)*v2
    s=1.0-t*t
    dt=s*du
    half=0.5*v
    return hp+half*dt, dt*(1.0-v*t*du)+half*s*((6*GS*GC)*v)

def lower_table(turned=False):
    i=lax.broadcasted_iota(jnp.int32,(MB,MB),1 if turned else 0); j=lax.broadcasted_iota(jnp.int32,(MB,MB),0 if turned else 1)
    return jnp.where(j<=i, 1.0/(i+1).astype(f32), 0.0)

def interleave(*runs):
    runs=list(runs)
    while runs:
        for run in list(runs):
            if next(run,"end")=="end": runs.remove(run)

Z1,U1,DE=slice(0,MB),slice(MB,2*MB),slice(2*MB,3*MB)
W1,W2,X2,G1=slice(0,AUG),slice(AUG,AUG+HS),slice(AUG+HS,AUG+HS+MB),slice(AUG+HS+MB,AUG+HS+2*MB)
ZC,N3,G2=slice(0,MB),slice(MB,2*MB),slice(2*MB,3*MB)

def load_rows(NH, proj, kq, kqt, tt, shift, width):
    rows=proj.shape[0]
    lane=lax.broadcasted_iota(jnp.int32,(1,1,128),2)
    one=jnp.where(lane==HS,1.0,0.0)
    for h in range(NH):
        q=proj[:,:,h*128:(h+1)*128]+one
        k=proj[:,:,(NH+h)*128:(NH+h+1)*128]+one
        kq[:,h,0:MB,:]=k.astype(bf16)
        kq[:,h,MB:2*MB,:]=q.astype(bf16)
        kk=proj[:,:,(NH+h)*128:(NH+h)*128+HS]
        vv=proj[:,:,(2*NH+h)*128:(2*NH+h)*128+HS]
        tt[:,h]=shift[h][None]-vv+kk
    @pl.loop(0,rows,step=4)
    def _(r0):
        for r in range(4):
            for h in range(NH):
                both=kq[r0+r,h,0:width,:].astype(f32)
                kqt[r0+r,h]=both.T[0:AUG].astype(bf16)

def forward_kernel(NH, micro, steps, flags, proj, rate, w1, w2, c2, gain, shift,
                   mixed, wide_out, state_out, thin_out,
                   wide, held, thin, sems, kq, kqt, tt, w1s, w2s, c2s, zus, c2h, heads):
    chains=[(c,m,h) for c,(m,h) in enumerate((m,h) for m in range(micro) for h in range(NH))]
    tab=lower_table()
    load_rows(NH,proj,kq,kqt,tt,shift,MB)
    def restart(b):
        for m in range(micro):
            @pl.when(flags[m,b]>0)
            def _():
                for h in range(NH):
                    c=m*NH+h
                    w1s[c]=w1[h]; w2s[c]=w2[h]; c2s[c]=c2[h]
                    zus[c]=dot(kq[m*steps+b,h,:,0:AUG],w1[h].astype(bf16),NN)
    def chain(b):
        w1b={};w2b={};x2b={};sl={};zc={};g2e={};g2b={};g1b={};g1c={};base={};coef={};de={}
        nb=jnp.minimum(b+1,steps-1)
        for c,m,h in chains:
            z=zus[c,0:MB]
            wide[b,c,Z1]=z
            wide[b,c,U1]=zus[c,MB:2*MB]
            x2,sl[c]=gelu_and_slope(z)
            x2b[c]=x2.astype(bf16)
            held[b,c,X2]=x2b[c]
        for c,m,h in chains:
            w2b[c]=w2s[c].astype(bf16)
            held[b,c,W2]=w2b[c]
            c2h[b,c]=c2s[c]
        yield
        for c,m,h in chains:
            zc[c]=dot(x2b[c],w2b[c],NT)+c2s[c]
        for c,m,h in chains:
            w1b[c]=w1s[c].astype(bf16)
            held[b,c,W1]=w1b[c]
        yield
        for c,m,h in chains:
            coef[c]=dot(kq[m*steps+nb,h],kq[m*steps+b,h,0:MB],NT).astype(bf16)
            base[c]=dot(kq[m*steps+nb,h,:,0:AUG],w1b[c],NN)
        for c,m,h in chains:
            r=m*steps+b
            g=gain[h]; t=g*tt[r,h]; z=zc[c]
            gz=g*g*z
            var=rsum(z*z)*INV
            m1=rsum(gz)*INV; m2=rsum(gz*z)*INV; m3=rsum(t*z)*INV; mt=rsum(t)*INV
            r2=lax.rsqrt(var+EPS)
            mean_e=r2*m1+mt
            a=r2*(r2*m2+m3)
            er=rate[r,:,h:h+1]*r2
            g2e[c]=er*(r2*gz+t-mean_e-(r2*a)*z)
            g2b[c]=g2e[c].astype(bf16)
            thin[b,c,G2,0:HS]=g2e[c]
            thin[b,c,ZC,0:HS]=z
            thin[b,c,ZC,HS:HS+1]=r2
            thin[b,c,ZC,HS+1:HS+2]=mean_e
            thin[b,c,ZC,HS+2:HS+3]=a
        yield
        for c,m,h in chains:
            de[c]=dot(g2b[c],w2b[c],NN)
        yield
        for c,m,h in chains:
            wide[b,c,DE]=de[c]
            g1=de[c]*sl[c]
            g1b[c]=g1.astype(bf16)
            g1c[c]=(g1*(1.0/MB)).astype(bf16)
            held[b,c,G1]=g1b[c]
        for c,m,h in chains:
            zus[c]=base[c]-dot(coef[c],g1c[c],NN)
        yield
        for c,m,h in chains:
            w1s[c]=w1s[c]-dot(kqt[m*steps+b,h],g1c[c],NN)
        for c,m,h in chains:
            w2s[c]=w2s[c]-dot((g2e[c]*(1.0/MB)).astype(bf16),x2b[c],TN)
            c2s[c]=c2s[c]-csum(g2e[c])*(1.0/MB)
        yield
    def query(b):
        m1={};u1={};x3={};s2={};ua={}
        for c,m,h in chains:
            r=m*steps+b
            m1[c]=(tab*dot(kq[r,h,MB:2*MB],kq[r,h,0:MB],NT)).astype(bf16)
        yield
        for c,m,h in chains:
            u1[c]=wide[b,c,U1]-dot(m1[c],held[b,c,G1],NN)
            wide[b,c,U1]=u1[c]
        yield
        for c,m,h in chains:
            x3[c]=gelu(u1[c]).astype(bf16)
        yield
        for c,m,h in chains:
            s2[c]=dot(x3[c],held[b,c,X2],NT)
            ua[c]=dot(x3[c],held[b,c,W2],NT)
        yield
        for c,m,h in chains:
            ua[c]=ua[c]+c2h[b,c]-dot((tab*(s2[c]+1.0)).astype(bf16),thin[b,c,G2,0:HS].astype(bf16),NN)
        yield
        for c,m,h in chains:
            u=ua[c]
            u=u-rsum(u)*INV
            r3=lax.rsqrt(rsum(u*u)*INV+EPS)
            n=u*r3
            thin[b,c,N3,0:HS]=n
            thin[b,c,N3,HS:HS+1]=r3
            r=m*steps+b
            heads[r,h]=proj[r,:,h*128:h*128+HS]+n*gain[h]+shift[h]
        yield
    for c,m,h in chains:
        w1s[c]=w1[h]; w2s[c]=w2[h]; c2s[c]=c2[h]
        zus[c]=dot(kq[m*steps,h,:,0:AUG],w1[h].astype(bf16),NN)
    def copies(b):
        return [pltpu.make_async_copy(x.at[b],y.at[b],sems.at[i,b])
                for i,(x,y) in enumerate(((wide,wide_out),(held,state_out),(thin,thin_out)))]
    interleave(chain(0))
    restart(1)
    @pl.loop(1,steps)
    def _(b):
        interleave(chain(b),query(b-1))
        for copy in copies(b-1): copy.start()
        @pl.when(b+1<steps)
        def _():
            restart(b+1)
    interleave(query(steps-1))
    for copy in copies(steps-1): copy.start()
    for m in range(micro):
        s=slice(m*steps,(m+1)*steps)
        mixed[s]=jnp.concatenate([heads[s,h] for h in range(NH)],-1).astype(bf16)
    @pl.loop(0,steps)
    def _(b):
        for copy in copies(b): copy.wait()

def history_shapes(steps,C):
    return [((steps,C,3*MB,FI),f32),((steps,C,AUG+HS+2*MB,FI),bf16),((steps,C,3*MB,128),f32)]

def scan_forward(flags,proj,rate,w1,w2,c2,gain,shift):
    rows,_,lanes=proj.shape
    micro=flags.shape[0]
    NH=lanes//384; steps=rows//micro; C=micro*NH
    vm=pl.BlockSpec(memory_space=pltpu.VMEM); sm=pl.BlockSpec(memory_space=pltpu.SMEM); hbm=pl.BlockSpec(memory_space=pltpu.HBM)
    S=jax.ShapeDtypeStruct; V=pltpu.VMEM
    past=history_shapes(steps,C)
    out=pl.pallas_call(partial(forward_kernel,NH,micro,steps),
        in_specs=[sm]+[vm]*7, out_specs=[vm,hbm,hbm,hbm],
        out_shape=[S((rows,MB,NH*HS),bf16)]+[S(*x) for x in past],
        scratch_shapes=[V(*x) for x in past]+[pltpu.SemaphoreType.DMA((3,steps)),
                        V((rows,NH,2*MB,128),bf16),V((rows,NH,AUG,MB),bf16),V((rows,NH,MB,HS),f32),
                        V((C,AUG,FI),f32),V((C,HS,FI),f32),V((C,1,HS),f32),
                        V((C,2*MB,FI),f32),V((steps,C,1,HS),f32),V((rows,NH,MB,HS),f32)],
        compiler_params=pltpu.CompilerParams(vmem_limit_bytes=FORWARD_VMEM),
        cost_estimate=pl.CostEstimate(flops=18_000_000_000,bytes_accessed=12_000_000,transcendentals=0),
        name="inner_forward")(flags,proj,rate,w1,w2,c2,gain,shift)
    return out[0],tuple(out[1:])

def backward_kernel(NH, micro, steps, flags, dmix, proj, rate, gain, shift, wide_in, state_in, thin_in,
                    dproj, drate, dw1, dw2, dc2, dgain, dshift,
                    wide, held, thin, sems, kq, kqt, tt, p1, p2, pc, eb, p1h, p2h, ff1, qg1, qx2, qg2, qk, qsl, qcv, qd2, qu2, qu1, qx3):
    chains=[(c,m,h) for c,(m,h) in enumerate((m,h) for m in range(micro) for h in range(NH))]
    C=micro*NH
    tab=lower_table(); tabt=lower_table(True)
    def copies(b):
        return [pltpu.make_async_copy(x.at[b],y.at[b],sems.at[i,b])
                for i,(x,y) in enumerate(((wide_in,wide),(state_in,held),(thin_in,thin)))]
    @pl.loop(0,steps)
    def _(b):
        for copy in copies(steps-1-b): copy.start()
    load_rows(NH,proj,kq,kqt,tt,shift,2*MB)
    p1[...]=jnp.zeros(p1.shape,f32); p2[...]=jnp.zeros(p2.shape,f32); pc[...]=jnp.zeros(pc.shape,f32)
    p1h[...]=jnp.zeros(p1h.shape,bf16); p2h[...]=jnp.zeros(p2h.shape,bf16); ff1[...]=jnp.zeros(ff1.shape,f32)
    dw1[...]=jnp.zeros(dw1.shape,f32); dw2[...]=jnp.zeros(dw2.shape,f32); dc2[...]=jnp.zeros(dc2.shape,f32)
    drate[...]=jnp.zeros(drate.shape,f32)
    def query(b):
        o=lax.rem(b,2)
        du2b={};s2t={};d2={};dx3={};m2t={};ds2={};sl3={};du1b={};ds1={};m1t={};dqa={};x3={}
        for c,m,h in chains:
            r=m*steps+b
            n3=thin[b,c,N3,0:HS]; r3=thin[b,c,N3,HS:HS+1]
            hh=dmix[r,:,h*HS:(h+1)*HS]*gain[h]
            du2=r3*(hh-rsum(hh)*INV-n3*(rsum(hh*n3)*INV))
            qd2[o,c]=du2
            du2b[c]=du2.astype(bf16)
            qu2[o,c]=du2b[c]
        for c,m,h in chains:
            x,sl3[c]=gelu_and_slope(wide[b,c,U1])
            x3[c]=x.astype(bf16)
            qx3[o,c]=x3[c]
        yield
        for c,m,h in chains:
            s2t[c]=dot(held[b,c,X2],x3[c],NT)
            d2[c]=dot(du2b[c],thin[b,c,G2,0:HS].astype(bf16),NT)
            dx3[c]=dot(du2b[c],held[b,c,W2],NN)
        yield
        for c,m,h in chains:
            m2t[c]=(tabt*(s2t[c]+1.0)).astype(bf16)
            ds2[c]=(tab*d2[c]).astype(bf16)
        for c,m,h in chains:
            dx3[c]=dx3[c]-dot(ds2[c],held[b,c,X2],NN)
            qg2[o,c]=-dot(m2t[c],du2b[c],NN)
            qx2[o,c]=-dot(ds2[c],x3[c],TN)
        yield
        for c,m,h in chains:
            du1b[c]=(dx3[c]*sl3[c]).astype(bf16)
            qu1[o,c]=du1b[c]
        for c,m,h in chains:
            r=m*steps+b
            ds1[c]=dot(du1b[c],held[b,c,G1],NT)
            m1t[c]=dot(kq[r,h,0:MB],kq[r,h,MB:2*MB],NT)
            dqa[c]=dot(du1b[c],held[b,c,W1],NT)[:,0:HS]
        yield
        for c,m,h in chains:
            ds1[c]=(tab*ds1[c]).astype(bf16)
            m1t[c]=(tabt*m1t[c]).astype(bf16)
        for c,m,h in chains:
            r=m*steps+b
            qg1[o,c]=-dot(m1t[c],du1b[c],NN)
            dr=dmix[r,:,h*HS:(h+1)*HS]
            dproj[r,:,h*128:h*128+HS]=(dr+dqa[c]-dot(ds1[c],kq[r,h,0:MB,:],NN)[:,0:HS]).astype(bf16)
            qk[o,c]=-dot(ds1[c],kq[r,h,MB:2*MB,:],TN)[:,0:HS]
        yield
        for c,m,h in chains:
            sl,cv=gelu_slope_curve(wide[b,c,Z1])
            qsl[o,c]=sl
            qcv[o,c]=wide[b,c,DE]*cv
        yield
    def chain(b):
        o=lax.rem(b,2); pb=jnp.maximum(b-1,0)
        dde={};dz1a={};n2p={};gh={};dz2b={};dx={};dz1b={};base={};coef={};dk={};x2p={}
        for c,m,h in chains:
            gg1=qg1[o,c]+ff1[c]
            dde[c]=(gg1*qsl[o,c]).astype(bf16)
            dz1a[c]=gg1*qcv[o,c]
        yield
        for c,m,h in chains:
            gh[c]=dot(dde[c],held[b,c,W2],NT)
        for c,m,h in chains:
            n2p[c]=dot(held[b,c,X2],p2h[c],NT)
        yield
        for c,m,h in chains:
            r=m*steps+b
            g=gain[h]; gg=g*g
            zc=thin[b,c,ZC,0:HS]; r2=thin[b,c,ZC,HS:HS+1]; me=thin[b,c,ZC,HS+1:HS+2]; a=thin[b,c,ZC,HS+2:HS+3]
            n=zc*r2
            e=gg*n+g*tt[r,h]
            g2=r2*(e-me-n*a)
            hg=gh[c]+qg2[o,c]+(n2p[c]+pc[c])*(1.0/MB)
            rt=rate[r,:,h:h+1]
            q=rsum(hg*g2)
            drate[r,:,h:h+1]=q
            G=rt*hg
            mg=rsum(G)*INV; bb=rsum(G*n)*INV
            ds=r2*(G-mg-n*bb)
            eb[b,c]=ds
            dn=gg*ds-r2*(G*a+e*bb)
            dz2=r2*(dn-rsum(dn)*INV-n*(rsum(dn*n)*INV+rt*q*INV))
            dz2b[c]=dz2.astype(bf16)
            pc[c]=pc[c]-csum(qd2[o,c]+dz2)
        for c,m,h in chains:
            base[c]=dot(kq[m*steps+pb,h,0:MB,0:AUG],p1h[c],NN)
            coef[c]=dot(kq[m*steps+pb,h,0:MB],kq[m*steps+b,h],NT).astype(bf16)
        for c,m,h in chains:
            x2p[c]=dot(thin[b,c,G2,0:HS].astype(bf16),p2h[c],NN)
            dk[c]=dot(held[b,c,G1],p1h[c],NT)[:,0:HS]
        yield
        for c,m,h in chains:
            dx[c]=dot(dz2b[c],held[b,c,W2],NN)
        yield
        for c,m,h in chains:
            full=dx[c]+qx2[o,c]+x2p[c]*(1.0/MB)
            dz1b[c]=(dz1a[c]+full*qsl[o,c]).astype(bf16)
        both={}
        for c,m,h in chains:
            both[c]=jnp.concatenate([dz1b[c],qu1[o,c]],0)
            ff1[c]=(base[c]-dot(coef[c],both[c],NN))*(1.0/MB)
        yield
        for c,m,h in chains:
            r=m*steps+b
            p1[c]=p1[c]-dot(kqt[r,h],both[c],NN)
            p2[c]=p2[c]-dot(jnp.concatenate([qu2[o,c],thin[b,c,G2,0:HS].astype(bf16),dz2b[c]],0),jnp.concatenate([qx3[o,c],dde[c],held[b,c,X2]],0),TN)
        for c,m,h in chains:
            r=m*steps+b
            dy=eb[b,c]*gain[h]
            dkk=dy+qk[o,c]+dk[c]*(1.0/MB)+dot(dz1b[c],held[b,c,W1],NT)[:,0:HS]
            dproj[r,:,(NH+h)*128:(NH+h)*128+HS]=dkk.astype(bf16)
            dproj[r,:,(2*NH+h)*128:(2*NH+h)*128+HS]=(-dy).astype(bf16)
        for c,m,h in chains:
            p1h[c]=p1[c].astype(bf16); p2h[c]=p2[c].astype(bf16)
        yield
    def restart(b):
        for m in range(micro):
            @pl.when(flags[m,b]>0)
            def _():
                for h in range(NH):
                    c=m*NH+h
                    dw1[h]=dw1[h]-p1[c]; dw2[h]=dw2[h]-p2[c]; dc2[h]=dc2[h]-pc[c]
                    p1[c]=jnp.zeros((AUG,FI),f32); p2[c]=jnp.zeros((HS,FI),f32); pc[c]=jnp.zeros((1,HS),f32)
                    p1h[c]=jnp.zeros((AUG,FI),bf16); p2h[c]=jnp.zeros((HS,FI),bf16); ff1[c]=jnp.zeros((MB,FI),f32)
    for copy in copies(steps-1): copy.wait()
    interleave(query(steps-1))
    @pl.loop(0,steps-1)
    def _(back):
        b=steps-1-back
        for copy in copies(b-1): copy.wait()
        interleave(chain(b),query(b-1))
        restart(b)
    interleave(chain(0))
    restart(0)
    for h in range(NH):
        dg=jnp.zeros((1,HS),f32); ds=jnp.zeros((1,HS),f32)
        for m in range(micro):
            c=m*NH+h; s=slice(m*steps,(m+1)*steps)
            dr=dmix[s,:,h*HS:(h+1)*HS]
            zc=thin[:,c,ZC,0:HS]; r2=thin[:,c,ZC,HS:HS+1]
            g=gain[h][None]
            dm=eb[:,c]
            part=dr*thin[:,c,N3,0:HS]+dm*(2.0*g*(zc*r2)+tt[s,h])
            dg=dg+jnp.sum(jnp.sum(part,0),0,keepdims=True)
            ds=ds+jnp.sum(jnp.sum(dr+dm*g,0),0,keepdims=True)
        dgain[h]=dg; dshift[h]=ds
    for p in range(3*NH):
        dproj[:,:,p*128+HS:(p+1)*128]=jnp.zeros((micro*steps,MB,128-HS),bf16)
    rt=rate[...]
    drate[...]=drate[...]*rt*(1.0-HS*rt)

def scan_backward(flags,dmix,proj,rate,gain,shift,hist):
    rows,_,lanes=proj.shape
    micro=flags.shape[0]
    NH=lanes//384; steps=rows//micro; C=micro*NH
    vm=pl.BlockSpec(memory_space=pltpu.VMEM); sm=pl.BlockSpec(memory_space=pltpu.SMEM); hbm=pl.BlockSpec(memory_space=pltpu.HBM)
    S=jax.ShapeDtypeStruct; V=pltpu.VMEM
    out=pl.pallas_call(partial(backward_kernel,NH,micro,steps),
        in_specs=[sm]+[vm]*5+[hbm]*3, out_specs=[vm]*7,
        out_shape=[S((rows,MB,lanes),bf16),S((rows,MB,8),f32),S((NH,AUG,FI),f32),S((NH,HS,FI),f32),S((NH,1,HS),f32),S((NH,1,HS),f32),S((NH,1,HS),f32)],
        scratch_shapes=[V(*x) for x in history_shapes(steps,C)]+[pltpu.SemaphoreType.DMA((3,steps)),V((rows,NH,2*MB,128),bf16),V((rows,NH,AUG,2*MB),bf16),V((rows,NH,MB,HS),f32),
                        V((C,AUG,FI),f32),V((C,HS,FI),f32),V((C,1,HS),f32),V((steps,C,MB,HS),f32),
                        V((C,AUG,FI),bf16),V((C,HS,FI),bf16),V((C,MB,FI),f32),
                        V((2,C,MB,FI),f32),V((2,C,MB,FI),f32),V((2,C,MB,HS),f32),V((2,C,MB,HS),f32),V((2,C,MB,FI),f32),V((2,C,MB,FI),f32),
                        V((2,C,MB,HS),f32),V((2,C,MB,HS),bf16),V((2,C,MB,FI),bf16),V((2,C,MB,FI),bf16)],
        compiler_params=pltpu.CompilerParams(vmem_limit_bytes=BACKWARD_VMEM),
        cost_estimate=pl.CostEstimate(flops=1000,bytes_accessed=1000,transcendentals=0),
        name="inner_backward")(flags,dmix,proj,rate,gain,shift,*hist)
    return out[0],out[1],tuple(out[2:])

def gelu_full(v):
    v2,t,hp=gelu_parts(v)
    q=(1.0-t*t)*(0.5*GS+(1.5*GS*GC)*v2)
    return v*hp, hp+v*q

def struct(shape, dtype):
    return jax.ShapeDtypeStruct(shape, dtype)

def call(kernel, name, flops, arrays, shapes, scratch=(), limit=None):
    vm=pl.BlockSpec(memory_space=pltpu.VMEM); sm=pl.BlockSpec(memory_space=pltpu.SMEM)
    specs=[sm if a.ndim==1 else vm for a in arrays]
    moved=1000 if flops<2000 else sum(a.size*a.dtype.itemsize for a in arrays)+sum(s.size*s.dtype.itemsize for s in shapes)
    return pl.pallas_call(kernel, in_specs=specs, out_specs=[vm]*len(shapes), out_shape=list(shapes), scratch_shapes=list(scratch),
        compiler_params=pltpu.CompilerParams(vmem_limit_bytes=limit or SMALL_VMEM),
        cost_estimate=pl.CostEstimate(flops=flops,bytes_accessed=moved,transcendentals=0), name=name)(*arrays)

def bits(n):
    return n.bit_length()-1

def near_slot(peer, m, rank, pair, micro):
    return peer*(micro*pair)+m*pair+rank

def far_slot(peer, m, rank, pair, micro, size, part):
    q=pair//size
    return lax.shift_right_logical(rank,bits(q))*part+peer*(micro*q)+m*q+(rank&(q-1))

def send_kernel(pair, size, given, owner, x, up, sent_x, sent_up, recv_col, recv_row, turn_row, fin_col, end_col):
    micro,tok=given.shape
    rows=micro*tok
    part=rows//size
    at=lax.broadcasted_iota(jnp.int32,(rows,tok),0)
    low=lax.broadcasted_iota(jnp.int32,(tok,tok),0); high=lax.broadcasted_iota(jnp.int32,(tok,tok),1)
    ax=None
    for m in range(micro):
        span=slice(m*tok,(m+1)*tok)
        along=jnp.broadcast_to(given[m:m+1,:].astype(f32),(tok,tok))
        down=along.T
        row=jnp.sum(jnp.where(down<along,1.0,0.0),0,keepdims=True).astype(jnp.int32)
        col=jnp.sum(jnp.where(along<down,1.0,0.0),1,keepdims=True).astype(jnp.int32)
        split=lambda r:(lax.shift_right_logical(r,bits(pair)),r&(pair-1))
        peer,rank=split(row)
        hot=jnp.where(at==near_slot(peer,m,rank,pair,micro),1.0,0.0).astype(bf16)
        a=dot(hot,x[m],NN); b=dot(hot,up[m],NN)
        if m==0: ax,au=a,b
        else: ax,au=ax+a,au+b
        peer,rank=split(col)
        fin_col[span,:]=near_slot(peer,m,rank,pair,micro)
        end_col[span,:]=far_slot(peer,m,rank,pair,micro,size,part)
        anchor=lax.shift_right_logical(owner[m:m+1,:],bits(tok))
        along=jnp.broadcast_to(anchor.astype(f32),(tok,tok))
        down=along.T
        same=jnp.where(along==down,1.0,0.0)
        col=jnp.sum(jnp.where(high<low,same,0.0),1,keepdims=True).astype(jnp.int32)
        row=jnp.sum(jnp.where(low<high,same,0.0),0,keepdims=True).astype(jnp.int32)
        recv_col[span,:]=near_slot(down[:,0:1].astype(jnp.int32),m,col,pair,micro)
        recv_row[:,span]=near_slot(anchor,m,row,pair,micro)
        turn_row[:,span]=far_slot(anchor,m,row,pair,micro,size,part)
    sent_x[...]=ax.astype(bf16)
    sent_up[...]=au.astype(bf16)

def send_rows(pair, size, given, owner, x, up):
    micro,tok,width=x.shape
    rows=micro*tok
    i=jnp.int32
    return call(partial(send_kernel,pair,size),"send_rows",2_000_000_000,[given,owner,x,up],
        [struct((rows,width),bf16),struct((rows,width),bf16),struct((rows,1),i),struct((1,rows),i),struct((1,rows),i),struct((rows,1),i),struct((rows,1),i)])

def hot_from_col(col, columns):
    n=col.shape[0]
    return jnp.where(lax.broadcasted_iota(jnp.int32,(n,columns),1)==col,1.0,0.0).astype(bf16)

def hot_from_row(row, count, first=0):
    n=row.shape[1]
    return jnp.where(lax.broadcasted_iota(jnp.int32,(count,n),0)+first==row,1.0,0.0).astype(bf16)

def project_kernel(arrived, col, ngain, qkv, ratew, rateb, resid, normed, proj, rate):
    rows=arrived.shape[0]
    r=dot(hot_from_col(col[...],rows),arrived[...],NN)
    resid[...]=r.astype(bf16)
    n=(r*lax.rsqrt(rsum(r*r)*(1.0/r.shape[1])+EPS)*ngain[...]).astype(bf16)
    normed[...]=n
    rate[...]=(1.0/HS)/(1.0+jnp.exp(-(dot(n,ratew[...],NN)+rateb[...])))
    proj[...]=dot(n,qkv[...],NT)

def project(arrived, col, ngain, qkv, ratew, rateb):
    rows,width=arrived.shape
    return call(project_kernel,"project",1_500_000_000,[arrived,col,ngain,qkv,ratew,rateb],
        [struct((rows,width),bf16),struct((rows,width),bf16),struct((rows,qkv.shape[0]),f32),struct((rows,ratew.shape[1]),f32)])

def middle_kernel(T, cut, me, col, row, turn, arrived, mixed, normed, resid, post, gateout, fgain, swiglu, down,
                  up, out_sent, act, sgrad, nmid, gated, mgrad, hgrad, ggrad, dpg, dpb, dfg, base, gpart, rpart,
                  gpre, hid, feed, mid, stats, pbuf):
    c=pl.program_id(0)
    rows,wide=resid.shape
    hw=mixed.shape[2]
    width=T*hw
    half=sgrad.shape[1]//2
    def flat(ref,i,lead=()):
        w=ref[i]
        return w.reshape(w.shape[0]*w.shape[1],w.shape[2])
    def vectors(i):
        v=post[i,0].astype(f32)
        return v[0:1,0:hw]+v[1:2,0:hw]+v[2:3,0:hw], v[3:4,0:hw]+v[4:5,0:hw]+v[5:6,0:hw]
    @pl.when(c==0)
    def _():
        up[...]=dot(hot_from_col(col[...],rows),arrived[...],NN).astype(bf16)
        center=sum(rsum(mixed[i].astype(f32)) for i in range(T))*(1.0/width)
        square=0.0
        for i in range(T):
            x=mixed[i].astype(f32)-center
            square=square+rsum(x*x)
        inv=lax.rsqrt(square*(1.0/width)+EPS)
        stats[:,0:1]=center
        stats[:,1:2]=inv
        mixer=None
        for i in range(T):
            w=flat(gateout,i)
            pg,pb=vectors(i)
            pre=dot(normed[...],w[0:hw],NT)
            gpre[i]=pre
            g=(((mixed[i].astype(f32)-center)*inv*pg+pb)*gelu(pre)).astype(bf16)
            @pl.when(me[0]==i)
            def _():
                gated[...]=g
            y=dot(g,w[hw:2*hw],NN)
            mixer=y if mixer is None else mixer+y
        h=resid[...].astype(f32)+mixer
        hid[...]=h
        nmid[...]=(h*lax.rsqrt(rsum(h*h)*(1.0/wide)+EPS)*fgain[...]).astype(bf16)
        feed[...]=jnp.zeros((rows,wide),f32)
        mid[...]=jnp.zeros((rows,wide),f32)
    block=rows
    @pl.loop(0,1)
    def _(b):
        at=pl.ds(pl.multiple_of(b*block,block),block)
        nm=nmid[at,:]
        dn=flat(down,0)
        w=swiglu[0]
        unit=w.shape[1]//2
        wg=w[:,0:unit].reshape(half,wide)
        wu=w[:,unit:2*unit].reshape(half,wide)
        gh=dot(nm,wg,NT)
        uh=dot(nm,wu,NT)
        da=dot(up[at,:],dn,NT)
        sg=1.0/(1.0+jnp.exp(-gh))
        silu=gh*sg
        a=(silu*uh).astype(bf16)
        s1=(da*uh*sg*(1.0+gh*(1.0-sg))).astype(bf16)
        s2=(da*silu).astype(bf16)
        @pl.when(me[0]==c)
        def _():
            act[at,:]=a
            sgrad[at,0:half]=s1
            sgrad[at,half:2*half]=s2
        mid[at,:]=mid[at,:]-(dot(s1,wg,NN)+dot(s2,wu,NN))
        feed[at,:]=feed[at,:]-dot(a,dn,NN)
    @pl.when(c==T-1)
    def _():
        h=hid[...]
        own=(h-feed[...]).astype(bf16)
        out_sent[...]=dot(hot_from_row(row[...],rows),own,NN).astype(bf16)
        sc=lax.rsqrt(rsum(h*h)*(1.0/wide)+EPS)
        m=-mid[...]
        dfg[...]=csum(m*h*sc)
        ms=m*fgain[...]
        hg=up[...].astype(f32)+sc*ms-h*(sc*sc*sc*(rsum(ms*h)*(1.0/wide)))
        full=hg.astype(bf16)
        mgrad[...]=full
        part=base.shape[0]
        hot=hot_from_row(turn[...],part,me[0]*part)
        base[...]=dot(hot,full,NN)+dot(hot,(hg-full.astype(f32)).astype(bf16),NN)
        rpart[...]=dot(hot,resid[...],NN)
        center=stats[:,0:1]; inv=stats[:,1:2]
        s1=0.0; s2=0.0
        for i in range(T):
            w=flat(gateout,i)
            pgn,pb=vectors(i)
            std=(mixed[i].astype(f32)-center)*inv
            a,slope=gelu_full(gpre[i])
            gg=dot(full,w[hw:2*hw],NT)
            gr=(gg*(std*pgn+pb)*slope).astype(bf16)
            y=dot(dot(hot,gr,NN).astype(bf16),w[0:hw],NN)
            if i==0: gpart[...]=y
            else: gpart[...]=gpart[...]-(-y)
            pg=gg*a
            p=pg*pgn
            pbuf[i]=p
            s1=s1+rsum(p); s2=s2+rsum(p*std)
            @pl.when(me[0]==i)
            def _():
                ggrad[...]=gr
                dpg[...]=csum(pg*std); dpb[...]=csum(pg)
        std=(mixed[me[0]].astype(f32)-center)*inv
        hgrad[...]=inv*(pbuf[me[0]]-s1*(1.0/width)-std*(s2*(1.0/width)))

def middle(me, col, row, turn, arrived, mixed, normed, resid, weights, fgain):
    T,rows,hw=mixed.shape; wide=resid.shape[1]; D,tall=weights.shape[1:3]
    a,b,g,p=weight_cuts(tall)
    half=a*D//2
    whole=lambda x:pl.BlockSpec(x.shape,lambda c,n=len(x.shape):(0,)*n,pipeline_mode=pl.Buffered(1))
    specs=[pl.BlockSpec(memory_space=pltpu.SMEM)]+[whole(x) for x in (col,row,turn,arrived,mixed,normed,resid)]
    specs+=[pl.BlockSpec((T,1,p,wide),lambda c:(0,0,(a+b+g)//p,0),pipeline_mode=pl.Buffered(1)),
            pl.BlockSpec((T,D,g,wide),lambda c:(0,0,(a+b)//g,0),pipeline_mode=pl.Buffered(1)),
            whole(fgain),
            pl.BlockSpec((1,D,a,wide),lambda c:(c,0,0,0)),
            pl.BlockSpec((1,D,b,wide),lambda c:(c,0,a//b,0))]
    shapes=[struct((rows,wide),bf16),struct((rows,wide),bf16),struct((rows,half),bf16),struct((rows,2*half),bf16),struct((rows,wide),bf16),
            struct((rows,hw),bf16),struct((rows,wide),bf16),struct((rows,hw),f32),struct((rows,hw),bf16),
            struct((1,hw),f32),struct((1,hw),f32),struct((1,wide),f32)]+[struct((rows//T,wide),f32)]*3
    V=pltpu.VMEM
    return pl.pallas_call(partial(middle_kernel,T,None),
        grid=(T,), in_specs=specs, out_specs=[pl.BlockSpec(s.shape,lambda c,n=len(s.shape):(0,)*n,pipeline_mode=pl.Buffered(1)) for s in shapes], out_shape=shapes,
        scratch_shapes=[V((T,rows,hw),f32),V((rows,wide),f32),V((rows,wide),f32),V((rows,wide),f32),V((rows,128),f32),V((T,rows,hw),f32)],
        compiler_params=pltpu.CompilerParams(vmem_limit_bytes=MIDDLE_VMEM,dimension_semantics=("arbitrary",)),
        cost_estimate=pl.CostEstimate(flops=14_000_000_000,bytes_accessed=25_000_000,transcendentals=0),name="middle")(
        me,col,row,turn,arrived,mixed,normed,resid,weights,weights,fgain,weights,weights)

def thirds(x):
    high=x.astype(bf16).astype(f32)
    rest=x-high
    center=rest.astype(bf16).astype(f32)
    return [high,center,rest-center]

def pack_kernel(count, d, wg, wu, down, turned, out, pgain, pbias, piece):
    unit=wg.shape[1]; width=down.shape[1]; hw=turned.shape[0]
    piece[0:unit,:]=wg[...].astype(f32).T.astype(bf16)
    piece[unit:2*unit,:]=wu[...].astype(f32).T.astype(bf16)
    at=2*unit
    n=down.shape[0]//count
    piece[at:at+n,:]=down[pl.ds(pl.multiple_of(d[0]*n,n),n),:]
    at+=n
    n=2*hw//count
    @pl.when(d[0]<count//2)
    def _():
        piece[at:at+n,:]=turned[pl.ds(pl.multiple_of(d[0]*n,n),n),:]
    @pl.when(d[0]>=count//2)
    def _():
        piece[at:at+n,:]=out[pl.ds(pl.multiple_of((d[0]-count//2)*n,n),n),:]
    at+=n
    rows=jnp.concatenate(thirds(pgain[...])+thirds(pbias[...])+[jnp.zeros((10,hw),f32)],0)
    piece[at:at+16,:]=jnp.concatenate([rows,jnp.zeros((16,width-hw),f32)],1).astype(bf16)

def pack_weights(count, d, wg, wu, down, turned, out, pgain, pbias):
    unit=wg.shape[1]; width=down.shape[1]
    tall=2*unit+(down.shape[0]+2*turned.shape[0])//count+16
    return call(partial(pack_kernel,count),"pack_weights",100_000_000,[d,wg,wu,down,turned,out,pgain,pbias],[struct((tall,width),bf16)])[0]

def weight_cuts(tall):
    unit=tall//16
    return 8*unit,4*unit,3*unit,unit

def in_part_kernel(T, me, row, dproj, logit, qkv, ratew, *sums):
    lg=logit[...]
    y=dot(dproj[...],qkv[...],NN)+dot(lg.astype(bf16),ratew[...],NT)
    y=y.astype(bf16)
    part=y.shape[0]//T
    for k in range(T):
        sums[k][...]=dot(hot_from_row(row[...],part,lax.rem(me[0]+k,T)*part),y,NN).astype(bf16)

def in_part(T, me, row, dproj, logit, qkv, ratew):
    rows=dproj.shape[0]; width=qkv.shape[1]
    return call(partial(in_part_kernel,T),"in_part",1000,[me,row,dproj,logit,qkv,ratew],[struct((rows//T,width),bf16)]*T)

def early_kernel(count, act, up, nmid, sgrad, gated, mgrad, normed, ggrad, *outs):
    width=nmid.shape[1]
    og=jnp.concatenate([dot(gated[...],mgrad[...],TN),dot(ggrad[...],normed[...],TN)],0).astype(bf16)
    dn=dot(act[...],up[...],TN).astype(bf16)
    left=dot(nmid[...],sgrad[:,0:width],TN).astype(bf16)
    right=dot(nmid[...],sgrad[:,width:],TN).astype(bf16)
    third=width//3
    right=jnp.concatenate([right[i*third:(i+1)*third] for i in range(3)],1)
    pieces=(left,right,dn,og)
    if len(outs)==1:
        at=0
        for y in pieces:
            n=y.shape[0]//count
            for d in range(count):
                outs[0][d,at:at+n]=y[d*n:(d+1)*n]
            at+=n
    else:
        for o,y in zip(outs,pieces): o[...]=y

def aligned(count, sizes):
    return all(n%(16*count)==0 for n in sizes)

def early_grads(count, act, up, nmid, sgrad, gated, mgrad, normed, ggrad):
    width=nmid.shape[1]; half=act.shape[1]; hw=gated.shape[1]
    sizes=(width,width//3,half,2*hw)
    whole=aligned(count,sizes)
    shapes=[struct((count,sum(sizes)//count,width),bf16)] if whole else [struct((n,width),bf16) for n in sizes]
    out=call(partial(early_kernel,count),"early_grads",1000,[act,up,nmid,sgrad,gated,mgrad,normed,ggrad],shapes)
    return out[0] if whole else jnp.concatenate([y.reshape(count,-1,width) for y in out],1)

def early_out_kernel(edges, early, swiglu, down, pair, full, sems):
    def piece(k):
        x=early[:,edges[k]:edges[k+1],:]
        return x.reshape(x.shape[0]*x.shape[1],x.shape[2]).astype(f32)
    width=early.shape[2]
    half=full.shape[2]
    left=piece(0)
    full[0]=left[:,0:half]
    full[1,:,0:width-half]=left[:,half:width]
    right=piece(1)
    third=width//3
    for k in range(3):
        full[1,k*third:(k+1)*third,width-half:]=right[:,k*third:(k+1)*third]
    copies=[pltpu.make_async_copy(full.at[k],swiglu.at[:,k,:],sems.at[k]) for k in range(2)]
    for copy in copies: copy.start()
    down[...]=piece(2)
    pair[...]=piece(3)
    for copy in copies: copy.wait()

def early_out(edges, early):
    count,_,width=early.shape
    rows=[count*(edges[k+1]-edges[k]) for k in range(4)]
    half=(width+width//3)//2
    vm=pl.BlockSpec(memory_space=pltpu.VMEM)
    return pl.pallas_call(partial(early_out_kernel,edges),in_specs=[vm],
        out_specs=[pl.BlockSpec(memory_space=pltpu.HBM),vm,vm],
        out_shape=[struct((width,2,half),f32),struct((rows[2],width),f32),struct((rows[3],width),f32)],
        scratch_shapes=[pltpu.VMEM((2,width,half),f32),pltpu.SemaphoreType.DMA((2,))],
        compiler_params=pltpu.CompilerParams(vmem_limit_bytes=FORWARD_VMEM),
        cost_estimate=pl.CostEstimate(flops=6_000_000_000,bytes_accessed=1000,transcendentals=0),name="early_out")(early)

def late_out_kernel(heads, hw, cut, late, big, first, second, first_b, second_b, dgain, dshift, dpg, dpb, dfg, rate_w, rate_b):
    count,tall,width=late.shape
    x=late[...].astype(f32)
    big[...]=x[:,0:cut].reshape(count*cut,width)
    rest=x[:,cut:].reshape(count*(tall-cut),width)
    for h in range(heads):
        first[h]=rest[0:HS,h*FI:(h+1)*FI]
        second[h]=rest[HS:2*HS,h*FI:(h+1)*FI]
        at=2*HS
        first_b[h:h+1,:]=rest[at+8:at+9,h*FI:(h+1)*FI]
        for ref,k in ((second_b,10),(dgain,11),(dshift,12)):
            ref[h:h+1,:]=rest[at+k:at+k+1,h*HS:(h+1)*HS]
    dfg[...]=rest[at+9:at+10,:]
    dpg[...]=rest[at+13:at+14,0:hw]
    dpb[...]=rest[at+14:at+15,0:hw]
    rate_w[...]=rest[at:at+heads,:]
    rate_b[...]=rest[at+15:at+16,0:heads]

def late_out(heads, hw, cut, late):
    width=late.shape[2]; count=late.shape[0]
    s=lambda *d:struct(d,f32)
    return call(partial(late_out_kernel,heads,hw,cut),"late_out",1000,[late],
        [s(count*cut,width),s(heads,HS,FI),s(heads,HS,FI),s(heads,FI),s(heads,HS),s(heads,HS),s(heads,HS),s(1,hw),s(1,hw),s(1,width),s(heads,width),s(1,heads)],
        limit=FORWARD_VMEM)

def late_kernel(heads, count, dproj, normed, logit, dw1, dw2, dc2, dgain, dshift, dpg, dpb, dfg, *refs):
    outs=refs[:-1]; rest=refs[-1]
    width=normed.shape[1]
    n=normed[...]
    packed=jnp.concatenate([dot(dproj[:,g*128:(g+1)*128],n,TN)[0:HS] for g in range(3*heads)],0)
    lg=logit[...]
    rest[...]=jnp.zeros(rest.shape,f32)
    for h in range(heads):
        rest[0:HS,h*FI:(h+1)*FI]=dw1[h,0:HS]
        rest[HS:2*HS,h*FI:(h+1)*FI]=dw2[h]
    rest[2*HS:2*HS+8,:]=dot(lg.astype(bf16),n,TN)
    for h in range(heads):
        rest[2*HS+8:2*HS+9,h*FI:(h+1)*FI]=dw1[h,HS:HS+1]
        rest[2*HS+10:2*HS+11,h*HS:(h+1)*HS]=dc2[h]
        rest[2*HS+11:2*HS+12,h*HS:(h+1)*HS]=dgain[h]
        rest[2*HS+12:2*HS+13,h*HS:(h+1)*HS]=dshift[h]
    hw=dpg.shape[1]
    rest[2*HS+9:2*HS+10,:]=dfg[...]
    rest[2*HS+13:2*HS+14,0:hw]=dpg[...]
    rest[2*HS+14:2*HS+15,0:hw]=dpb[...]
    rest[2*HS+15:2*HS+16,0:lg.shape[1]]=csum(lg)
    if len(outs)==1:
        per=packed.shape[0]//count; more=rest.shape[0]//count
        for d in range(count):
            outs[0][d,0:per+more]=jnp.concatenate([packed[d*per:(d+1)*per],rest[d*more:(d+1)*more,:]],0).astype(bf16)
    else:
        outs[0][...]=packed.astype(bf16); outs[1][...]=rest[...].astype(bf16)

def late_grads(count, dproj, normed, logit, dw1, dw2, dc2, dgain, dshift, dpg, dpb, dfg):
    heads=dw1.shape[0]; width=normed.shape[1]
    sizes=(3*heads*HS,3*HS)
    whole=all(n%(8*count)==0 for n in sizes) and sum(sizes)%(16*count)==0
    shapes=[struct((count,sum(sizes)//count,width),bf16)] if whole else [struct((n,width),bf16) for n in sizes]
    out=call(partial(late_kernel,heads,count),"late_grads",1000,[dproj,normed,logit,dw1,dw2,dc2,dgain,dshift,dpg,dpb,dfg],
        shapes,[pltpu.VMEM((3*HS,width),f32)])
    return out[0] if whole else jnp.concatenate([y.reshape(count,-1,width) for y in out],1)

def in_rows_kernel(T, *refs):
    got=refs[:T]
    base,gpart,rpart,ngain=refs[T:T+4]
    outs=refs[T+4:]
    part,wide=base.shape
    r=rpart[...]
    sc=lax.rsqrt(rsum(r*r)*(1.0/wide)+EPS)
    s=gpart[...]
    for k in range(T):
        s=s+got[k][...].astype(f32)
    g=csum(s*(r*sc))
    high=g.astype(bf16)
    rest=g-high.astype(f32)
    center=rest.astype(bf16)
    three=jnp.concatenate([high.astype(f32),center.astype(f32),rest-center.astype(f32),jnp.zeros((13,wide),f32)],0)
    s=s*ngain[...]
    y=(base[...]+sc*s-r*(sc*sc*sc*(rsum(s*r)*(1.0/wide)))).astype(bf16)
    three=three.astype(bf16)
    if len(outs)==1:
        count=outs[0].shape[0]; lines=part//count
        for d in range(count):
            outs[0][d,0:lines]=y[d*lines:(d+1)*lines]
            outs[0][d,lines:lines+16]=three
    else:
        outs[0][...]=y; outs[1][...]=three

def in_rows(count, got, base, gpart, rpart, ngain):
    part,wide=base.shape; T=len(got)
    out=call(partial(in_rows_kernel,T),"in_rows",1000,[*got,base,gpart,rpart,ngain],
        [struct((count,part//count+16,wide),bf16)] if aligned(count,(part,)) else [struct((part,wide),bf16),struct((16,wide),bf16)],
        limit=FORWARD_VMEM)
    if len(out)==1: return out[0]
    return jnp.concatenate([out[0].reshape(count,-1,wide),jnp.broadcast_to(out[1][None],(count,16,wide))],1)

def settle_kernel(micro, spans, col, *refs):
    got=refs[:-1]; out=refs[-1]
    tok=col.shape[0]//micro
    for m in range(micro):
        y=None
        for k,g in enumerate(got):
            hot=jnp.where(lax.broadcasted_iota(jnp.int32,(tok,spans),1)+k*spans==col[m*tok:(m+1)*tok,:],1.0,0.0).astype(bf16)
            z=dot(hot,g[0:spans,:],NN)
            y=z if y is None else y+z
        out[m]=y.astype(bf16)

def settle(micro, col, got, spans, name):
    rows=col.shape[0]; wide=got[0].shape[1]
    return call(partial(settle_kernel,micro,spans),name,1000,[col,*got],[struct((micro,rows//micro,wide),bf16)])[0]

from jax.sharding import PartitionSpec as P

MICRO=2

def restart_flags(lengths, steps):
    k = jnp.arange(lengths.shape[1], dtype=jnp.int32)
    starts = jnp.sum(jnp.where((k[None, :] < k[:, None])[None], lengths[:, None, :], 0), 2)
    at = jnp.arange(steps, dtype=jnp.int32) * MB
    hit = (starts[:, None, :] == at[None, :, None]) & (lengths[:, None, :] > 0)
    return jnp.pad(jnp.any(hit, 2).astype(jnp.int32), ((0, 0), (0, 1)))

def pad_heads(array, axis):
    shape = array.shape
    split = shape[:axis] + (shape[axis] // HS, HS) + shape[axis + 1:]
    padded = jnp.pad(array.reshape(split), [(0, 0)] * (axis + 1) + [(0, HS)] + [(0, 0)] * (len(shape) - axis - 1))
    return padded.reshape(shape[:axis] + (2 * shape[axis],) + shape[axis + 1:])

def drop_pad(array, axis):
    shape = array.shape
    split = array.reshape(shape[:axis] + (shape[axis] // 128, 128) + shape[axis + 1:])
    kept = lax.slice_in_dim(split, 0, HS, axis=axis + 1)
    return kept.reshape(shape[:axis] + (shape[axis] // 2,) + shape[axis + 1:])

def swap(array, axis="dp"):
    return lax.all_to_all(array, axis, split_axis=0, concat_axis=0, tiled=True)

def turn(array, k):
    size = lax.axis_size("tensor")
    return lax.ppermute(array, "tensor", [(i, (i + k) % size) for i in range(size)])

def split_three(array):
    high = array.astype(bf16)
    rest = array - high.astype(f32)
    middle_part = rest.astype(bf16)
    return [high, middle_part, (rest - middle_part.astype(f32)).astype(bf16)]

def gather_weights(swiglu, down, gate, out, post_gain, post_bias):
    count = lax.axis_size("dp")
    size = lax.axis_size("tensor")
    d = lax.axis_index("dp")
    width = out.shape[1]
    def rows_of(array):
        piece = array.shape[0] // count
        return lax.dynamic_slice_in_dim(array, d * piece, piece, 0)
    piece = swiglu.shape[2] // count
    if count == 8:
        cut = lax.dynamic_slice_in_dim(swiglu, d * piece, piece, 2)
        mine = pack_weights(
            count, d.astype(jnp.int32).reshape(1), cut[:, 0], cut[:, 1], down, gate.T, out, post_gain[None], post_bias[None]
        )
        return lax.all_gather(mine, ("tensor", "dp")).reshape(size, count, -1, width)
    turned = lax.dynamic_slice_in_dim(swiglu, d * piece, piece, 2).transpose(1, 2, 0)
    post = jnp.stack(split_three(post_gain) + split_three(post_bias))
    post = jnp.pad(post, ((0, 10), (0, width - post.shape[1])))
    lines = [turned.reshape(-1, width), rows_of(down), rows_of(jnp.concatenate([gate.T, out], 0))]
    lines.append(rows_of(jnp.concatenate([post] * 8, 0)))
    got = lax.all_gather(jnp.concatenate(lines, 0), ("tensor", "dp"))
    first = got[:, :2 * piece].reshape(size, 8, count // 8, 2, piece, width)
    parts = [jnp.swapaxes(first, 2, 3).reshape(size, 8, -1, width)]
    at = 2 * piece
    for x in lines[1:]:
        parts.append(got[:, at:at + x.shape[0]].reshape(size, 8, -1, width))
        at += x.shape[0]
    return jnp.concatenate(parts, 2)

def shards(
    inputs, cotangent, lengths, owner_rows, given_rows, norm_gain, qkv_weight, rate_weight, rate_bias,
    inner_first, inner_first_bias, inner_second, inner_second_bias, inner_gain, inner_shift, gate_weight,
    post_gain, post_bias, out_weight, ffn_gain, swiglu_weight, down_weight,
):
    tok = inputs.shape[1]
    width = inputs.shape[2]
    rows = MICRO * tok
    blocks = rows // MB
    steps = tok // MB
    heads = rate_weight.shape[1]
    size = lax.axis_size("tensor")
    pair = tok // lax.axis_size("dp")
    me = lax.axis_index("tensor").astype(jnp.int32).reshape(1)
    weights = gather_weights(swiglu_weight, down_weight, gate_weight, out_weight, post_gain, post_bias)
    sent_in, sent_up, recv_col, recv_row, turn_row, fin_col, end_col = send_rows(
        pair, size, given_rows, owner_rows, inputs, cotangent
    )
    arrived_in = swap(sent_in)
    arrived_up = swap(sent_up)
    flags = restart_flags(lengths, steps)
    qkv_pad = pad_heads(qkv_weight.transpose(1, 2, 0).reshape(-1, width), 0)
    rate_pad = jnp.pad(rate_weight, ((0, 0), (0, 8 - heads)))
    bias_pad = jnp.pad(rate_bias, (0, 8 - heads))[None]
    first = jnp.concatenate(
        [inner_first, inner_first_bias[:, None], jnp.zeros((heads, AUG - HS - 1, FI), f32)], 1
    )
    second = jnp.swapaxes(inner_second - jnp.mean(inner_second, -1, keepdims=True), 1, 2)
    second_bias = (inner_second_bias - jnp.mean(inner_second_bias, -1, keepdims=True))[:, None]
    gain = inner_gain[:, None]
    shift = inner_shift[:, None]
    resid, normed, projected, rates = project(arrived_in, recv_col, norm_gain[None], qkv_pad, rate_pad, bias_pad)
    projected = projected.reshape(blocks, MB, -1)
    rate_blocks = rates.reshape(blocks, MB, -1)
    own, past = scan_forward(flags, projected, rate_blocks, first, second, second_bias, gain, shift)
    mixed = lax.all_gather(own.reshape(rows, -1), "tensor")
    (
        up, out_sent, act, sgrad, nmid, gated, mixer_grad, heads_grad, gate_grad, grad_pgain, grad_pbias, gain_mid,
        base, gate_part, resid_part
    ) = middle(
        me, recv_col, recv_row, turn_row, arrived_up, mixed, normed, resid, weights, ffn_gain[None]
    )
    count = lax.axis_size("dp")
    def exchanged(chunks):
        return swap(chunks.reshape(-1, width)).reshape(chunks.shape)
    def summed(got):
        return jnp.sum(got.astype(f32), 0).astype(bf16)
    early_in = early_grads(count, act, up, nmid, sgrad, gated, mixer_grad, normed, gate_grad)
    heads_grad, early_in = lax.optimization_barrier((heads_grad, early_in))
    early_got = exchanged(early_in)
    dproj, drate, carry = scan_backward(
        flags, heads_grad.reshape(blocks, MB, -1), projected, rate_blocks, gain, shift, past
    )
    dproj, early_got = lax.optimization_barrier((dproj.reshape(rows, -1), early_got))
    dproj, early_sum = lax.optimization_barrier((dproj, summed(early_got)))
    early = lax.all_gather(early_sum, "dp")
    logit = drate.reshape(rows, -1)
    late_in = late_grads(count, dproj, normed, logit, *carry, grad_pgain, grad_pbias, gain_mid)
    dproj, late_in = lax.optimization_barrier((dproj, late_in))
    late_got = exchanged(late_in)
    sums = in_part(size, me, turn_row, dproj, logit, qkv_pad, rate_pad)
    got = [sums[0]] + [turn(sums[k], k) for k in range(1, size)]
    late_sum = summed(late_got)
    got, late_sum = lax.optimization_barrier((got, late_sum))
    cut = 3 * heads * HS // count
    back = in_rows(count, got, base, gate_part, resid_part, norm_gain[None])
    late_sum, early, _ = lax.optimization_barrier((late_sum, early, back))
    late = lax.all_gather(late_sum, "dp")
    part = rows // size
    sent, out_sent = lax.optimization_barrier((exchanged(back), out_sent))
    lines = part // count
    gains = jnp.concatenate(split_three(jnp.sum(sent[:, lines:lines + 3].astype(f32), (0, 1))[None]), 0)
    mine = jnp.concatenate([sent[:, :lines].reshape(part, width), jnp.pad(gains, ((0, 13), (0, 0)))], 0)
    third = width // 3
    edges = [0]
    for lines_of in (width, third, act.shape[1], 2 * heads * HS):
        edges.append(edges[-1] + lines_of // count)
    if aligned(count, (width, third, act.shape[1], 2 * heads * HS)):
        grad_swiglu, grad_down, pair_grads = early_out(edges, early)
    else:
        left, right, grad_down, pair_grads = [
            early[:, edges[i]:edges[i + 1]].astype(f32).reshape(-1, width) for i in range(4)
        ]
        right = jnp.concatenate([right[:, i * third:(i + 1) * third] for i in range(3)], 0)
        grad_swiglu = jnp.concatenate([left, right], 1).reshape(swiglu_weight.shape)
    final = [mine] + [turn(mine, k) for k in range(1, size)]
    final, grad_swiglu, grad_down, pair_grads = lax.optimization_barrier((final, grad_swiglu, grad_down, pair_grads))
    end_turned = ((me[0] - end_col // part) % size) * part + end_col % part
    input_grad = settle(MICRO, end_turned, final, part, "settle_in")
    norm_total = sum(jnp.sum(x[part:part + 3].astype(f32), 0) for x in final)
    out_got = lax.optimization_barrier((swap(out_sent), final))[0]
    outputs = settle(MICRO, fin_col, [out_got], rows, "settle_out")
    if count == 8:
        canonical = late
    else:
        canonical = jnp.concatenate([late[:, :cut].reshape(8, -1, width), late[:, cut:].reshape(8, -1, width)], 1)
    (
        big, grad_first, grad_second, first_bias, second_b, grad_gain, grad_shift, grad_pg, grad_pb, grad_fg, grad_rate, grad_rb
    ) = late_out(heads, heads * HS, 3 * heads * HS // canonical.shape[0], canonical)
    return (
        outputs,
        input_grad,
        norm_total,
        big.reshape(3, heads * HS, width).transpose(2, 0, 1),
        grad_rate.T,
        grad_rb[0],
        grad_first,
        first_bias,
        jnp.swapaxes(grad_second, 1, 2),
        second_b,
        grad_gain,
        grad_shift,
        pair_grads[heads * HS:].T,
        grad_pg[0],
        grad_pb[0],
        pair_grads[:heads * HS],
        grad_fg[0],
        grad_swiglu,
        grad_down,
    )

def solution(mesh):
    rows, heads, columns = P(None, "dp", None), P("tensor", None), P(None, "tensor")
    table = P(None, "dp")
    vector = P("tensor")
    cube = P("tensor", None, None)
    wide = P(None, None, "tensor")
    return jax.shard_map(
        shards,
        mesh=mesh,
        in_specs=(
            rows, rows, table, table, table, P(), wide, columns, vector, cube, heads, cube, heads, heads, heads,
            columns, vector, vector, heads, P(), wide, heads,
        ),
        out_specs=(
            rows, rows, P(), wide, columns, vector, cube, heads, cube, heads, heads, heads, columns, vector, vector,
            heads, P(), wide, heads,
        ),
        check_vma=False,
    )
```

```python
from functools import partial
import jax, jax.numpy as jnp
from jax import lax
from jax.experimental import pallas as pl
from jax.experimental.pallas import tpu as pltpu

HS=64; MB=16; FI=256; EPS=1e-6
GS=0.7978845608028654; GC=0.044715
bf16=jnp.bfloat16; f32=jnp.float32
NN=((1,),(0,)); NT=((1,),(1,)); TN=((0,),(0,))
def dot(a,b,dims): return lax.dot_general(a,b,(dims,((),())),preferred_element_type=f32)
def rsum(x): return jnp.sum(x,-1,keepdims=True)
def csum(x): return jnp.sum(x,0,keepdims=True)
AUG=80
INV=1.0/HS
FORWARD_VMEM=58<<20
BACKWARD_VMEM=58<<20
MIDDLE_VMEM=38<<20
SMALL_VMEM=20<<20

def gelu_parts(v):
    v2=v*v
    t=jnp.tanh(v*(GS+(GS*GC)*v2))
    hp=0.5+0.5*t
    return v2,t,hp
def gelu(v):
    _,_,hp=gelu_parts(v)
    return v*hp
def gelu_and_slope(v):
    v2,t,hp=gelu_parts(v)
    q=(1.0-t*t)*(0.5*GS+(1.5*GS*GC)*v2)
    return v*hp, hp+v*q
def gelu_slope_curve(v):
    v2,t,hp=gelu_parts(v)
    du=GS+(3*GS*GC)*v2
    s=1.0-t*t
    dt=s*du
    half=0.5*v
    return hp+half*dt, dt*(1.0-v*t*du)+half*s*((6*GS*GC)*v)

def lower_table(turned=False):
    i=lax.broadcasted_iota(jnp.int32,(MB,MB),1 if turned else 0); j=lax.broadcasted_iota(jnp.int32,(MB,MB),0 if turned else 1)
    return jnp.where(j<=i, 1.0/(i+1).astype(f32), 0.0)

def interleave(*runs):
    runs=list(runs)
    while runs:
        for run in list(runs):
            if next(run,"end")=="end": runs.remove(run)

Z1,U1,DE=slice(0,MB),slice(MB,2*MB),slice(2*MB,3*MB)
W1,W2,X2,G1=slice(0,AUG),slice(AUG,AUG+HS),slice(AUG+HS,AUG+HS+MB),slice(AUG+HS+MB,AUG+HS+2*MB)
ZC,N3,G2=slice(0,MB),slice(MB,2*MB),slice(2*MB,3*MB)

def load_rows(NH, proj, kq, kqt, tt, shift, width):
    rows=proj.shape[0]
    lane=lax.broadcasted_iota(jnp.int32,(1,1,128),2)
    one=jnp.where(lane==HS,1.0,0.0)
    for h in range(NH):
        q=proj[:,:,h*128:(h+1)*128]+one
        k=proj[:,:,(NH+h)*128:(NH+h+1)*128]+one
        kq[:,h,0:MB,:]=k.astype(bf16)
        kq[:,h,MB:2*MB,:]=q.astype(bf16)
        kk=proj[:,:,(NH+h)*128:(NH+h)*128+HS]
        vv=proj[:,:,(2*NH+h)*128:(2*NH+h)*128+HS]
        tt[:,h]=shift[h][None]-vv+kk
    @pl.loop(0,rows,step=4)
    def _(r0):
        for r in range(4):
            for h in range(NH):
                both=kq[r0+r,h,0:width,:].astype(f32)
                kqt[r0+r,h]=both.T[0:AUG].astype(bf16)

def forward_kernel(NH, micro, steps, flags, proj, rate, w1, w2, c2, gain, shift,
                   mixed, wide_out, state_out, thin_out,
                   wide, held, thin, sems, kq, kqt, tt, w1s, w2s, c2s, zus, c2h, heads):
    chains=[(c,m,h) for c,(m,h) in enumerate((m,h) for m in range(micro) for h in range(NH))]
    tab=lower_table()
    load_rows(NH,proj,kq,kqt,tt,shift,MB)
    def restart(b):
        for m in range(micro):
            @pl.when(flags[m,b]>0)
            def _():
                for h in range(NH):
                    c=m*NH+h
                    w1s[c]=w1[h]; w2s[c]=w2[h]; c2s[c]=c2[h]
                    zus[c]=dot(kq[m*steps+b,h,:,0:AUG],w1[h].astype(bf16),NN)
    def chain(b):
        w1b={};w2b={};x2b={};sl={};zc={};g2e={};g2b={};g1b={};g1c={};base={};coef={};de={}
        nb=jnp.minimum(b+1,steps-1)
        for c,m,h in chains:
            z=zus[c,0:MB]
            wide[b,c,Z1]=z
            wide[b,c,U1]=zus[c,MB:2*MB]
            x2,sl[c]=gelu_and_slope(z)
            x2b[c]=x2.astype(bf16)
            held[b,c,X2]=x2b[c]
        for c,m,h in chains:
            w2b[c]=w2s[c].astype(bf16)
            held[b,c,W2]=w2b[c]
            c2h[b,c]=c2s[c]
        yield
        for c,m,h in chains:
            zc[c]=dot(x2b[c],w2b[c],NT)+c2s[c]
        for c,m,h in chains:
            w1b[c]=w1s[c].astype(bf16)
            held[b,c,W1]=w1b[c]
        yield
        for c,m,h in chains:
            coef[c]=dot(kq[m*steps+nb,h],kq[m*steps+b,h,0:MB],NT).astype(bf16)
            base[c]=dot(kq[m*steps+nb,h,:,0:AUG],w1b[c],NN)
        for c,m,h in chains:
            r=m*steps+b
            g=gain[h]; t=g*tt[r,h]; z=zc[c]
            gz=g*g*z
            var=rsum(z*z)*INV
            m1=rsum(gz)*INV; m2=rsum(gz*z)*INV; m3=rsum(t*z)*INV; mt=rsum(t)*INV
            r2=lax.rsqrt(var+EPS)
            mean_e=r2*m1+mt
            a=r2*(r2*m2+m3)
            er=rate[r,:,h:h+1]*r2
            g2e[c]=er*(r2*gz+t-mean_e-(r2*a)*z)
            g2b[c]=g2e[c].astype(bf16)
            thin[b,c,G2,0:HS]=g2e[c]
            thin[b,c,ZC,0:HS]=z
            thin[b,c,ZC,HS:HS+1]=r2
            thin[b,c,ZC,HS+1:HS+2]=mean_e
            thin[b,c,ZC,HS+2:HS+3]=a
        yield
        for c,m,h in chains:
            de[c]=dot(g2b[c],w2b[c],NN)
        yield
        for c,m,h in chains:
            wide[b,c,DE]=de[c]
            g1=de[c]*sl[c]
            g1b[c]=g1.astype(bf16)
            g1c[c]=(g1*(1.0/MB)).astype(bf16)
            held[b,c,G1]=g1b[c]
        for c,m,h in chains:
            zus[c]=base[c]-dot(coef[c],g1c[c],NN)
        yield
        for c,m,h in chains:
            w1s[c]=w1s[c]-dot(kqt[m*steps+b,h],g1c[c],NN)
        for c,m,h in chains:
            w2s[c]=w2s[c]-dot((g2e[c]*(1.0/MB)).astype(bf16),x2b[c],TN)
            c2s[c]=c2s[c]-csum(g2e[c])*(1.0/MB)
        yield
    def query(b):
        m1={};u1={};x3={};s2={};ua={}
        for c,m,h in chains:
            r=m*steps+b
            m1[c]=(tab*dot(kq[r,h,MB:2*MB],kq[r,h,0:MB],NT)).astype(bf16)
        yield
        for c,m,h in chains:
            u1[c]=wide[b,c,U1]-dot(m1[c],held[b,c,G1],NN)
            wide[b,c,U1]=u1[c]
        yield
        for c,m,h in chains:
            x3[c]=gelu(u1[c]).astype(bf16)
        yield
        for c,m,h in chains:
            s2[c]=dot(x3[c],held[b,c,X2],NT)
            ua[c]=dot(x3[c],held[b,c,W2],NT)
        yield
        for c,m,h in chains:
            ua[c]=ua[c]+c2h[b,c]-dot((tab*(s2[c]+1.0)).astype(bf16),thin[b,c,G2,0:HS].astype(bf16),NN)
        yield
        for c,m,h in chains:
            u=ua[c]
            u=u-rsum(u)*INV
            r3=lax.rsqrt(rsum(u*u)*INV+EPS)
            n=u*r3
            thin[b,c,N3,0:HS]=n
            thin[b,c,N3,HS:HS+1]=r3
            r=m*steps+b
            heads[r,h]=proj[r,:,h*128:h*128+HS]+n*gain[h]+shift[h]
        yield
    for c,m,h in chains:
        w1s[c]=w1[h]; w2s[c]=w2[h]; c2s[c]=c2[h]
        zus[c]=dot(kq[m*steps,h,:,0:AUG],w1[h].astype(bf16),NN)
    def copies(b):
        return [pltpu.make_async_copy(x.at[b],y.at[b],sems.at[i,b])
                for i,(x,y) in enumerate(((wide,wide_out),(held,state_out),(thin,thin_out)))]
    interleave(chain(0))
    restart(1)
    @pl.loop(1,steps)
    def _(b):
        interleave(chain(b),query(b-1))
        for copy in copies(b-1): copy.start()
        @pl.when(b+1<steps)
        def _():
            restart(b+1)
    interleave(query(steps-1))
    for copy in copies(steps-1): copy.start()
    for m in range(micro):
        s=slice(m*steps,(m+1)*steps)
        mixed[s]=jnp.concatenate([heads[s,h] for h in range(NH)],-1).astype(bf16)
    @pl.loop(0,steps)
    def _(b):
        for copy in copies(b): copy.wait()

def history_shapes(steps,C):
    return [((steps,C,3*MB,FI),f32),((steps,C,AUG+HS+2*MB,FI),bf16),((steps,C,3*MB,128),f32)]

def scan_forward(flags,proj,rate,w1,w2,c2,gain,shift):
    rows,_,lanes=proj.shape
    micro=flags.shape[0]
    NH=lanes//384; steps=rows//micro; C=micro*NH
    vm=pl.BlockSpec(memory_space=pltpu.VMEM); sm=pl.BlockSpec(memory_space=pltpu.SMEM); hbm=pl.BlockSpec(memory_space=pltpu.HBM)
    S=jax.ShapeDtypeStruct; V=pltpu.VMEM
    past=history_shapes(steps,C)
    out=pl.pallas_call(partial(forward_kernel,NH,micro,steps),
        in_specs=[sm]+[vm]*7, out_specs=[vm,hbm,hbm,hbm],
        out_shape=[S((rows,MB,NH*HS),bf16)]+[S(*x) for x in past],
        scratch_shapes=[V(*x) for x in past]+[pltpu.SemaphoreType.DMA((3,steps)),
                        V((rows,NH,2*MB,128),bf16),V((rows,NH,AUG,MB),bf16),V((rows,NH,MB,HS),f32),
                        V((C,AUG,FI),f32),V((C,HS,FI),f32),V((C,1,HS),f32),
                        V((C,2*MB,FI),f32),V((steps,C,1,HS),f32),V((rows,NH,MB,HS),f32)],
        compiler_params=pltpu.CompilerParams(vmem_limit_bytes=FORWARD_VMEM),
        cost_estimate=pl.CostEstimate(flops=18_000_000_000,bytes_accessed=12_000_000,transcendentals=0),
        name="inner_forward")(flags,proj,rate,w1,w2,c2,gain,shift)
    return out[0],tuple(out[1:])

def backward_kernel(NH, micro, steps, flags, dmix, proj, rate, gain, shift, wide_in, state_in, thin_in,
                    dproj, drate, dw1, dw2, dc2, dgain, dshift,
                    wide, held, thin, sems, kq, kqt, tt, p1, p2, pc, eb, p1h, p2h, ff1, qg1, qx2, qg2, qk, qsl, qcv, qd2, qu2, qu1, qx3):
    chains=[(c,m,h) for c,(m,h) in enumerate((m,h) for m in range(micro) for h in range(NH))]
    C=micro*NH
    tab=lower_table(); tabt=lower_table(True)
    def copies(b):
        return [pltpu.make_async_copy(x.at[b],y.at[b],sems.at[i,b])
                for i,(x,y) in enumerate(((wide_in,wide),(state_in,held),(thin_in,thin)))]
    @pl.loop(0,steps)
    def _(b):
        for copy in copies(steps-1-b): copy.start()
    load_rows(NH,proj,kq,kqt,tt,shift,2*MB)
    p1[...]=jnp.zeros(p1.shape,f32); p2[...]=jnp.zeros(p2.shape,f32); pc[...]=jnp.zeros(pc.shape,f32)
    p1h[...]=jnp.zeros(p1h.shape,bf16); p2h[...]=jnp.zeros(p2h.shape,bf16); ff1[...]=jnp.zeros(ff1.shape,f32)
    dw1[...]=jnp.zeros(dw1.shape,f32); dw2[...]=jnp.zeros(dw2.shape,f32); dc2[...]=jnp.zeros(dc2.shape,f32)
    drate[...]=jnp.zeros(drate.shape,f32)
    def query(b):
        o=lax.rem(b,2)
        du2b={};s2t={};d2={};dx3={};m2t={};ds2={};sl3={};du1b={};ds1={};m1t={};dqa={};x3={}
        for c,m,h in chains:
            r=m*steps+b
            n3=thin[b,c,N3,0:HS]; r3=thin[b,c,N3,HS:HS+1]
            hh=dmix[r,:,h*HS:(h+1)*HS]*gain[h]
            du2=r3*(hh-rsum(hh)*INV-n3*(rsum(hh*n3)*INV))
            qd2[o,c]=du2
            du2b[c]=du2.astype(bf16)
            qu2[o,c]=du2b[c]
        for c,m,h in chains:
            x,sl3[c]=gelu_and_slope(wide[b,c,U1])
            x3[c]=x.astype(bf16)
            qx3[o,c]=x3[c]
        yield
        for c,m,h in chains:
            s2t[c]=dot(held[b,c,X2],x3[c],NT)
            d2[c]=dot(du2b[c],thin[b,c,G2,0:HS].astype(bf16),NT)
            dx3[c]=dot(du2b[c],held[b,c,W2],NN)
        yield
        for c,m,h in chains:
            m2t[c]=(tabt*(s2t[c]+1.0)).astype(bf16)
            ds2[c]=(tab*d2[c]).astype(bf16)
        for c,m,h in chains:
            dx3[c]=dx3[c]-dot(ds2[c],held[b,c,X2],NN)
            qg2[o,c]=-dot(m2t[c],du2b[c],NN)
            qx2[o,c]=-dot(ds2[c],x3[c],TN)
        yield
        for c,m,h in chains:
            du1b[c]=(dx3[c]*sl3[c]).astype(bf16)
            qu1[o,c]=du1b[c]
        for c,m,h in chains:
            r=m*steps+b
            ds1[c]=dot(du1b[c],held[b,c,G1],NT)
            m1t[c]=dot(kq[r,h,0:MB],kq[r,h,MB:2*MB],NT)
            dqa[c]=dot(du1b[c],held[b,c,W1],NT)[:,0:HS]
        yield
        for c,m,h in chains:
            ds1[c]=(tab*ds1[c]).astype(bf16)
            m1t[c]=(tabt*m1t[c]).astype(bf16)
        for c,m,h in chains:
            r=m*steps+b
            qg1[o,c]=-dot(m1t[c],du1b[c],NN)
            dr=dmix[r,:,h*HS:(h+1)*HS]
            dproj[r,:,h*128:h*128+HS]=(dr+dqa[c]-dot(ds1[c],kq[r,h,0:MB,:],NN)[:,0:HS]).astype(bf16)
            qk[o,c]=-dot(ds1[c],kq[r,h,MB:2*MB,:],TN)[:,0:HS]
        yield
        for c,m,h in chains:
            sl,cv=gelu_slope_curve(wide[b,c,Z1])
            qsl[o,c]=sl
            qcv[o,c]=wide[b,c,DE]*cv
        yield
    def chain(b):
        o=lax.rem(b,2); pb=jnp.maximum(b-1,0)
        dde={};dz1a={};n2p={};gh={};dz2b={};dx={};dz1b={};base={};coef={};dk={};x2p={}
        for c,m,h in chains:
            gg1=qg1[o,c]+ff1[c]
            dde[c]=(gg1*qsl[o,c]).astype(bf16)
            dz1a[c]=gg1*qcv[o,c]
        yield
        for c,m,h in chains:
            gh[c]=dot(dde[c],held[b,c,W2],NT)
        for c,m,h in chains:
            n2p[c]=dot(held[b,c,X2],p2h[c],NT)
        yield
        for c,m,h in chains:
            r=m*steps+b
            g=gain[h]; gg=g*g
            zc=thin[b,c,ZC,0:HS]; r2=thin[b,c,ZC,HS:HS+1]; me=thin[b,c,ZC,HS+1:HS+2]; a=thin[b,c,ZC,HS+2:HS+3]
            n=zc*r2
            e=gg*n+g*tt[r,h]
            g2=r2*(e-me-n*a)
            hg=gh[c]+qg2[o,c]+(n2p[c]+pc[c])*(1.0/MB)
            rt=rate[r,:,h:h+1]
            q=rsum(hg*g2)
            drate[r,:,h:h+1]=q
            G=rt*hg
            mg=rsum(G)*INV; bb=rsum(G*n)*INV
            ds=r2*(G-mg-n*bb)
            eb[b,c]=ds
            dn=gg*ds-r2*(G*a+e*bb)
            dz2=r2*(dn-rsum(dn)*INV-n*(rsum(dn*n)*INV+rt*q*INV))
            dz2b[c]=dz2.astype(bf16)
            pc[c]=pc[c]-csum(qd2[o,c]+dz2)
        for c,m,h in chains:
            base[c]=dot(kq[m*steps+pb,h,0:MB,0:AUG],p1h[c],NN)
            coef[c]=dot(kq[m*steps+pb,h,0:MB],kq[m*steps+b,h],NT).astype(bf16)
        for c,m,h in chains:
            x2p[c]=dot(thin[b,c,G2,0:HS].astype(bf16),p2h[c],NN)
            dk[c]=dot(held[b,c,G1],p1h[c],NT)[:,0:HS]
        yield
        for c,m,h in chains:
            dx[c]=dot(dz2b[c],held[b,c,W2],NN)
        yield
        for c,m,h in chains:
            full=dx[c]+qx2[o,c]+x2p[c]*(1.0/MB)
            dz1b[c]=(dz1a[c]+full*qsl[o,c]).astype(bf16)
        both={}
        for c,m,h in chains:
            both[c]=jnp.concatenate([dz1b[c],qu1[o,c]],0)
            ff1[c]=(base[c]-dot(coef[c],both[c],NN))*(1.0/MB)
        yield
        for c,m,h in chains:
            r=m*steps+b
            p1[c]=p1[c]-dot(kqt[r,h],both[c],NN)
            p2[c]=p2[c]-dot(jnp.concatenate([qu2[o,c],thin[b,c,G2,0:HS].astype(bf16),dz2b[c]],0),jnp.concatenate([qx3[o,c],dde[c],held[b,c,X2]],0),TN)
        for c,m,h in chains:
            r=m*steps+b
            dy=eb[b,c]*gain[h]
            dkk=dy+qk[o,c]+dk[c]*(1.0/MB)+dot(dz1b[c],held[b,c,W1],NT)[:,0:HS]
            dproj[r,:,(NH+h)*128:(NH+h)*128+HS]=dkk.astype(bf16)
            dproj[r,:,(2*NH+h)*128:(2*NH+h)*128+HS]=(-dy).astype(bf16)
        for c,m,h in chains:
            p1h[c]=p1[c].astype(bf16); p2h[c]=p2[c].astype(bf16)
        yield
    def restart(b):
        for m in range(micro):
            @pl.when(flags[m,b]>0)
            def _():
                for h in range(NH):
                    c=m*NH+h
                    dw1[h]=dw1[h]-p1[c]; dw2[h]=dw2[h]-p2[c]; dc2[h]=dc2[h]-pc[c]
                    p1[c]=jnp.zeros((AUG,FI),f32); p2[c]=jnp.zeros((HS,FI),f32); pc[c]=jnp.zeros((1,HS),f32)
                    p1h[c]=jnp.zeros((AUG,FI),bf16); p2h[c]=jnp.zeros((HS,FI),bf16); ff1[c]=jnp.zeros((MB,FI),f32)
    for copy in copies(steps-1): copy.wait()
    interleave(query(steps-1))
    @pl.loop(0,steps-1)
    def _(back):
        b=steps-1-back
        for copy in copies(b-1): copy.wait()
        interleave(chain(b),query(b-1))
        restart(b)
    interleave(chain(0))
    restart(0)
    for h in range(NH):
        dg=jnp.zeros((1,HS),f32); ds=jnp.zeros((1,HS),f32)
        for m in range(micro):
            c=m*NH+h; s=slice(m*steps,(m+1)*steps)
            dr=dmix[s,:,h*HS:(h+1)*HS]
            zc=thin[:,c,ZC,0:HS]; r2=thin[:,c,ZC,HS:HS+1]
            g=gain[h][None]
            dm=eb[:,c]
            part=dr*thin[:,c,N3,0:HS]+dm*(2.0*g*(zc*r2)+tt[s,h])
            dg=dg+jnp.sum(jnp.sum(part,0),0,keepdims=True)
            ds=ds+jnp.sum(jnp.sum(dr+dm*g,0),0,keepdims=True)
        dgain[h]=dg; dshift[h]=ds
    for p in range(3*NH):
        dproj[:,:,p*128+HS:(p+1)*128]=jnp.zeros((micro*steps,MB,128-HS),bf16)
    rt=rate[...]
    drate[...]=drate[...]*rt*(1.0-HS*rt)

def scan_backward(flags,dmix,proj,rate,gain,shift,hist):
    rows,_,lanes=proj.shape
    micro=flags.shape[0]
    NH=lanes//384; steps=rows//micro; C=micro*NH
    vm=pl.BlockSpec(memory_space=pltpu.VMEM); sm=pl.BlockSpec(memory_space=pltpu.SMEM); hbm=pl.BlockSpec(memory_space=pltpu.HBM)
    S=jax.ShapeDtypeStruct; V=pltpu.VMEM
    out=pl.pallas_call(partial(backward_kernel,NH,micro,steps),
        in_specs=[sm]+[vm]*5+[hbm]*3, out_specs=[vm]*7,
        out_shape=[S((rows,MB,lanes),bf16),S((rows,MB,8),f32),S((NH,AUG,FI),f32),S((NH,HS,FI),f32),S((NH,1,HS),f32),S((NH,1,HS),f32),S((NH,1,HS),f32)],
        scratch_shapes=[V(*x) for x in history_shapes(steps,C)]+[pltpu.SemaphoreType.DMA((3,steps)),V((rows,NH,2*MB,128),bf16),V((rows,NH,AUG,2*MB),bf16),V((rows,NH,MB,HS),f32),
                        V((C,AUG,FI),f32),V((C,HS,FI),f32),V((C,1,HS),f32),V((steps,C,MB,HS),f32),
                        V((C,AUG,FI),bf16),V((C,HS,FI),bf16),V((C,MB,FI),f32),
                        V((2,C,MB,FI),f32),V((2,C,MB,FI),f32),V((2,C,MB,HS),f32),V((2,C,MB,HS),f32),V((2,C,MB,FI),f32),V((2,C,MB,FI),f32),
                        V((2,C,MB,HS),f32),V((2,C,MB,HS),bf16),V((2,C,MB,FI),bf16),V((2,C,MB,FI),bf16)],
        compiler_params=pltpu.CompilerParams(vmem_limit_bytes=BACKWARD_VMEM),
        cost_estimate=pl.CostEstimate(flops=1000,bytes_accessed=1000,transcendentals=0),
        name="inner_backward")(flags,dmix,proj,rate,gain,shift,*hist)
    return out[0],out[1],tuple(out[2:])

def gelu_full(v):
    v2,t,hp=gelu_parts(v)
    q=(1.0-t*t)*(0.5*GS+(1.5*GS*GC)*v2)
    return v*hp, hp+v*q

def struct(shape, dtype):
    return jax.ShapeDtypeStruct(shape, dtype)

def call(kernel, name, flops, arrays, shapes, scratch=(), limit=None):
    vm=pl.BlockSpec(memory_space=pltpu.VMEM); sm=pl.BlockSpec(memory_space=pltpu.SMEM)
    specs=[sm if a.ndim==1 else vm for a in arrays]
    moved=1000 if flops<2000 else sum(a.size*a.dtype.itemsize for a in arrays)+sum(s.size*s.dtype.itemsize for s in shapes)
    return pl.pallas_call(kernel, in_specs=specs, out_specs=[vm]*len(shapes), out_shape=list(shapes), scratch_shapes=list(scratch),
        compiler_params=pltpu.CompilerParams(vmem_limit_bytes=limit or SMALL_VMEM),
        cost_estimate=pl.CostEstimate(flops=flops,bytes_accessed=moved,transcendentals=0), name=name)(*arrays)

def bits(n):
    return n.bit_length()-1

def near_slot(peer, m, rank, pair, micro):
    return peer*(micro*pair)+m*pair+rank

def far_slot(peer, m, rank, pair, micro, size, part):
    q=pair//size
    return lax.shift_right_logical(rank,bits(q))*part+peer*(micro*q)+m*q+(rank&(q-1))

def send_kernel(pair, size, given, owner, x, up, sent_x, sent_up, recv_col, recv_row, turn_row, fin_col, end_col):
    micro,tok=given.shape
    rows=micro*tok
    part=rows//size
    at=lax.broadcasted_iota(jnp.int32,(rows,tok),0)
    low=lax.broadcasted_iota(jnp.int32,(tok,tok),0); high=lax.broadcasted_iota(jnp.int32,(tok,tok),1)
    ax=None
    for m in range(micro):
        span=slice(m*tok,(m+1)*tok)
        along=jnp.broadcast_to(given[m:m+1,:].astype(f32),(tok,tok))
        down=along.T
        row=jnp.sum(jnp.where(down<along,1.0,0.0),0,keepdims=True).astype(jnp.int32)
        col=jnp.sum(jnp.where(along<down,1.0,0.0),1,keepdims=True).astype(jnp.int32)
        split=lambda r:(lax.shift_right_logical(r,bits(pair)),r&(pair-1))
        peer,rank=split(row)
        hot=jnp.where(at==near_slot(peer,m,rank,pair,micro),1.0,0.0).astype(bf16)
        a=dot(hot,x[m],NN); b=dot(hot,up[m],NN)
        if m==0: ax,au=a,b
        else: ax,au=ax+a,au+b
        peer,rank=split(col)
        fin_col[span,:]=near_slot(peer,m,rank,pair,micro)
        end_col[span,:]=far_slot(peer,m,rank,pair,micro,size,part)
        anchor=lax.shift_right_logical(owner[m:m+1,:],bits(tok))
        along=jnp.broadcast_to(anchor.astype(f32),(tok,tok))
        down=along.T
        same=jnp.where(along==down,1.0,0.0)
        col=jnp.sum(jnp.where(high<low,same,0.0),1,keepdims=True).astype(jnp.int32)
        row=jnp.sum(jnp.where(low<high,same,0.0),0,keepdims=True).astype(jnp.int32)
        recv_col[span,:]=near_slot(down[:,0:1].astype(jnp.int32),m,col,pair,micro)
        recv_row[:,span]=near_slot(anchor,m,row,pair,micro)
        turn_row[:,span]=far_slot(anchor,m,row,pair,micro,size,part)
    sent_x[...]=ax.astype(bf16)
    sent_up[...]=au.astype(bf16)

def send_rows(pair, size, given, owner, x, up):
    micro,tok,width=x.shape
    rows=micro*tok
    i=jnp.int32
    return call(partial(send_kernel,pair,size),"send_rows",2_000_000_000,[given,owner,x,up],
        [struct((rows,width),bf16),struct((rows,width),bf16),struct((rows,1),i),struct((1,rows),i),struct((1,rows),i),struct((rows,1),i),struct((rows,1),i)])

def hot_from_col(col, columns):
    n=col.shape[0]
    return jnp.where(lax.broadcasted_iota(jnp.int32,(n,columns),1)==col,1.0,0.0).astype(bf16)

def hot_from_row(row, count, first=0):
    n=row.shape[1]
    return jnp.where(lax.broadcasted_iota(jnp.int32,(count,n),0)+first==row,1.0,0.0).astype(bf16)

def project_kernel(arrived, col, ngain, qkv, ratew, rateb, resid, normed, proj, rate):
    rows=arrived.shape[0]
    r=dot(hot_from_col(col[...],rows),arrived[...],NN)
    resid[...]=r.astype(bf16)
    n=(r*lax.rsqrt(rsum(r*r)*(1.0/r.shape[1])+EPS)*ngain[...]).astype(bf16)
    normed[...]=n
    rate[...]=(1.0/HS)/(1.0+jnp.exp(-(dot(n,ratew[...],NN)+rateb[...])))
    proj[...]=dot(n,qkv[...],NT)

def project(arrived, col, ngain, qkv, ratew, rateb):
    rows,width=arrived.shape
    return call(project_kernel,"project",1_500_000_000,[arrived,col,ngain,qkv,ratew,rateb],
        [struct((rows,width),bf16),struct((rows,width),bf16),struct((rows,qkv.shape[0]),f32),struct((rows,ratew.shape[1]),f32)])

def middle_kernel(T, cut, me, col, row, turn, arrived, mixed, normed, resid, post, gateout, fgain, swiglu, down,
                  up, out_sent, act, sgrad, nmid, gated, mgrad, hgrad, ggrad, dpg, dpb, dfg, base, gpart, rpart,
                  gpre, hid, feed, mid, stats, pbuf):
    c=pl.program_id(0)
    rows,wide=resid.shape
    hw=mixed.shape[2]
    width=T*hw
    half=sgrad.shape[1]//2
    def flat(ref,i,lead=()):
        w=ref[i]
        return w.reshape(w.shape[0]*w.shape[1],w.shape[2])
    def vectors(i):
        v=post[i,0].astype(f32)
        return v[0:1,0:hw]+v[1:2,0:hw]+v[2:3,0:hw], v[3:4,0:hw]+v[4:5,0:hw]+v[5:6,0:hw]
    @pl.when(c==0)
    def _():
        up[...]=dot(hot_from_col(col[...],rows),arrived[...],NN).astype(bf16)
        center=sum(rsum(mixed[i].astype(f32)) for i in range(T))*(1.0/width)
        square=0.0
        for i in range(T):
            x=mixed[i].astype(f32)-center
            square=square+rsum(x*x)
        inv=lax.rsqrt(square*(1.0/width)+EPS)
        stats[:,0:1]=center
        stats[:,1:2]=inv
        mixer=None
        for i in range(T):
            w=flat(gateout,i)
            pg,pb=vectors(i)
            pre=dot(normed[...],w[0:hw],NT)
            gpre[i]=pre
            g=(((mixed[i].astype(f32)-center)*inv*pg+pb)*gelu(pre)).astype(bf16)
            @pl.when(me[0]==i)
            def _():
                gated[...]=g
            y=dot(g,w[hw:2*hw],NN)
            mixer=y if mixer is None else mixer+y
        h=resid[...].astype(f32)+mixer
        hid[...]=h
        nmid[...]=(h*lax.rsqrt(rsum(h*h)*(1.0/wide)+EPS)*fgain[...]).astype(bf16)
        feed[...]=jnp.zeros((rows,wide),f32)
        mid[...]=jnp.zeros((rows,wide),f32)
    block=rows
    @pl.loop(0,1)
    def _(b):
        at=pl.ds(pl.multiple_of(b*block,block),block)
        nm=nmid[at,:]
        dn=flat(down,0)
        w=swiglu[0]
        unit=w.shape[1]//2
        wg=w[:,0:unit].reshape(half,wide)
        wu=w[:,unit:2*unit].reshape(half,wide)
        gh=dot(nm,wg,NT)
        uh=dot(nm,wu,NT)
        da=dot(up[at,:],dn,NT)
        sg=1.0/(1.0+jnp.exp(-gh))
        silu=gh*sg
        a=(silu*uh).astype(bf16)
        s1=(da*uh*sg*(1.0+gh*(1.0-sg))).astype(bf16)
        s2=(da*silu).astype(bf16)
        @pl.when(me[0]==c)
        def _():
            act[at,:]=a
            sgrad[at,0:half]=s1
            sgrad[at,half:2*half]=s2
        mid[at,:]=mid[at,:]-(dot(s1,wg,NN)+dot(s2,wu,NN))
        feed[at,:]=feed[at,:]-dot(a,dn,NN)
    @pl.when(c==T-1)
    def _():
        h=hid[...]
        own=(h-feed[...]).astype(bf16)
        out_sent[...]=dot(hot_from_row(row[...],rows),own,NN).astype(bf16)
        sc=lax.rsqrt(rsum(h*h)*(1.0/wide)+EPS)
        m=-mid[...]
        dfg[...]=csum(m*h*sc)
        ms=m*fgain[...]
        hg=up[...].astype(f32)+sc*ms-h*(sc*sc*sc*(rsum(ms*h)*(1.0/wide)))
        full=hg.astype(bf16)
        mgrad[...]=full
        part=base.shape[0]
        hot=hot_from_row(turn[...],part,me[0]*part)
        base[...]=dot(hot,full,NN)+dot(hot,(hg-full.astype(f32)).astype(bf16),NN)
        rpart[...]=dot(hot,resid[...],NN)
        center=stats[:,0:1]; inv=stats[:,1:2]
        s1=0.0; s2=0.0
        for i in range(T):
            w=flat(gateout,i)
            pgn,pb=vectors(i)
            std=(mixed[i].astype(f32)-center)*inv
            a,slope=gelu_full(gpre[i])
            gg=dot(full,w[hw:2*hw],NT)
            gr=(gg*(std*pgn+pb)*slope).astype(bf16)
            y=dot(dot(hot,gr,NN).astype(bf16),w[0:hw],NN)
            if i==0: gpart[...]=y
            else: gpart[...]=gpart[...]-(-y)
            pg=gg*a
            p=pg*pgn
            pbuf[i]=p
            s1=s1+rsum(p); s2=s2+rsum(p*std)
            @pl.when(me[0]==i)
            def _():
                ggrad[...]=gr
                dpg[...]=csum(pg*std); dpb[...]=csum(pg)
        std=(mixed[me[0]].astype(f32)-center)*inv
        hgrad[...]=inv*(pbuf[me[0]]-s1*(1.0/width)-std*(s2*(1.0/width)))

def middle(me, col, row, turn, arrived, mixed, normed, resid, weights, fgain):
    T,rows,hw=mixed.shape; wide=resid.shape[1]; D,tall=weights.shape[1:3]
    a,b,g,p=weight_cuts(tall)
    half=a*D//2
    whole=lambda x:pl.BlockSpec(x.shape,lambda c,n=len(x.shape):(0,)*n,pipeline_mode=pl.Buffered(1))
    specs=[pl.BlockSpec(memory_space=pltpu.SMEM)]+[whole(x) for x in (col,row,turn,arrived,mixed,normed,resid)]
    specs+=[pl.BlockSpec((T,1,p,wide),lambda c:(0,0,(a+b+g)//p,0),pipeline_mode=pl.Buffered(1)),
            pl.BlockSpec((T,D,g,wide),lambda c:(0,0,(a+b)//g,0),pipeline_mode=pl.Buffered(1)),
            whole(fgain),
            pl.BlockSpec((1,D,a,wide),lambda c:(c,0,0,0)),
            pl.BlockSpec((1,D,b,wide),lambda c:(c,0,a//b,0))]
    shapes=[struct((rows,wide),bf16),struct((rows,wide),bf16),struct((rows,half),bf16),struct((rows,2*half),bf16),struct((rows,wide),bf16),
            struct((rows,hw),bf16),struct((rows,wide),bf16),struct((rows,hw),f32),struct((rows,hw),bf16),
            struct((1,hw),f32),struct((1,hw),f32),struct((1,wide),f32)]+[struct((rows//T,wide),f32)]*3
    V=pltpu.VMEM
    return pl.pallas_call(partial(middle_kernel,T,None),
        grid=(T,), in_specs=specs, out_specs=[pl.BlockSpec(s.shape,lambda c,n=len(s.shape):(0,)*n,pipeline_mode=pl.Buffered(1)) for s in shapes], out_shape=shapes,
        scratch_shapes=[V((T,rows,hw),f32),V((rows,wide),f32),V((rows,wide),f32),V((rows,wide),f32),V((rows,128),f32),V((T,rows,hw),f32)],
        compiler_params=pltpu.CompilerParams(vmem_limit_bytes=MIDDLE_VMEM,dimension_semantics=("arbitrary",)),
        cost_estimate=pl.CostEstimate(flops=14_000_000_000,bytes_accessed=25_000_000,transcendentals=0),name="middle")(
        me,col,row,turn,arrived,mixed,normed,resid,weights,weights,fgain,weights,weights)

def thirds(x):
    high=x.astype(bf16).astype(f32)
    rest=x-high
    center=rest.astype(bf16).astype(f32)
    return [high,center,rest-center]

def pack_kernel(count, d, wg, wu, down, turned, out, pgain, pbias, piece):
    unit=wg.shape[1]; width=down.shape[1]; hw=turned.shape[0]
    piece[0:unit,:]=wg[...].astype(f32).T.astype(bf16)
    piece[unit:2*unit,:]=wu[...].astype(f32).T.astype(bf16)
    at=2*unit
    n=down.shape[0]//count
    piece[at:at+n,:]=down[pl.ds(pl.multiple_of(d[0]*n,n),n),:]
    at+=n
    n=2*hw//count
    @pl.when(d[0]<count//2)
    def _():
        piece[at:at+n,:]=turned[pl.ds(pl.multiple_of(d[0]*n,n),n),:]
    @pl.when(d[0]>=count//2)
    def _():
        piece[at:at+n,:]=out[pl.ds(pl.multiple_of((d[0]-count//2)*n,n),n),:]
    at+=n
    rows=jnp.concatenate(thirds(pgain[...])+thirds(pbias[...])+[jnp.zeros((10,hw),f32)],0)
    piece[at:at+16,:]=jnp.concatenate([rows,jnp.zeros((16,width-hw),f32)],1).astype(bf16)

def pack_weights(count, d, wg, wu, down, turned, out, pgain, pbias):
    unit=wg.shape[1]; width=down.shape[1]
    tall=2*unit+(down.shape[0]+2*turned.shape[0])//count+16
    return call(partial(pack_kernel,count),"pack_weights",100_000_000,[d,wg,wu,down,turned,out,pgain,pbias],[struct((tall,width),bf16)])[0]

def weight_cuts(tall):
    unit=tall//16
    return 8*unit,4*unit,3*unit,unit

def in_part_kernel(T, me, row, dproj, logit, qkv, ratew, *sums):
    lg=logit[...]
    y=dot(dproj[...],qkv[...],NN)+dot(lg.astype(bf16),ratew[...],NT)
    y=y.astype(bf16)
    part=y.shape[0]//T
    for k in range(T):
        sums[k][...]=dot(hot_from_row(row[...],part,lax.rem(me[0]+k,T)*part),y,NN).astype(bf16)

def in_part(T, me, row, dproj, logit, qkv, ratew):
    rows=dproj.shape[0]; width=qkv.shape[1]
    return call(partial(in_part_kernel,T),"in_part",1000,[me,row,dproj,logit,qkv,ratew],[struct((rows//T,width),bf16)]*T)

def early_kernel(count, act, up, nmid, sgrad, gated, mgrad, normed, ggrad, sent, *outs):
    width=nmid.shape[1]
    og=jnp.concatenate([dot(gated[...],mgrad[...],TN),dot(ggrad[...],normed[...],TN)],0).astype(bf16)
    dn=dot(act[...],up[...],TN).astype(bf16)
    left=dot(nmid[...],sgrad[:,0:width],TN).astype(bf16)
    right=dot(nmid[...],sgrad[:,width:],TN).astype(bf16)
    third=width//3
    right=jnp.concatenate([right[i*third:(i+1)*third] for i in range(3)],1)
    pieces=(left,right,dn,og)
    if len(outs)==1:
        at=0
        for y in pieces:
            n=y.shape[0]//count
            for d in range(count):
                outs[0][d,at:at+n]=y[d*n:(d+1)*n]
            at+=n
        n=sent.shape[0]//count
        for d in range(count): outs[0][d,at:at+n]=sent[d*n:(d+1)*n,:]
    else:
        for o,y in zip(outs,pieces): o[...]=y

def aligned(count, sizes):
    return all(n%(16*count)==0 for n in sizes)

def early_grads(count, act, up, nmid, sgrad, gated, mgrad, normed, ggrad, sent):
    width=nmid.shape[1]; half=act.shape[1]; hw=gated.shape[1]
    sizes=(width,width//3,half,2*hw)
    whole=aligned(count,sizes+(sent.shape[0],))
    shapes=[struct((count,(sum(sizes)+sent.shape[0])//count,width),bf16)] if whole else [struct((n,width),bf16) for n in sizes]
    out=call(partial(early_kernel,count),"early_grads",1000,[act,up,nmid,sgrad,gated,mgrad,normed,ggrad,sent],shapes)
    return out[0] if whole else jnp.concatenate([y.reshape(count,-1,width) for y in (*out,sent)],1)

def early_out_kernel(edges, early, swiglu, down, pair, full, sems):
    def piece(k):
        x=early[:,edges[k]:edges[k+1],:]
        return x.reshape(x.shape[0]*x.shape[1],x.shape[2]).astype(f32)
    width=early.shape[2]
    half=full.shape[2]
    left=piece(0)
    full[0]=left[:,0:half]
    full[1,:,0:width-half]=left[:,half:width]
    right=piece(1)
    third=width//3
    for k in range(3):
        full[1,k*third:(k+1)*third,width-half:]=right[:,k*third:(k+1)*third]
    copies=[pltpu.make_async_copy(full.at[k],swiglu.at[:,k,:],sems.at[k]) for k in range(2)]
    for copy in copies: copy.start()
    down[...]=piece(2)
    pair[...]=piece(3)
    for copy in copies: copy.wait()

def early_out(edges, early):
    count,_,width=early.shape
    rows=[count*(edges[k+1]-edges[k]) for k in range(4)]
    half=(width+width//3)//2
    vm=pl.BlockSpec(memory_space=pltpu.VMEM)
    return pl.pallas_call(partial(early_out_kernel,edges),in_specs=[vm],
        out_specs=[pl.BlockSpec(memory_space=pltpu.HBM),vm,vm],
        out_shape=[struct((width,2,half),f32),struct((rows[2],width),f32),struct((rows[3],width),f32)],
        scratch_shapes=[pltpu.VMEM((2,width,half),f32),pltpu.SemaphoreType.DMA((2,))],
        compiler_params=pltpu.CompilerParams(vmem_limit_bytes=FORWARD_VMEM),
        cost_estimate=pl.CostEstimate(flops=6_000_000_000,bytes_accessed=1000,transcendentals=0),name="early_out")(early)

def late_out_kernel(heads, hw, cut, late, big, first, second, first_b, second_b, dgain, dshift, dpg, dpb, dfg, rate_w, rate_b):
    count,tall,width=late.shape
    x=late[...].astype(f32)
    big[...]=x[:,0:cut].reshape(count*cut,width)
    rest=x[:,cut:].reshape(count*(tall-cut),width)
    for h in range(heads):
        first[h]=rest[0:HS,h*FI:(h+1)*FI]
        second[h]=rest[HS:2*HS,h*FI:(h+1)*FI]
        at=2*HS
        first_b[h:h+1,:]=rest[at+8:at+9,h*FI:(h+1)*FI]
        for ref,k in ((second_b,10),(dgain,11),(dshift,12)):
            ref[h:h+1,:]=rest[at+k:at+k+1,h*HS:(h+1)*HS]
    dfg[...]=rest[at+9:at+10,:]
    dpg[...]=rest[at+13:at+14,0:hw]
    dpb[...]=rest[at+14:at+15,0:hw]
    rate_w[...]=rest[at:at+heads,:]
    rate_b[...]=rest[at+15:at+16,0:heads]

def late_out(heads, hw, cut, late):
    width=late.shape[2]; count=late.shape[0]
    s=lambda *d:struct(d,f32)
    return call(partial(late_out_kernel,heads,hw,cut),"late_out",1000,[late],
        [s(count*cut,width),s(heads,HS,FI),s(heads,HS,FI),s(heads,FI),s(heads,HS),s(heads,HS),s(heads,HS),s(1,hw),s(1,hw),s(1,width),s(heads,width),s(1,heads)],
        limit=FORWARD_VMEM)

def late_kernel(heads, count, dproj, normed, logit, dw1, dw2, dc2, dgain, dshift, dpg, dpb, dfg, *refs):
    outs=refs[:-1]; rest=refs[-1]
    width=normed.shape[1]
    n=normed[...]
    packed=jnp.concatenate([dot(dproj[:,g*128:(g+1)*128],n,TN)[0:HS] for g in range(3*heads)],0)
    lg=logit[...]
    rest[...]=jnp.zeros(rest.shape,f32)
    for h in range(heads):
        rest[0:HS,h*FI:(h+1)*FI]=dw1[h,0:HS]
        rest[HS:2*HS,h*FI:(h+1)*FI]=dw2[h]
    rest[2*HS:2*HS+8,:]=dot(lg.astype(bf16),n,TN)
    for h in range(heads):
        rest[2*HS+8:2*HS+9,h*FI:(h+1)*FI]=dw1[h,HS:HS+1]
        rest[2*HS+10:2*HS+11,h*HS:(h+1)*HS]=dc2[h]
        rest[2*HS+11:2*HS+12,h*HS:(h+1)*HS]=dgain[h]
        rest[2*HS+12:2*HS+13,h*HS:(h+1)*HS]=dshift[h]
    hw=dpg.shape[1]
    rest[2*HS+9:2*HS+10,:]=dfg[...]
    rest[2*HS+13:2*HS+14,0:hw]=dpg[...]
    rest[2*HS+14:2*HS+15,0:hw]=dpb[...]
    rest[2*HS+15:2*HS+16,0:lg.shape[1]]=csum(lg)
    if len(outs)==1:
        per=packed.shape[0]//count; more=rest.shape[0]//count
        for d in range(count):
            outs[0][d,0:per+more]=jnp.concatenate([packed[d*per:(d+1)*per],rest[d*more:(d+1)*more,:]],0).astype(bf16)
    else:
        outs[0][...]=packed.astype(bf16); outs[1][...]=rest[...].astype(bf16)

def late_grads(count, dproj, normed, logit, dw1, dw2, dc2, dgain, dshift, dpg, dpb, dfg):
    heads=dw1.shape[0]; width=normed.shape[1]
    sizes=(3*heads*HS,3*HS)
    whole=all(n%(8*count)==0 for n in sizes) and sum(sizes)%(16*count)==0
    shapes=[struct((count,sum(sizes)//count,width),bf16)] if whole else [struct((n,width),bf16) for n in sizes]
    out=call(partial(late_kernel,heads,count),"late_grads",1000,[dproj,normed,logit,dw1,dw2,dc2,dgain,dshift,dpg,dpb,dfg],
        shapes,[pltpu.VMEM((3*HS,width),f32)])
    return out[0] if whole else jnp.concatenate([y.reshape(count,-1,width) for y in out],1)

def in_rows_kernel(T, *refs):
    got=refs[:T]
    base,gpart,rpart,ngain=refs[T:T+4]
    outs=refs[T+4:]
    part,wide=base.shape
    r=rpart[...]
    sc=lax.rsqrt(rsum(r*r)*(1.0/wide)+EPS)
    s=gpart[...]
    for k in range(T):
        s=s+got[k][...].astype(f32)
    g=csum(s*(r*sc))
    high=g.astype(bf16)
    rest=g-high.astype(f32)
    center=rest.astype(bf16)
    three=jnp.concatenate([high.astype(f32),center.astype(f32),rest-center.astype(f32),jnp.zeros((13,wide),f32)],0)
    s=s*ngain[...]
    y=(base[...]+sc*s-r*(sc*sc*sc*(rsum(s*r)*(1.0/wide)))).astype(bf16)
    three=three.astype(bf16)
    if len(outs)==1:
        count=outs[0].shape[0]; lines=part//count
        for d in range(count):
            outs[0][d,0:lines]=y[d*lines:(d+1)*lines]
            outs[0][d,lines:lines+16]=three
    else:
        outs[0][...]=y; outs[1][...]=three

def in_rows(count, got, base, gpart, rpart, ngain):
    part,wide=base.shape; T=len(got)
    out=call(partial(in_rows_kernel,T),"in_rows",1000,[*got,base,gpart,rpart,ngain],
        [struct((count,part//count+16,wide),bf16)] if aligned(count,(part,)) else [struct((part,wide),bf16),struct((16,wide),bf16)],
        limit=FORWARD_VMEM)
    if len(out)==1: return out[0]
    return jnp.concatenate([out[0].reshape(count,-1,wide),jnp.broadcast_to(out[1][None],(count,16,wide))],1)

def settle_kernel(micro, spans, col, *refs):
    got=refs[:-1]; out=refs[-1]
    tok=col.shape[0]//micro
    for m in range(micro):
        y=None
        for k,g in enumerate(got):
            hot=jnp.where(lax.broadcasted_iota(jnp.int32,(tok,spans),1)+k*spans==col[m*tok:(m+1)*tok,:],1.0,0.0).astype(bf16)
            z=dot(hot,g[0:spans,:],NN)
            y=z if y is None else y+z
        out[m]=y.astype(bf16)

def settle(micro, col, got, spans, name):
    rows=col.shape[0]; wide=got[0].shape[1]
    return call(partial(settle_kernel,micro,spans),name,1000,[col,*got],[struct((micro,rows//micro,wide),bf16)])[0]

from jax.sharding import PartitionSpec as P

MICRO=2

def restart_flags(lengths, steps):
    k = jnp.arange(lengths.shape[1], dtype=jnp.int32)
    starts = jnp.sum(jnp.where((k[None, :] < k[:, None])[None], lengths[:, None, :], 0), 2)
    at = jnp.arange(steps, dtype=jnp.int32) * MB
    hit = (starts[:, None, :] == at[None, :, None]) & (lengths[:, None, :] > 0)
    return jnp.pad(jnp.any(hit, 2).astype(jnp.int32), ((0, 0), (0, 1)))

def pad_heads(array, axis):
    shape = array.shape
    split = shape[:axis] + (shape[axis] // HS, HS) + shape[axis + 1:]
    padded = jnp.pad(array.reshape(split), [(0, 0)] * (axis + 1) + [(0, HS)] + [(0, 0)] * (len(shape) - axis - 1))
    return padded.reshape(shape[:axis] + (2 * shape[axis],) + shape[axis + 1:])

def drop_pad(array, axis):
    shape = array.shape
    split = array.reshape(shape[:axis] + (shape[axis] // 128, 128) + shape[axis + 1:])
    kept = lax.slice_in_dim(split, 0, HS, axis=axis + 1)
    return kept.reshape(shape[:axis] + (shape[axis] // 2,) + shape[axis + 1:])

def swap(array, axis="dp"):
    return lax.all_to_all(array, axis, split_axis=0, concat_axis=0, tiled=True)

def turn(array, k):
    size = lax.axis_size("tensor")
    return lax.ppermute(array, "tensor", [(i, (i + k) % size) for i in range(size)])

def split_three(array):
    high = array.astype(bf16)
    rest = array - high.astype(f32)
    middle_part = rest.astype(bf16)
    return [high, middle_part, (rest - middle_part.astype(f32)).astype(bf16)]

def gather_weights(swiglu, down, gate, out, post_gain, post_bias):
    count = lax.axis_size("dp")
    size = lax.axis_size("tensor")
    d = lax.axis_index("dp")
    width = out.shape[1]
    def rows_of(array):
        piece = array.shape[0] // count
        return lax.dynamic_slice_in_dim(array, d * piece, piece, 0)
    piece = swiglu.shape[2] // count
    if count == 8:
        cut = lax.dynamic_slice_in_dim(swiglu, d * piece, piece, 2)
        mine = pack_weights(
            count, d.astype(jnp.int32).reshape(1), cut[:, 0], cut[:, 1], down, gate.T, out, post_gain[None], post_bias[None]
        )
        return lax.all_gather(mine, ("tensor", "dp")).reshape(size, count, -1, width)
    turned = lax.dynamic_slice_in_dim(swiglu, d * piece, piece, 2).transpose(1, 2, 0)
    post = jnp.stack(split_three(post_gain) + split_three(post_bias))
    post = jnp.pad(post, ((0, 10), (0, width - post.shape[1])))
    lines = [turned.reshape(-1, width), rows_of(down), rows_of(jnp.concatenate([gate.T, out], 0))]
    lines.append(rows_of(jnp.concatenate([post] * 8, 0)))
    got = lax.all_gather(jnp.concatenate(lines, 0), ("tensor", "dp"))
    first = got[:, :2 * piece].reshape(size, 8, count // 8, 2, piece, width)
    parts = [jnp.swapaxes(first, 2, 3).reshape(size, 8, -1, width)]
    at = 2 * piece
    for x in lines[1:]:
        parts.append(got[:, at:at + x.shape[0]].reshape(size, 8, -1, width))
        at += x.shape[0]
    return jnp.concatenate(parts, 2)

def shards(
    inputs, cotangent, lengths, owner_rows, given_rows, norm_gain, qkv_weight, rate_weight, rate_bias,
    inner_first, inner_first_bias, inner_second, inner_second_bias, inner_gain, inner_shift, gate_weight,
    post_gain, post_bias, out_weight, ffn_gain, swiglu_weight, down_weight,
):
    tok = inputs.shape[1]
    width = inputs.shape[2]
    rows = MICRO * tok
    blocks = rows // MB
    steps = tok // MB
    heads = rate_weight.shape[1]
    size = lax.axis_size("tensor")
    pair = tok // lax.axis_size("dp")
    me = lax.axis_index("tensor").astype(jnp.int32).reshape(1)
    weights = gather_weights(swiglu_weight, down_weight, gate_weight, out_weight, post_gain, post_bias)
    sent_in, sent_up, recv_col, recv_row, turn_row, fin_col, end_col = send_rows(
        pair, size, given_rows, owner_rows, inputs, cotangent
    )
    arrived_in = swap(sent_in)
    arrived_up = swap(sent_up)
    flags = restart_flags(lengths, steps)
    qkv_pad = pad_heads(qkv_weight.transpose(1, 2, 0).reshape(-1, width), 0)
    rate_pad = jnp.pad(rate_weight, ((0, 0), (0, 8 - heads)))
    bias_pad = jnp.pad(rate_bias, (0, 8 - heads))[None]
    first = jnp.concatenate(
        [inner_first, inner_first_bias[:, None], jnp.zeros((heads, AUG - HS - 1, FI), f32)], 1
    )
    second = jnp.swapaxes(inner_second - jnp.mean(inner_second, -1, keepdims=True), 1, 2)
    second_bias = (inner_second_bias - jnp.mean(inner_second_bias, -1, keepdims=True))[:, None]
    gain = inner_gain[:, None]
    shift = inner_shift[:, None]
    resid, normed, projected, rates = project(arrived_in, recv_col, norm_gain[None], qkv_pad, rate_pad, bias_pad)
    projected = projected.reshape(blocks, MB, -1)
    rate_blocks = rates.reshape(blocks, MB, -1)
    own, past = scan_forward(flags, projected, rate_blocks, first, second, second_bias, gain, shift)
    mixed = lax.all_gather(own.reshape(rows, -1), "tensor")
    (
        up, out_sent, act, sgrad, nmid, gated, mixer_grad, heads_grad, gate_grad, grad_pgain, grad_pbias, gain_mid,
        base, gate_part, resid_part
    ) = middle(
        me, recv_col, recv_row, turn_row, arrived_up, mixed, normed, resid, weights, ffn_gain[None]
    )
    count = lax.axis_size("dp")
    def exchanged(chunks):
        return swap(chunks.reshape(-1, width)).reshape(chunks.shape)
    def summed(got):
        return jnp.sum(got.astype(f32), 0).astype(bf16)
    early_in = early_grads(count, act, up, nmid, sgrad, gated, mixer_grad, normed, gate_grad, out_sent)
    heads_grad, early_in = lax.optimization_barrier((heads_grad, early_in))
    early_got = exchanged(early_in)
    dproj, drate, carry = scan_backward(
        flags, heads_grad.reshape(blocks, MB, -1), projected, rate_blocks, gain, shift, past
    )
    dproj = dproj.reshape(rows, -1)
    logit = drate.reshape(rows, -1)
    sums = in_part(size, me, turn_row, dproj, logit, qkv_pad, rate_pad)
    got = [sums[0]] + [turn(sums[k], k) for k in range(1, size)]
    own_sum, early_got = lax.optimization_barrier((sums[0], early_got))
    got[0] = own_sum
    lines = rows // count
    out_got = early_got[:, -lines:].reshape(rows, width)
    early_sum = summed(early_got[:, :-lines])
    early = lax.all_gather(early_sum, "dp")
    dproj, early_sum = lax.optimization_barrier((dproj, early_sum))
    late_in = late_grads(count, dproj, normed, logit, *carry, grad_pgain, grad_pbias, gain_mid)
    late_sum = summed(exchanged(late_in))
    got, late_sum = lax.optimization_barrier((got, late_sum))
    cut = 3 * heads * HS // count
    back = in_rows(count, got, base, gate_part, resid_part, norm_gain[None])
    late_sum, early, _ = lax.optimization_barrier((late_sum, early, back))
    late = lax.all_gather(late_sum, "dp")
    part = rows // size
    sent = exchanged(back)
    lines = part // count
    gains = jnp.concatenate(split_three(jnp.sum(sent[:, lines:lines + 3].astype(f32), (0, 1))[None]), 0)
    mine = jnp.concatenate([sent[:, :lines].reshape(part, width), jnp.pad(gains, ((0, 13), (0, 0)))], 0)
    third = width // 3
    edges = [0]
    for lines_of in (width, third, act.shape[1], 2 * heads * HS):
        edges.append(edges[-1] + lines_of // count)
    if aligned(count, (width, third, act.shape[1], 2 * heads * HS)):
        grad_swiglu, grad_down, pair_grads = early_out(edges, early)
    else:
        left, right, grad_down, pair_grads = [
            early[:, edges[i]:edges[i + 1]].astype(f32).reshape(-1, width) for i in range(4)
        ]
        right = jnp.concatenate([right[:, i * third:(i + 1) * third] for i in range(3)], 0)
        grad_swiglu = jnp.concatenate([left, right], 1).reshape(swiglu_weight.shape)
    final = [mine] + [turn(mine, k) for k in range(1, size)]
    final, grad_swiglu, grad_down, pair_grads = lax.optimization_barrier((final, grad_swiglu, grad_down, pair_grads))
    end_turned = ((me[0] - end_col // part) % size) * part + end_col % part
    input_grad = settle(MICRO, end_turned, final, part, "settle_in")
    norm_total = sum(jnp.sum(x[part:part + 3].astype(f32), 0) for x in final)
    outputs = settle(MICRO, fin_col, [lax.optimization_barrier((out_got, final))[0]], rows, "settle_out")
    if count == 8:
        canonical = late
    else:
        canonical = jnp.concatenate([late[:, :cut].reshape(8, -1, width), late[:, cut:].reshape(8, -1, width)], 1)
    (
        big, grad_first, grad_second, first_bias, second_b, grad_gain, grad_shift, grad_pg, grad_pb, grad_fg, grad_rate, grad_rb
    ) = late_out(heads, heads * HS, 3 * heads * HS // canonical.shape[0], canonical)
    return (
        outputs,
        input_grad,
        norm_total,
        big.reshape(3, heads * HS, width).transpose(2, 0, 1),
        grad_rate.T,
        grad_rb[0],
        grad_first,
        first_bias,
        jnp.swapaxes(grad_second, 1, 2),
        second_b,
        grad_gain,
        grad_shift,
        pair_grads[heads * HS:].T,
        grad_pg[0],
        grad_pb[0],
        pair_grads[:heads * HS],
        grad_fg[0],
        grad_swiglu,
        grad_down,
    )

def solution(mesh):
    rows, heads, columns = P(None, "dp", None), P("tensor", None), P(None, "tensor")
    table = P(None, "dp")
    vector = P("tensor")
    cube = P("tensor", None, None)
    wide = P(None, None, "tensor")
    return jax.shard_map(
        shards,
        mesh=mesh,
        in_specs=(
            rows, rows, table, table, table, P(), wide, columns, vector, cube, heads, cube, heads, heads, heads,
            columns, vector, vector, heads, P(), wide, heads,
        ),
        out_specs=(
            rows, rows, P(), wide, columns, vector, cube, heads, cube, heads, heads, heads, columns, vector, vector,
            heads, P(), wide, heads,
        ),
        check_vma=False,
    )
```
